32 devices in a mesh: groups: 2 (over y), tm: 4 (over z), head: 2 (over x), batch: 2 (over core).
Axes of the slice: x: 2, y: 2, z: 4, core: 2. Of those that a mesh axis runs over, the one named last changes fastest.
Arguments:
- u_input: bfloat16 [4, 1024, 1536], P(('groups', 'batch'), 'tm'), parts along dimension 0, may hold values from -6 to 6
- head_values: bfloat16 [4, 1024, 3072], P(('groups', 'batch'), 'tm', 'head'), parts along dimension 0, may hold values from -6 to 6
- grad_output: bfloat16 [4, 1024, 3072], P(('groups', 'batch'), 'tm', 'head'), parts along dimension 0, may hold values from -6 to 6
- w_bc: bfloat16 [1536, 256], replicated, may hold values from -0.15625 to 0.15625
- w_dt: bfloat16 [1536, 48], P(None, 'head'), may hold values from -0.15625 to 0.15625
- dt_bias: float32 [48], P('head'), may hold values from -1.5 to 0.5
- a_log: float32 [48], P('head'), as said below
Outputs:
- grad_input: bfloat16 [4, 1024, 1536], P(('groups', 'batch'), 'tm'), parts along dimension 0
- grad_values: bfloat16 [4, 1024, 3072], P(('groups', 'batch'), 'tm', 'head'), parts along dimension 0
- grad_w_bc: float32 [3072, 256], P(('groups', 'tm', 'batch')), parts along dimension 0
- grad_w_dt: float32 [3072, 48], P('groups', 'head'), parts along dimension 0
- grad_dt_bias: float32 [96], P(('groups', 'head')), parts along dimension 0
- grad_a_log: float32 [96], P(('groups', 'head')), parts along dimension 0
The draws below stay inside these ranges and needn't reach their ends.
There are 2 independent parts, one for each index of `groups`. The reference program is written for one: setup_inputs(seed, part) draws one part's arguments, and reference() takes and returns one part's arrays. A program takes and returns all parts, laid end to end along the dimension named above; an argument that names none is the same for every part. Nothing has to cross between parts.
Inputs may be any that keep to these rules, and one draw needn't show every extreme that they name: a_log lies between log(0.3 / 1024) and log(0.08).
All inputs are finite; a program needn't handle non-finite values.
Results may differ from the reference program's by a relative error of at most 0.0059.
Values may be sent and summed in bfloat16 or wider, within the bound.
A program may use at most 64 MiB of HBM per device.

```python
import math
import jax
import jax.numpy as jnp
from jax import lax

D = 1536
HEADS = 48
HEAD_DIM = 64
STATE = 128
TOK_DEV = 256
LENGTH = 1024
SEQS = 2
N_TM = 4


def draw_a_log(key, part):
    length_all = TOK_DEV * N_TM
    lowest = math.log(1.0 / length_all)
    highest = math.log(0.08)
    return jax.random.uniform(key, (HEADS,), jnp.float32, lowest, highest)


def block_levels(rng, shape, split, low, largest):
    def one(dim, shards_of):
        draws = jax.random.uniform(jax.random.fold_in(jax.random.fold_in(rng, 6), dim), (shards_of,), jnp.float32, low / len(split), largest / len(split))
        return jnp.repeat(jnp.exp(draws), shape[dim] // shards_of).reshape((-1,) + (1,) * (len(shape) - dim - 1))

    gain = one(*split[0])
    for cut in split[1:]:
        gain = gain * one(*cut)
    return gain


def noise(stream_key, shape, deviation, reach, cuts=(), dtype=jnp.bfloat16):
    factor_of = block_levels(stream_key, shape, cuts, -0.22, 0.18) if cuts else 1.0
    drawn = jax.random.normal(stream_key, shape, jnp.float32) * deviation * factor_of
    return jnp.minimum(jnp.maximum(drawn, -reach), reach).astype(dtype)


def setup_inputs(seed: int = 0, part: int = 0) -> dict:
    keys = jax.random.split(jax.random.key(seed), 8)
    part_keys = jax.random.split(jax.random.fold_in(keys[7], part), 8)
    u_input = noise(part_keys[0], (SEQS, LENGTH, D), 1.0, 6.0, ((0, 2), (1, 4)))
    head_values = noise(part_keys[1], (SEQS, LENGTH, HEADS * HEAD_DIM), 1.0, 6.0, ((0, 2), (1, 4), (2, 2)))
    grad_output = noise(part_keys[2], (SEQS, LENGTH, HEADS * HEAD_DIM), 1.0, 6.0, ((0, 2), (1, 4), (2, 2)))
    w_bc = noise(keys[3], (D, 2 * STATE), D ** -0.5, 0.15625)
    w_dt = noise(keys[4], (D, HEADS), D ** -0.5, 0.15625, ((1, 2),))
    dt_bias = jnp.clip(-1.5 + 2.0 * jax.random.uniform(keys[5], (HEADS,), jnp.float32) ** block_levels(keys[5], (HEADS,), ((0, 2),), -0.2, 0.2), -1.5, 0.5)
    a_log = draw_a_log(jax.random.fold_in(keys[7], 71), part)
    return dict(u_input=u_input, head_values=head_values, grad_output=grad_output, w_bc=w_bc, w_dt=w_dt, dt_bias=dt_bias, a_log=a_log)


def span_core(b_rows, c_rows, time_step, values_in, rate, state_in):
    highest = lax.Precision.HIGHEST
    log_decay = jnp.cumsum(time_step * rate[None, :], axis=0)
    length_t = time_step.shape[0]
    causal = jnp.arange(length_t)[:, None] >= jnp.arange(length_t)[None, :]
    differ = log_decay.T[:, :, None] - log_decay.T[:, None, :]
    decay = jnp.exp(jnp.where(causal[None], differ, -jnp.inf))
    scores = jnp.dot(c_rows, b_rows.T, precision=highest)
    mixing = decay * scores[None] * time_step.T[:, None, :]
    inner = jnp.einsum('hts,shp->thp', mixing, values_in, precision=highest)
    carried = jnp.exp(log_decay)[:, :, None] * jnp.einsum('tn,hpn->thp', c_rows, state_in, precision=highest)
    output = inner + carried
    tail_w = jnp.exp(log_decay[-1][None, :] - log_decay) * time_step
    final = jnp.exp(log_decay[-1])[:, None, None] * state_in + jnp.einsum('sh,shp,sn->hpn', tail_w, values_in, b_rows, precision=highest)
    return (output, final)

def sequence_forward(b_rows, c_rows, time_step, values_in, rate):

    def advance(state_in, pieces):
        output, final = span_core(pieces[0], pieces[1], pieces[2], pieces[3], rate, state_in)
        return (final, output)
    start = jnp.zeros((HEADS, HEAD_DIM, STATE), jnp.float32)
    blocks = (b_rows.reshape(N_TM, TOK_DEV, STATE), c_rows.reshape(N_TM, TOK_DEV, STATE), time_step.reshape(N_TM, TOK_DEV, HEADS), values_in.reshape(N_TM, TOK_DEV, HEADS, HEAD_DIM))
    _, outputs = lax.scan(advance, start, blocks)
    return outputs.reshape(LENGTH, HEADS, HEAD_DIM)

def reference(u_input, head_values, grad_output, w_bc, w_dt, dt_bias, a_log):
    rate = -jnp.exp(a_log)
    flat = u_input.reshape(SEQS * LENGTH, D)
    proj = jnp.dot(flat, w_bc, preferred_element_type=jnp.float32).astype(jnp.bfloat16)
    pre = jnp.dot(flat, w_dt, preferred_element_type=jnp.float32) + dt_bias[None, :]
    delta = jax.nn.softplus(pre).reshape(SEQS, LENGTH, HEADS)
    b_all = proj[:, :STATE].astype(jnp.float32).reshape(SEQS, LENGTH, STATE)
    c_all = proj[:, STATE:].astype(jnp.float32).reshape(SEQS, LENGTH, STATE)
    values_all = head_values.astype(jnp.float32).reshape(SEQS, LENGTH, HEADS, HEAD_DIM)
    cotangent = grad_output.astype(jnp.float32).reshape(SEQS, LENGTH, HEADS, HEAD_DIM)
    grad_b_list = []
    grad_c_list = []
    grad_delta_list = []
    grad_x_list = []
    rate_total = jnp.zeros((HEADS,), jnp.float32)
    for seq_index in range(SEQS):
        _, pull_back = jax.vjp(sequence_forward, b_all[seq_index], c_all[seq_index], delta[seq_index], values_all[seq_index], rate)
        g_b, g_c, g_delta, g_x, g_rate = pull_back(cotangent[seq_index])
        grad_b_list.append(g_b)
        grad_c_list.append(g_c)
        grad_delta_list.append(g_delta)
        grad_x_list.append(g_x)
        rate_total = rate_total + g_rate
    grad_proj = jnp.concatenate([jnp.stack(grad_b_list), jnp.stack(grad_c_list)], axis=-1)
    grad_proj = grad_proj.reshape(SEQS * LENGTH, 2 * STATE).astype(jnp.bfloat16)
    grad_pre = jnp.stack(grad_delta_list).reshape(SEQS * LENGTH, HEADS) * jax.nn.sigmoid(pre)
    grad_pre_b = grad_pre.astype(jnp.bfloat16)
    grad_input = (jnp.dot(grad_proj, w_bc.T, preferred_element_type=jnp.float32) + jnp.dot(grad_pre_b, w_dt.T, preferred_element_type=jnp.float32)).astype(jnp.bfloat16)
    grad_values = jnp.stack(grad_x_list).reshape(SEQS, LENGTH, HEADS * HEAD_DIM).astype(jnp.bfloat16)
    grad_w_bc = jnp.dot(flat.T, grad_proj, preferred_element_type=jnp.float32)
    grad_w_dt = jnp.dot(flat.T, grad_pre_b, preferred_element_type=jnp.float32)
    grad_dt_bias = lax.optimization_barrier(jnp.sum(grad_pre, axis=0))
    return (grad_input.reshape(SEQS, LENGTH, D), grad_values, grad_w_bc, grad_w_dt, grad_dt_bias, rate_total * rate)
```

```python
import functools

import jax
import jax.numpy as jnp
from jax import lax
from jax.experimental import pallas as pl
from jax.experimental.pallas import tpu as pltpu
from jax.sharding import PartitionSpec as P

MESH = pl.DeviceIdType.MESH
F32 = jnp.float32
BF16 = jnp.bfloat16
LANES = 128
NT = (((1,), (1,)), ((), ()))
TN = (((0,), (0,)), ((), ()))


def dot(a, b, dims=(((1,), (0,)), ((), ()))):
    return lax.dot_general(a, b, dims, preferred_element_type=F32)


def dot_exact(a, b):
    return lax.dot_general(
        a, b, (((1,), (0,)), ((), ())),
        precision=lax.Precision.HIGHEST, preferred_element_type=F32,
    )


def kernel(
    zn, hn, bn, heads, split,
    u, x, g, wbc, wdt, bias, alog,
    gin, gval, gwbc, gwdt, gbias, galog,
    wpad, ut, rows, proj, l_t, l_sel, d_sel, xs, gs, own_f, own_b, gxi, st, dst, col_e, erows,
    direct, qd, gl, fin, gacc,
    sf, rf, sb, rb, wx, px, gpx, csend, crecv, plocal, zsend, zrecv, fsend, frecv,
    wsend, wrecv, wsum, wzsend, wzrecv, wfsend, wfrecv, smsend, smrecv, smzsend, smzrecv,
    f_ss, f_rs, b_ss, b_rs, h_ss, h_rs, c_ss, c_rs, z_ss, z_rs,
):
    z, hx, bt = lax.axis_index("tm"), lax.axis_index("head"), lax.axis_index("batch")
    tokens, width = u.shape
    pairs = heads // 2
    per = 2 if pairs % 2 == 0 else 1
    chunks = pairs // per
    stride = 2
    state = LANES
    rpad = wx.shape[1]
    half = width // bn

    def several(body, i, carry):
        for j in range(per):
            carry = body(i * per + j, carry)
        return carry

    lane = lax.broadcasted_iota(jnp.int32, (tokens, LANES), 1)
    lane1 = lax.broadcasted_iota(jnp.int32, (1, LANES), 1)
    low = lane < 64
    low1 = lane1 < 64

    barrier = pltpu.get_barrier_semaphore()
    for k in range(1, zn):
        pl.semaphore_signal(barrier, inc=1, device_id={"tm": lax.rem(z + k, zn)}, device_id_type=MESH)
    for k in range(1, hn):
        pl.semaphore_signal(barrier, inc=1, device_id={"head": lax.rem(hx + k, hn)}, device_id_type=MESH)
    for k in range(1, bn):
        pl.semaphore_signal(barrier, inc=1, device_id={"batch": lax.rem(bt + k, bn)}, device_id_type=MESH)

    wpad[...] = jnp.zeros_like(wpad)
    wpad[:heads, :] = wdt[...]
    rows[...] = jnp.zeros_like(rows)
    rows[0:1, :heads] = bias[...]
    rows[1:2, :heads] = alog[...]
    uu = u[...]
    proj[...] = dot(uu, wbc[...]).astype(BF16)
    pre = dot(uu, wpad[...], NT) + rows[0:1, :]
    delta = jnp.maximum(pre, 0.0) + jnp.log1p(jnp.exp(-jnp.abs(pre)))
    rate = -jnp.exp(rows[1:2, :])
    ti = lax.broadcasted_iota(jnp.int32, (tokens, tokens), 0)
    si = lax.broadcasted_iota(jnp.int32, (tokens, tokens), 1)
    log_decay = dot_exact((ti >= si).astype(F32), delta * rate)
    l_rows = log_decay.T
    for h in range(heads):
        l_t[h] = l_rows[h:h + 1, :]
    b_all, c_all = proj[:, :state], proj[:, state:]
    b_t = b_all.astype(F32).T.astype(BF16)
    c_t = c_all.astype(F32).T.astype(BF16)
    st[...] = jnp.where(ti <= si, dot(b_all, c_all, NT), 0.0)
    wx[hx] = wpad[:rpad, :]

    def pick(value, head):
        return jnp.sum(jnp.where(lane == head, value, 0.0), axis=1, keepdims=True)

    def summarize(p, carry):
        cols = pl.ds(pl.multiple_of(p * LANES, LANES), LANES)
        ls = jnp.where(low, pick(log_decay, 2 * p), pick(log_decay, 2 * p + 1))
        ds = jnp.where(low, pick(delta, 2 * p), pick(delta, 2 * p + 1))
        l_sel[p] = ls
        d_sel[p] = ds
        xv = (jnp.exp(ls[tokens - 1:tokens, :] - ls) * ds * x[:, cols].astype(F32)).astype(BF16)
        gv = (jnp.exp(ls) * g[:, cols].astype(F32)).astype(BF16)
        xs[p] = xv
        gs[p] = gv
        own_f[p] = dot(b_t, xv)
        own_b[p] = dot(c_t, gv)
        return carry

    lax.fori_loop(0, pairs // per, lambda i, carry: several(summarize, i, carry), 0)

    dst[...] = jnp.zeros_like(dst)
    erows[...] = jnp.zeros_like(erows)
    direct[...] = jnp.zeros_like(direct)
    qd[...] = jnp.zeros_like(qd)
    gl[...] = jnp.zeros_like(gl)
    fin[...] = jnp.zeros_like(fin)
    gacc[...] = jnp.zeros_like(gacc)

    @pl.when(z == 0)
    def _():
        rf[...] = jnp.zeros_like(rf)

    @pl.when(z == zn - 1)
    def _():
        rb[...] = jnp.zeros_like(rb)

    pl.semaphore_wait(barrier, zn + hn + bn - 3)

    def head_copies(k):
        to = {"head": lax.rem(hx + k, hn)}
        return [
            pltpu.make_async_remote_copy(
                ref.at[hx], ref.at[hx], h_ss.at[i, k], h_rs.at[i, k], device_id=to, device_id_type=MESH
            )
            for i, ref in enumerate((wx, px, gpx))
        ]

    for k in range(1, hn):
        head_copies(k)[0].start()

    def chain_f(c):
        part = pl.ds(c * per, per)
        return pltpu.make_async_remote_copy(
            sf.at[part], rf.at[part], f_ss.at[c], f_rs.at[c],
            device_id={"tm": lax.rem(z + 1, zn)}, device_id_type=MESH,
        )

    def chain_b(c):
        part = pl.ds(c * per, per)
        return pltpu.make_async_remote_copy(
            sb.at[part], rb.at[part], b_ss.at[c], b_rs.at[c],
            device_id={"tm": lax.rem(z + zn - 1, zn)}, device_id_type=MESH,
        )

    def chain_step(c, first, last, make, own, send, recv):
        @pl.when((c >= 0) & (c < chunks))
        def _():
            @pl.when(jnp.logical_not(first))
            def _():
                make(c).wait_recv()

            @pl.when(jnp.logical_not(last))
            def _():
                for j in range(per):
                    p = c * per + j
                    total = jnp.exp(l_sel[p, tokens - 1:tokens, :])
                    send[p] = (total * recv[p].astype(F32) + own[p]).astype(BF16)
                make(c).start()

    lm = low.astype(F32).astype(BF16)

    def local_pair(p):
        cols = pl.ds(pl.multiple_of(p * LANES, LANES), LANES)
        gb = g[:, cols]
        xb = x[:, cols]
        sh = tokens // 2
        for s0 in (0, sh):
            t0 = s0
            gx = []
            gt = gb[t0:, :]
            sm = st[s0:s0 + sh, t0:]
            add = jnp.zeros((sh, tokens - t0), F32)
            zero = [jnp.zeros((1, t0), F32)] if t0 else []
            dr = direct[s0:s0 + sh, :]
            for j in range(2):
                keep = lm[s0:s0 + sh, :]
                xm = xb[s0:s0 + sh, :] * (keep if j == 0 else (1.0 - keep).astype(BF16))
                dm = dot(xm, gt, NT)
                lc = l_sel[p, s0:s0 + sh, 64 * j:64 * j + 1]
                dc = d_sel[p, s0:s0 + sh, 64 * j:64 * j + 1]
                lr = l_t[2 * p + j][:, t0:]
                decay = jnp.exp(jnp.minimum(lr - lc, 0.0))
                gx.append(dot((decay * sm).astype(BF16), gt))
                dmd = dm * decay
                add = add + dmd * dc
                w = dmd * sm
                dr = dr + jnp.where(lane[:sh] == 2 * p + j, jnp.sum(w, axis=1, keepdims=True), 0.0)
                ce = jnp.concatenate(zero + [jnp.sum(w * dc, axis=0, keepdims=True)], axis=1)
                col_e[2 * p + j] = ce if s0 == 0 else col_e[2 * p + j] + ce
            direct[s0:s0 + sh, :] = dr
            dst[s0:s0 + sh, t0:] += add
            gxi[p, s0:s0 + sh, :] = jnp.where(low[:sh], gx[0], gx[1])

    def mixed(i, carry):
        chain_step(i - z * stride, z == 0, z == zn - 1, chain_f, own_f, sf, rf)
        chain_step(i - (zn - 1 - z) * stride, z == zn - 1, z == 0, chain_b, own_b, sb, rb)

        @pl.when(i < pairs)
        def _():
            local_pair(i)

        return carry

    lax.fori_loop(0, max(pairs, (zn - 1) * stride + chunks), mixed, 0)

    def carried(p, carry):
        cols = pl.ds(pl.multiple_of(p * LANES, LANES), LANES)
        entering, leaving = rf[p], rb[p]
        ls, ds = l_sel[p], d_sel[p]
        last = ls[tokens - 1:tokens, :]
        car = jnp.exp(ls) * g[:, cols].astype(F32) * dot(c_all, entering)
        br = jnp.exp(last - ls) * dot(b_all, leaving)
        gval[:, cols] = (ds * (gxi[p] + br)).astype(BF16)
        q = x[:, cols].astype(F32) * br
        ends = jnp.exp(last) * jnp.sum(entering.astype(F32) * leaving.astype(F32), axis=0, keepdims=True)
        q_new, c_new, e_new = qd[...], gl[...], fin[...]
        for j in range(2):
            mine, mine1 = (low, low1) if j == 0 else (~low, ~low1)
            at, at1 = lane == 2 * p + j, lane1 == 2 * p + j
            q_new = q_new + jnp.where(at, jnp.sum(jnp.where(mine, q, 0.0), axis=1, keepdims=True), 0.0)
            c_new = c_new + jnp.where(at, jnp.sum(jnp.where(mine, car, 0.0), axis=1, keepdims=True), 0.0)
            e_new = e_new + jnp.where(at1, jnp.sum(jnp.where(mine1, ends, 0.0), axis=1, keepdims=True), 0.0)
        qd[...], gl[...], fin[...] = q_new, c_new, e_new
        gacc[:, :state] += dot(xs[p], leaving, NT)
        gacc[:, state:] += dot(gs[p], entering, NT)
        return carry

    lax.fori_loop(0, pairs // per, lambda i, carry: several(carried, i, carry), 0)

    d_masked = jnp.where(ti <= si, dst[...], 0.0).astype(BF16)
    px[hx, :, :state] = (gacc[:, :state] + dot(d_masked, c_all)).astype(BF16)
    px[hx, :, state:] = (gacc[:, state:] + dot(d_masked, b_all, TN)).astype(BF16)
    for k in range(1, hn):
        head_copies(k)[1].start()

    q_all = qd[...]
    straight = direct[...] + q_all
    for h in range(heads):
        erows[h:h + 1, :] = col_e[h]
    g_log = gl[...] + erows[...].T - delta * straight
    tail = jnp.sum(delta * q_all, axis=0, keepdims=True) + fin[...]
    back = dot_exact((ti <= si).astype(F32), g_log) + tail
    g_delta = straight + rate * back
    g_pre = g_delta * jax.nn.sigmoid(pre)
    smsend[...] = jnp.zeros_like(smsend)
    smsend[0:1, :] = jnp.sum(g_pre, axis=0, keepdims=True)
    smsend[1:2, :] = jnp.sum(delta * back, axis=0, keepdims=True) * rate
    gpx[hx] = g_pre.T[:rpad, :].astype(BF16)
    for k in range(1, hn):
        head_copies(k)[2].start()
    wsend[...] = dot(gpx[hx], uu).astype(BF16)

    other = {"batch": lax.rem(bt + 1, bn)}

    def core_copy(i, src, to):
        return pltpu.make_async_remote_copy(src, to, c_ss.at[i], c_rs.at[i], device_id=other, device_id_type=MESH)

    core_w = core_copy(0, wsend, wrecv)
    core_s = core_copy(1, smsend, smrecv)
    core_p = core_copy(2, csend, crecv)
    core_f = core_copy(3, wfsend, wfrecv)
    core_w.start()
    core_s.start()

    def along(i, src, to, k):
        there = lax.rem(z + k, zn)
        return pltpu.make_async_remote_copy(
            src, to.at[z], z_ss.at[i, k], z_rs.at[i, k], device_id={"tm": there}, device_id_type=MESH
        )

    def each_z(body):
        def turn(k, carry):
            body(k)
            return carry

        lax.fori_loop(1, zn, turn, 0)

    def z_start_small(k):
        along(0, wzsend, wzrecv, k).start()
        along(1, smzsend, smzrecv, k).start()

    def z_start_large(k):
        along(2, zsend.at[lax.rem(z + k, zn)], zrecv, k).start()

    def z_wait_small(k):
        along(0, wzsend, wzrecv, k).wait()
        along(1, smzsend, smzrecv, k).wait()

    def z_wait_large(k):
        along(2, zsend.at[lax.rem(z + k, zn)], zrecv, k).wait()

    for k in range(width // 256):
        at = k * 256
        ut[at:at + 256, :] = u[:, at:at + 256].astype(F32).T.astype(BF16)

    core_w.wait()
    core_s.wait()
    wsum[...] = wsend[...].astype(F32) + wrecv[...].astype(F32)
    mine = pl.ds(pl.multiple_of(bt * half, LANES), half)
    theirs = pl.ds(pl.multiple_of(lax.rem(bt + 1, bn) * half, LANES), half)
    wz = wsum[:, mine].astype(BF16)
    wzsend[...] = wz
    wzrecv[z] = wz
    sz = smsend[...] + smrecv[...]
    smzsend[...] = sz
    smzrecv[z] = sz
    each_z(z_start_small)

    for k in range(1, hn):
        for copy in head_copies(k):
            copy.wait()
    gp = px[0].astype(F32)
    for k in range(1, hn):
        gp = gp + px[k].astype(F32)
    gp = gp.astype(BF16)
    wide = zrecv.shape[2]
    if split:
        piece = jnp.where(hx == 0, gp[:, :wide], gp[:, wide:])
    else:
        piece = gp
    block = zrecv.shape[1]
    local = dot(ut[...], piece)
    for k in range(zn * bn):
        plocal[k] = local[k * block:(k + 1) * block, :]
    for k in range(zn):
        csend[k] = plocal[k * bn + lax.rem(bt + 1, bn)].astype(BF16)
    core_p.start()

    core_p.wait()
    for k in range(zn):
        zsend[k] = (plocal[k * bn + bt] + crecv[k].astype(F32)).astype(BF16)
    zrecv[z] = zsend[z]
    each_z(z_start_large)

    gpa = gpx[...].reshape(hn * rpad, tokens).astype(F32).T.astype(BF16)
    wa = wx[...].reshape(hn * rpad, width)
    gin[...] = (dot(gp, wbc[...], NT) + dot(gpa, wa)).astype(BF16)

    each_z(z_wait_small)
    total_w = wzrecv[0].astype(F32)
    total_s = smzrecv[0]
    for k in range(1, zn):
        total_w = total_w + wzrecv[k].astype(F32)
        total_s = total_s + smzrecv[k]
    wfsend[...] = total_w
    core_f.start()
    gbias[...] = total_s[0:1, :heads]
    galog[...] = total_s[1:2, :heads]
    gwdt[:, mine] = total_w[:heads, :]

    each_z(z_wait_large)
    total = zrecv[0].astype(F32)
    for k in range(1, zn):
        total = total + zrecv[k].astype(F32)
    if split:
        fsend[...] = total
        final = pltpu.make_async_remote_copy(
            fsend, frecv, c_ss.at[4], c_rs.at[4], device_id={"head": lax.rem(hx + 1, hn)}, device_id_type=MESH
        )
        final.start()
        gwbc[:, pl.ds(pl.multiple_of(hx * wide, LANES), wide)] = total
        final.wait()
        gwbc[:, pl.ds(pl.multiple_of((1 - hx) * wide, LANES), wide)] = frecv[...]
    else:
        gwbc[...] = total
    core_f.wait()
    gwdt[:, theirs] = wfrecv[:heads, :]

    def drain(c, carry):
        @pl.when(z < zn - 1)
        def _():
            chain_f(c).wait_send()

        @pl.when(z > 0)
        def _():
            chain_b(c).wait_send()

        return carry

    lax.fori_loop(0, chunks, drain, 0)


def on_device(sizes, u_input, head_values, grad_output, w_bc, w_dt, dt_bias, a_log):
    zn, hn, bn = sizes
    seqs, tokens, width = u_input.shape
    assert seqs == 1 and bn == 2
    heads = w_dt.shape[1]
    values = head_values.shape[2]
    both = w_bc.shape[1]
    pairs = heads // 2
    assert values == heads * 64 and both == 2 * LANES and heads % 2 == 0
    split = hn == 2
    wide = both // 2 if split else both
    block = width // (zn * bn)
    rpad = -(-heads // 16) * 16
    half = width // bn
    chunks = pairs // 2 if pairs % 2 == 0 else pairs
    vm = pltpu.VMEM
    dma = pltpu.SemaphoreType.DMA
    scratch = [
        vm((LANES, width), BF16), vm((width, tokens), BF16), vm((8, LANES), F32), vm((tokens, both), BF16), vm((heads, 1, tokens), F32),
        vm((pairs, tokens, LANES), F32), vm((pairs, tokens, LANES), F32),
        vm((pairs, tokens, LANES), BF16), vm((pairs, tokens, LANES), BF16),
        vm((pairs, LANES, LANES), F32), vm((pairs, LANES, LANES), F32), vm((pairs, tokens, LANES), F32),
        vm((tokens, tokens), F32), vm((tokens, tokens), F32), vm((heads, 1, tokens), F32), vm((LANES, tokens), F32),
        vm((tokens, LANES), F32), vm((tokens, LANES), F32), vm((tokens, LANES), F32), vm((1, LANES), F32),
        vm((tokens, both), F32),
        vm((pairs, LANES, LANES), BF16), vm((pairs, LANES, LANES), BF16),
        vm((pairs, LANES, LANES), BF16), vm((pairs, LANES, LANES), BF16),
        vm((hn, rpad, width), BF16), vm((hn, tokens, both), BF16), vm((hn, rpad, tokens), BF16),
        vm((zn, block, wide), BF16), vm((zn, block, wide), BF16), vm((zn * bn, block, wide), F32),
        vm((zn, block, wide), BF16), vm((zn, block, wide), BF16), vm((block, wide), F32), vm((block, wide), F32),
        vm((rpad, width), BF16), vm((rpad, width), BF16), vm((rpad, width), F32),
        vm((rpad, half), BF16), vm((zn, rpad, half), BF16), vm((rpad, half), F32), vm((rpad, half), F32),
        vm((8, LANES), F32), vm((8, LANES), F32), vm((8, LANES), F32), vm((zn, 8, LANES), F32),
        dma((chunks,)), dma((chunks,)), dma((chunks,)), dma((chunks,)),
        dma((3, hn)), dma((3, hn)), dma((5,)), dma((5,)), dma((3, zn)), dma((3, zn)),
    ]
    spec = pl.BlockSpec(memory_space=pltpu.VMEM)
    shapes = (
        ((tokens, width), BF16), ((tokens, values), BF16), ((block, both), F32),
        ((heads, width), F32), ((1, heads), F32), ((1, heads), F32),
    )
    kept = pl.pallas_call(
        functools.partial(kernel, zn, hn, bn, heads, split),
        out_shape=tuple(vm(*s) for s in shapes),
        in_specs=[spec] * 7,
        out_specs=[spec] * 6,
        scratch_shapes=scratch,
        compiler_params=pltpu.CompilerParams(
            collective_id=0, has_side_effects=True, vmem_limit_bytes=56 << 20
        ),
    )(
        u_input.reshape(tokens, width), head_values.reshape(tokens, values), grad_output.reshape(tokens, values),
        w_bc, w_dt.T, dt_bias.reshape(1, heads), a_log.reshape(1, heads),
    )
    gin, gval, gwbc, gwdt, gbias, galog = pl.pallas_call(
        write,
        out_shape=tuple(jax.ShapeDtypeStruct(*s) for s in shapes),
        in_specs=[spec] * 6,
        out_specs=[pl.BlockSpec(memory_space=pl.ANY)] * 6,
        scratch_shapes=[dma((6,))],
        compiler_params=pltpu.CompilerParams(vmem_limit_bytes=1 << 20),
    )(*kept)
    return (
        gin.reshape(1, tokens, width), gval.reshape(1, tokens, values), gwbc,
        gwdt.T, gbias.reshape(heads), galog.reshape(heads),
    )


def write(*refs):
    sems = refs[12]
    copies = [pltpu.make_async_copy(refs[i], refs[6 + i], sems.at[i]) for i in range(6)]
    for copy in copies:
        copy.start()
    for copy in copies:
        copy.wait()


def solution(mesh):
    sizes = (mesh.shape["tm"], mesh.shape["head"], mesh.shape["batch"])
    return jax.shard_map(
        functools.partial(on_device, sizes),
        mesh=mesh,
        in_specs=(
            P(("groups", "batch"), "tm", None),
            P(("groups", "batch"), "tm", "head"),
            P(("groups", "batch"), "tm", "head"),
            P(),
            P(None, "head"),
            P("head"),
            P("head"),
        ),
        out_specs=(
            P(("groups", "batch"), "tm", None),
            P(("groups", "batch"), "tm", "head"),
            P(("groups", "tm", "batch"), None),
            P("groups", "head"),
            P(("groups", "head")),
            P(("groups", "head")),
        ),
        check_vma=False,
    )
```

```python
import functools

import jax
import jax.numpy as jnp
from jax import lax
from jax.experimental import pallas as pl
from jax.experimental.pallas import tpu as pltpu
from jax.sharding import PartitionSpec as P

MESH = pl.DeviceIdType.MESH
F32 = jnp.float32
BF16 = jnp.bfloat16
LANES = 128
NT = (((1,), (1,)), ((), ()))
TN = (((0,), (0,)), ((), ()))


def dot(a, b, dims=(((1,), (0,)), ((), ()))):
    return lax.dot_general(a, b, dims, preferred_element_type=F32)


def split3(v):
    hi = v.astype(BF16)
    rest = v - hi.astype(F32)
    mid = rest.astype(BF16)
    return hi, mid, (rest - mid.astype(F32)).astype(BF16)


def dot_ones(a, v):
    hi, mid, lo = split3(v)
    return dot(a, hi) + dot(a, mid) + dot(a, lo)


def dot_sel(v, ones):
    hi = v.astype(BF16)
    lo = (v - hi.astype(F32)).astype(BF16)
    return dot(hi, ones, NT) + dot(lo, ones, NT)


def kernel(
    zn, hn, bn, heads, split,
    u_h, x_h, g_h, wbc_h, wdt_h, bias_h, alog_h,
    gin, gval, gwbc, gwdt, gbias, galog,
    u, x, g, wbc, wdt, bias, alog, in_s,
    wpad, ut, rows, proj, l_t, l_b, e1_b, e1_p, e2_p, ends_b, sel, xs, gs, own_f, own_b, gxi, st, dst, col_e, erows,
    direct, qd, gl, tails, gacc_b, gacc_c, smid, gmid,
    sf, rf, sb, rb, wx, px, gpx, csend, crecv, plocal, zsend, zrecv, fsend, frecv,
    wsend, wrecv, wsum, wzsend, wzrecv, wfsend, wfrecv, smsend, smrecv, smzsend, smzrecv,
    f_ss, f_rs, b_ss, b_rs, h_ss, h_rs, c_ss, c_rs, z_ss, z_rs,
):
    z, hx, bt = lax.axis_index("tm"), lax.axis_index("head"), lax.axis_index("batch")
    tokens, width = u.shape
    pairs = heads // 2
    groups = pairs // 2
    stride = 4
    state = LANES
    sh = tokens // 2
    rpad = wx.shape[1]
    half = width // bn

    loads = [
        pltpu.make_async_copy(src, to, in_s.at[i])
        for i, (src, to) in enumerate((
            (wdt_h, wdt), (bias_h, bias), (alog_h, alog), (u_h, u), (wbc_h, wbc), (x_h, x), (g_h, g)
        ))
    ]
    for load in loads:
        load.start()

    barrier = pltpu.get_barrier_semaphore()
    for k in range(1, zn):
        pl.semaphore_signal(barrier, inc=1, device_id={"tm": lax.rem(z + k, zn)}, device_id_type=MESH)
    for k in range(1, hn):
        pl.semaphore_signal(barrier, inc=1, device_id={"head": lax.rem(hx + k, hn)}, device_id_type=MESH)
    for k in range(1, bn):
        pl.semaphore_signal(barrier, inc=1, device_id={"batch": lax.rem(bt + k, bn)}, device_id_type=MESH)

    lane = lax.broadcasted_iota(jnp.int32, (tokens, LANES), 1)
    low = lax.broadcasted_iota(jnp.int32, (sh, LANES), 1) < 64
    lm = low.astype(F32).astype(BF16)
    hm = 1.0 - lm
    ti = lax.broadcasted_iota(jnp.int32, (tokens, tokens), 0)
    si = lax.broadcasted_iota(jnp.int32, (tokens, tokens), 1)
    lower = (ti >= si).astype(F32).astype(BF16)
    causal = ti[:sh, :sh] <= si[:sh, :sh]

    with jax.named_scope("initial"):
        wpad[...] = jnp.zeros_like(wpad)
        rows[...] = jnp.zeros_like(rows)
        which = lax.broadcasted_iota(jnp.int32, (LANES, LANES), 0)
        head_of = lax.shift_right_logical(lax.broadcasted_iota(jnp.int32, (LANES, LANES), 1), 6)
        used = jnp.where(which < 96, which & 31, -1)
        for p in range(pairs):
            sel[:, p * LANES:(p + 1) * LANES] = (used == head_of + 2 * p).astype(F32).astype(BF16)
        dst[...] = jnp.zeros_like(dst)
        direct[...] = jnp.zeros_like(direct)
        gl[...] = jnp.zeros_like(gl)
        qd[...] = jnp.zeros_like(qd)
        gacc_b[...] = jnp.zeros_like(gacc_b)
        gacc_c[...] = jnp.zeros_like(gacc_c)
        tails[...] = jnp.zeros_like(tails)
        erows[...] = jnp.zeros_like(erows)

        @pl.when(z == 0)
        def _():
            rf[...] = jnp.zeros_like(rf)

        @pl.when(z == zn - 1)
        def _():
            rb[...] = jnp.zeros_like(rb)

    def packed(v):
        hi, mid, lo = split3(v)
        at = lane[:v.shape[0]]
        mid, lo = pltpu.roll(mid.astype(F32), 32, 1), pltpu.roll(lo.astype(F32), 64, 1)
        return jnp.where(at < 32, hi.astype(F32), jnp.where(at < 64, mid, jnp.where(at < 96, lo, 0.0))).astype(BF16)

    with jax.named_scope("wait for u"):
        for load in loads[:5]:
            load.wait()
    wpad[:heads, :] = wdt[...]
    rows[0:1, :heads] = bias[...]
    rows[1:2, :heads] = alog[...]
    wx[hx] = wpad[:rpad, :]
    uu = u[...]
    proj[...] = dot(uu, wbc[...]).astype(BF16)
    b_all, c_all = proj[:, :state], proj[:, state:]
    b_t = b_all.astype(F32).T.astype(BF16)
    c_t = c_all.astype(F32).T.astype(BF16)
    pre = dot(uu, wpad[...], NT) + rows[0:1, :]
    small = jnp.exp(-jnp.abs(pre))
    delta = jnp.maximum(pre, 0.0) + jnp.log1p(small)
    rate = -jnp.exp(rows[1:2, :])
    log_decay = dot_ones(lower, delta * rate)
    l_rows = log_decay.T
    for h in range(heads):
        l_t[h] = l_rows[h:h + 1, :]
    mid_l, last_l = log_decay[sh - 1:sh, :], log_decay[tokens - 1:tokens, :]
    first = lax.broadcasted_iota(jnp.int32, (tokens, LANES), 0) < sh
    e1 = packed(jnp.exp(jnp.where(first, mid_l, last_l) - log_decay) * delta)
    e2 = packed(jnp.exp(jnp.where(first, log_decay, log_decay - mid_l)))
    lc = packed(log_decay - jnp.log(jnp.maximum(delta, 1e-37)))
    e1_p[...] = e1
    e2_p[...] = e2
    ends = jnp.concatenate([jnp.exp(mid_l), jnp.exp(last_l - mid_l), jnp.zeros((6, LANES), F32)], axis=0)
    ends_b[...] = dot(packed(ends), sel[...])
    with jax.named_scope("wait for values"):
        loads[5].wait()
        loads[6].wait()
    with jax.named_scope("wait for devices"):
        pl.semaphore_wait(barrier, zn + hn + bn - 3)

    def head_copy(i, ref, k):
        return pltpu.make_async_remote_copy(
            ref, ref, h_ss.at[i, k], h_rs.at[i, k],
            device_id={"head": lax.rem(hx + k, hn)}, device_id_type=MESH,
        )

    def weights_copy(k):
        return head_copy(0, wx.at[hx], k)

    def steps_copy(k):
        return head_copy(1, gpx.at[hx], k)

    def maps_copy(part, k):
        return head_copy(2 + part, px.at[hx, part], k)

    def chain_f(p):
        return pltpu.make_async_remote_copy(
            sf.at[p], rf.at[p], f_ss.at[p], f_rs.at[p],
            device_id={"tm": lax.rem(z + 1, zn)}, device_id_type=MESH,
        )

    def chain_b(p):
        return pltpu.make_async_remote_copy(
            sb.at[p], rb.at[p], b_ss.at[p], b_rs.at[p],
            device_id={"tm": lax.rem(z + zn - 1, zn)}, device_id_type=MESH,
        )

    def columns(p, n=1):
        return pl.ds(pl.multiple_of(p * n * LANES, LANES), n * LANES)

    def forward(p):
        cols = columns(p)
        middle = ends_b[0:1, cols] * rf[p].astype(F32) + own_f[0, p]
        smid[p] = middle.astype(BF16)
        sf[p] = (ends_b[1:2, cols] * middle + own_f[1, p]).astype(BF16)

        @pl.when(z < zn - 1)
        def _():
            chain_f(p).start()

    def backward(p):
        cols = columns(p)
        middle = ends_b[1:2, cols] * rb[p].astype(F32) + own_b[1, p]
        gmid[p] = middle.astype(BF16)
        sb[p] = (ends_b[0:1, cols] * middle + own_b[0, p]).astype(BF16)

        @pl.when(z > 0)
        def _():
            chain_b(p).start()

    def summarize(q, carry):
        cols = columns(q, 2)
        spread = dot(e1_p[...], sel[:, cols])
        e1_b[:, cols] = spread
        xv = (spread * x[:, cols].astype(F32)).astype(BF16)
        gv = (dot(e2_p[...], sel[:, cols]) * g[:, cols].astype(F32)).astype(BF16)
        xs[:, cols] = xv
        gs[:, cols] = gv
        for k in range(2):
            part = slice(k * sh, (k + 1) * sh)
            of, ob = dot(b_t[:, part], xv[part]), dot(c_t[:, part], gv[part])
            for j in range(2):
                own_f[k, 2 * q + j] = of[:, j * LANES:(j + 1) * LANES]
                own_b[k, 2 * q + j] = ob[:, j * LANES:(j + 1) * LANES]

        @pl.when(z == 0)
        def _():
            forward(2 * q)
            forward(2 * q + 1)

        @pl.when(z == zn - 1)
        def _():
            backward(2 * q)
            backward(2 * q + 1)

        return carry

    with jax.named_scope("summaries"):
        lax.fori_loop(0, groups, summarize, 0)

    for k in range(1, hn):
        weights_copy(k).start()

    with jax.named_scope("scores"):
        l_b[...] = dot(lc, sel[...])
        for k in range(2):
            part = slice(k * sh, (k + 1) * sh)
            st[k] = jnp.where(causal, dot(b_all[part], c_all[part], NT), 0.0)
        for k in range(width // 256):
            at = k * 256
            ut[at:at + 256, :] = u[:, at:at + 256].astype(F32).T.astype(BF16)

    def local_pair(p):
        cols = columns(p)
        for k in range(2):
            part = slice(k * sh, (k + 1) * sh)
            gt = g[part, cols]
            xb = x[part, cols]
            sm = st[k]
            dm = dot(jnp.concatenate([xb * lm, xb * hm], axis=0), gt, NT)
            add = None
            mixed = []
            dr = direct[part]
            for j in range(2):
                lr = l_t[2 * p + j][:, part]
                lcol = l_b[part, cols][:, 64 * j:64 * j + 1]
                decay = jnp.exp(jnp.minimum(lr - lcol, 30.0))
                mixed.append((decay * sm).astype(BF16))
                a = dm[j * sh:(j + 1) * sh] * decay
                add = a if add is None else add + a
                w = a * sm
                col_e[2 * p + j, :, part] = jnp.sum(w, axis=0, keepdims=True)
                dr = dr + jnp.where(lane[:sh] == 2 * p + j, jnp.sum(w, axis=1, keepdims=True), 0.0)
            direct[part] = dr
            dst[k] += add
            gx = dot(jnp.concatenate(mixed, axis=0), gt)
            gxi[part, cols] = jnp.where(low, gx[:sh], gx[sh:])

    def two(ref, q):
        return jnp.concatenate([ref[2 * q], ref[2 * q + 1]], axis=1)

    def from_before(q):
        cols = columns(q, 2)
        for k, ref in enumerate((rf, smid)):
            part = slice(k * sh, (k + 1) * sh)
            s_in = two(ref, q)
            car = gs[part, cols].astype(F32) * dot(c_all[part], s_in)
            gl[part] += dot_sel(car, sel[:, cols])
            gacc_c[part] += dot(gs[part, cols], s_in, NT)

    def from_after(q):
        cols = columns(q, 2)
        for k, ref in enumerate((gmid, rb)):
            part = slice(k * sh, (k + 1) * sh)
            s_out = two(ref, q)
            br = e1_b[part, cols] * dot(b_all[part], s_out)
            gval[part, cols] = (gxi[part, cols] + br).astype(BF16)
            qd[part] += dot_sel(x[part, cols].astype(F32) * br, sel[:, cols])
            gacc_b[part] += dot(xs[part, cols], s_out, NT)

    def through(q):
        cols = columns(q, 2)
        for k, (before, after) in enumerate(((rf, gmid), (smid, rb))):
            both_ends = two(before, q).astype(F32) * two(after, q).astype(F32)
            tails[k:k + 1, cols] = ends_b[k:k + 1, cols] * jnp.sum(both_ends, axis=0, keepdims=True)

    def turn(i, carry):
        pf = i - z * stride
        pb = i - (zn - 1 - z) * stride
        in_f, in_b = (pf >= 0) & (pf < pairs), (pb >= 0) & (pb < pairs)

        @pl.when(in_f & (z > 0))
        def _():
            with jax.named_scope("forward"):
                chain_f(pf).wait_recv()
                forward(pf)

        @pl.when(in_b & (z < zn - 1))
        def _():
            with jax.named_scope("backward"):
                chain_b(pb).wait_recv()
                backward(pb)

        @pl.when(i < pairs)
        def _():
            with jax.named_scope("local"):
                local_pair(i)

        kf = i - jnp.where(z == 0, 1, jnp.maximum(z * stride + 1, pairs))
        kb = i - jnp.where(z == zn - 1, 1, jnp.maximum((zn - 1 - z) * stride + 1, pairs))

        @pl.when((kf >= 0) & (kf < pairs) & (kf % 2 == 0))
        def _():
            with jax.named_scope("before"):
                from_before(kf // 2)

        @pl.when((kb >= 0) & (kb < pairs) & (kb % 2 == 0))
        def _():
            with jax.named_scope("after"):
                from_after(kb // 2)

        kt = i - jnp.maximum(z, zn - 1 - z) * stride - 1

        @pl.when((kt >= 0) & (kt < pairs) & (kt % 2 == 0))
        def _():
            with jax.named_scope("through"):
                through(kt // 2)

        return carry

    lax.fori_loop(0, pairs + max((zn - 1) * stride + 1, pairs), turn, 0)

    with jax.named_scope("state map gradients"):
        d_masked = [jnp.where(causal, dst[k], 0.0).astype(BF16) for k in range(2)]
        for k in range(2):
            part = slice(k * sh, (k + 1) * sh)
            px[hx, 0, part] = (gacc_b[part] + dot(d_masked[k], c_all[part])).astype(BF16)
            px[hx, 1, part] = (gacc_c[part] + dot(d_masked[k], b_all[part], TN)).astype(BF16)
        first_part = 1 - hx if split else 0
        for k in range(1, hn):
            maps_copy(first_part, k).start()
        for k in range(1, hn):
            maps_copy(1 - first_part, k).start()

    with jax.named_scope("step gradients"):
        upper = ((ti <= si) & ((ti < sh) == (si < sh))).astype(F32).astype(BF16)
        carried = qd[...]
        weighted = direct[...] + carried
        for h in range(heads):
            erows[h:h + 1, :] = col_e[h]
        g_log = gl[...] + erows[...].T - weighted
        ends_sum = sum(dot(part, sel[...], NT) for part in split3(tails[...]))
        tail = [
            jnp.sum(carried[k * sh:(k + 1) * sh], axis=0, keepdims=True) + ends_sum[k:k + 1] for k in range(2)
        ]
        back = dot_ones(upper, g_log) + jnp.where(first, tail[0], tail[1])
        gate = jax.nn.sigmoid(pre)
        per_delta = jnp.where(delta > 1e-30, gate / jnp.maximum(delta, 1e-30), 1.0)
        g_pre = weighted * per_delta + rate * back * gate
        smsend[...] = jnp.zeros_like(smsend)
        smsend[0:1, :] = jnp.sum(g_pre, axis=0, keepdims=True)
        smsend[1:2, :] = jnp.sum(delta * back, axis=0, keepdims=True) * rate
    gpx[hx] = g_pre.T[:rpad, :].astype(BF16)
    for k in range(1, hn):
        steps_copy(k).start()
    with jax.named_scope("step weight product"):
        wsend[...] = dot(gpx[hx], uu).astype(BF16)

    other = {"batch": lax.rem(bt + 1, bn)}

    def core_copy(i, src, to):
        return pltpu.make_async_remote_copy(src, to, c_ss.at[i], c_rs.at[i], device_id=other, device_id_type=MESH)

    core_w = core_copy(0, wsend, wrecv)
    core_s = core_copy(1, smsend, smrecv)
    core_p = core_copy(2, csend, crecv)
    core_f = core_copy(3, wfsend, wfrecv)
    core_w.start()
    core_s.start()

    def along(i, src, to, k):
        there = lax.rem(z + k, zn)
        return pltpu.make_async_remote_copy(
            src, to.at[z], z_ss.at[i, k], z_rs.at[i, k], device_id={"tm": there}, device_id_type=MESH
        )

    def each_z(body):
        def turn(k, carry):
            body(k)
            return carry

        lax.fori_loop(1, zn, turn, 0)

    def z_start_small(k):
        along(0, wzsend, wzrecv, k).start()
        along(1, smzsend, smzrecv, k).start()

    def z_start_large(k):
        along(2, zsend.at[lax.rem(z + k, zn)], zrecv, k).start()

    def z_wait_small(k):
        along(0, wzsend, wzrecv, k).wait()
        along(1, smzsend, smzrecv, k).wait()

    def z_wait_large(k):
        along(2, zsend.at[lax.rem(z + k, zn)], zrecv, k).wait()

    with jax.named_scope("core w"):
        core_w.wait()
    core_s.wait()
    wsum[...] = wsend[...].astype(F32) + wrecv[...].astype(F32)
    mine = pl.ds(pl.multiple_of(bt * half, LANES), half)
    theirs = pl.ds(pl.multiple_of(lax.rem(bt + 1, bn) * half, LANES), half)
    wz = wsum[:, mine].astype(BF16)
    wzsend[...] = wz
    wzrecv[z] = wz
    sz = smsend[...] + smrecv[...]
    smzsend[...] = sz
    smzrecv[z] = sz
    each_z(z_start_small)

    def both_heads(part):
        total = px[0, part].astype(F32)
        for k in range(1, hn):
            total = total + px[k, part].astype(F32)
        return total.astype(BF16)

    wide = zrecv.shape[2]
    with jax.named_scope("wait for heads"):
        for k in range(1, hn):
            maps_copy(first_part, k).wait_send()
            maps_copy(1 - first_part, k).wait_recv()
            if not split:
                maps_copy(first_part, k).wait_recv()
    if split:
        piece = both_heads(hx)
    else:
        piece = jnp.concatenate([both_heads(0), both_heads(1)], axis=1)
    block = zrecv.shape[1]
    with jax.named_scope("weight product"):
        local = dot(ut[...], piece)
    for k in range(zn * bn):
        plocal[k] = local[k * block:(k + 1) * block, :]
    for k in range(zn):
        csend[k] = plocal[k * bn + lax.rem(bt + 1, bn)].astype(BF16)
    core_p.start()

    with jax.named_scope("core p"):
        core_p.wait()
    for k in range(zn):
        zsend[k] = (plocal[k * bn + bt] + crecv[k].astype(F32)).astype(BF16)
    zrecv[z] = zsend[z]
    each_z(z_start_large)

    for k in range(1, hn):
        weights_copy(k).wait()
        steps_copy(k).wait()
        maps_copy(1 - first_part, k).wait_send()
        if split:
            maps_copy(first_part, k).wait_recv()
    gp = jnp.concatenate([both_heads(0), both_heads(1)], axis=1)
    gpa = gpx[...].reshape(hn * rpad, tokens).astype(F32).T.astype(BF16)
    wa = wx[...].reshape(hn * rpad, width)
    with jax.named_scope("input gradient"):
        gin[...] = (dot(gp, wbc[...], NT) + dot(gpa, wa)).astype(BF16)

    with jax.named_scope("small along z"):
        each_z(z_wait_small)
    total_w = wzrecv[0].astype(F32)
    total_s = smzrecv[0]
    for k in range(1, zn):
        total_w = total_w + wzrecv[k].astype(F32)
        total_s = total_s + smzrecv[k]
    wfsend[...] = total_w
    core_f.start()
    gbias[...] = total_s[0:1, :heads]
    galog[...] = total_s[1:2, :heads]
    gwdt[:, mine] = total_w[:heads, :]

    with jax.named_scope("large along z"):
        each_z(z_wait_large)
    total = zrecv[0].astype(F32)
    for k in range(1, zn):
        total = total + zrecv[k].astype(F32)
    if split:
        fsend[...] = total.astype(BF16)
        final = pltpu.make_async_remote_copy(
            fsend, frecv, c_ss.at[4], c_rs.at[4], device_id={"head": lax.rem(hx + 1, hn)}, device_id_type=MESH
        )
        final.start()
        gwbc[:, pl.ds(pl.multiple_of(hx * wide, LANES), wide)] = total
        with jax.named_scope("last exchange"):
            final.wait()
        gwbc[:, pl.ds(pl.multiple_of((1 - hx) * wide, LANES), wide)] = frecv[...].astype(F32)
    else:
        gwbc[...] = total
    with jax.named_scope("core f"):
        core_f.wait()
    gwdt[:, theirs] = wfrecv[:heads, :]

    def drain(c, carry):
        @pl.when(z < zn - 1)
        def _():
            chain_f(c).wait_send()

        @pl.when(z > 0)
        def _():
            chain_b(c).wait_send()

        return carry

    with jax.named_scope("drain"):
        lax.fori_loop(0, pairs, drain, 0)


def on_device(sizes, u_input, head_values, grad_output, w_bc, w_dt, dt_bias, a_log):
    zn, hn, bn = sizes
    seqs, tokens, width = u_input.shape
    assert seqs == 1 and bn == 2
    heads = w_dt.shape[1]
    values = head_values.shape[2]
    both = w_bc.shape[1]
    pairs = heads // 2
    assert values == heads * 64 and both == 2 * LANES and heads % 4 == 0 and heads <= 32 and tokens == 2 * LANES
    split = hn == 2
    wide = both // 2 if split else both
    block = width // (zn * bn)
    rpad = -(-heads // 16) * 16
    half = width // bn
    sh = tokens // 2
    vm = pltpu.VMEM
    dma = pltpu.SemaphoreType.DMA
    scratch = [
        vm((tokens, width), BF16), vm((tokens, values), BF16), vm((tokens, values), BF16), vm((width, both), BF16),
        vm((heads, width), BF16), vm((1, heads), F32), vm((1, heads), F32), dma((7,)),
        vm((LANES, width), BF16), vm((width, tokens), BF16), vm((8, LANES), F32), vm((tokens, both), BF16),
        vm((heads, 1, tokens), F32), vm((tokens, values), F32), vm((tokens, values), F32),
        vm((tokens, LANES), BF16), vm((tokens, LANES), BF16),
        vm((8, values), F32), vm((LANES, values), BF16), vm((tokens, values), BF16), vm((tokens, values), BF16),
        vm((2, pairs, LANES, LANES), F32), vm((2, pairs, LANES, LANES), F32), vm((tokens, values), F32),
        vm((2, sh, sh), F32), vm((2, sh, sh), F32), vm((heads, 1, tokens), F32), vm((LANES, tokens), F32),
        vm((tokens, LANES), F32), vm((tokens, LANES), F32), vm((tokens, LANES), F32), vm((8, values), F32),
        vm((tokens, LANES), F32), vm((tokens, LANES), F32),
        vm((pairs, LANES, LANES), BF16), vm((pairs, LANES, LANES), BF16),
        vm((pairs, LANES, LANES), BF16), vm((pairs, LANES, LANES), BF16),
        vm((pairs, LANES, LANES), BF16), vm((pairs, LANES, LANES), BF16),
        vm((hn, rpad, width), BF16), vm((hn, 2, tokens, LANES), BF16), vm((hn, rpad, tokens), BF16),
        vm((zn, block, wide), BF16), vm((zn, block, wide), BF16), vm((zn * bn, block, wide), F32),
        vm((zn, block, wide), BF16), vm((zn, block, wide), BF16), vm((block, wide), BF16), vm((block, wide), BF16),
        vm((rpad, width), BF16), vm((rpad, width), BF16), vm((rpad, width), F32),
        vm((rpad, half), BF16), vm((zn, rpad, half), BF16), vm((rpad, half), F32), vm((rpad, half), F32),
        vm((8, LANES), F32), vm((8, LANES), F32), vm((8, LANES), F32), vm((zn, 8, LANES), F32),
        dma((pairs,)), dma((pairs,)), dma((pairs,)), dma((pairs,)),
        dma((4, hn)), dma((4, hn)), dma((5,)), dma((5,)), dma((3, zn)), dma((3, zn)),
    ]
    spec = pl.BlockSpec(memory_space=pltpu.VMEM)
    shapes = (
        ((tokens, width), BF16), ((tokens, values), BF16), ((block, both), F32),
        ((heads, width), F32), ((1, heads), F32), ((1, heads), F32),
    )
    kept = pl.pallas_call(
        functools.partial(kernel, zn, hn, bn, heads, split),
        out_shape=tuple(vm(*s) for s in shapes),
        in_specs=[pl.BlockSpec(memory_space=pl.ANY)] * 7,
        out_specs=[spec] * 6,
        scratch_shapes=scratch,
        compiler_params=pltpu.CompilerParams(
            collective_id=0, has_side_effects=True, vmem_limit_bytes=56 << 20
        ),
    )(
        u_input.reshape(tokens, width), head_values.reshape(tokens, values), grad_output.reshape(tokens, values),
        w_bc, w_dt.T, dt_bias.reshape(1, heads), a_log.reshape(1, heads),
    )
    gin, gval, gwbc, gwdt, gbias, galog = pl.pallas_call(
        write,
        out_shape=tuple(jax.ShapeDtypeStruct(*s) for s in shapes),
        in_specs=[spec] * 6,
        out_specs=[pl.BlockSpec(memory_space=pl.ANY)] * 6,
        scratch_shapes=[dma((6,))],
        compiler_params=pltpu.CompilerParams(vmem_limit_bytes=1 << 20),
    )(*kept)
    return (
        gin.reshape(1, tokens, width), gval.reshape(1, tokens, values), gwbc,
        gwdt.T, gbias.reshape(heads), galog.reshape(heads),
    )


def write(*refs):
    sems = refs[12]
    copies = [pltpu.make_async_copy(refs[i], refs[6 + i], sems.at[i]) for i in range(6)]
    for copy in copies:
        copy.start()
    for copy in copies:
        copy.wait()


def solution(mesh):
    sizes = (mesh.shape["tm"], mesh.shape["head"], mesh.shape["batch"])
    return jax.shard_map(
        functools.partial(on_device, sizes),
        mesh=mesh,
        in_specs=(
            P(("groups", "batch"), "tm", None),
            P(("groups", "batch"), "tm", "head"),
            P(("groups", "batch"), "tm", "head"),
            P(),
            P(None, "head"),
            P("head"),
            P("head"),
        ),
        out_specs=(
            P(("groups", "batch"), "tm", None),
            P(("groups", "batch"), "tm", "head"),
            P(("groups", "tm", "batch"), None),
            P("groups", "head"),
            P(("groups", "head")),
            P(("groups", "head")),
        ),
        check_vma=False,
    )
```

```python
import functools
import math

import jax
import jax.numpy as jnp
from jax import lax
from jax.experimental import pallas as pl
from jax.experimental.pallas import tpu as pltpu
from jax.sharding import PartitionSpec as P

MESH = pl.DeviceIdType.MESH
F32 = jnp.float32
BF16 = jnp.bfloat16
LANES = 128
NT = (((1,), (1,)), ((), ()))
TN = (((0,), (0,)), ((), ()))


def dot(a, b, dims=(((1,), (0,)), ((), ()))):
    return lax.dot_general(a, b, dims, preferred_element_type=F32)


def split3(v):
    hi = v.astype(BF16)
    rest = v - hi.astype(F32)
    mid = rest.astype(BF16)
    return hi, mid, (rest - mid.astype(F32)).astype(BF16)


def dot_ones(a, v):
    hi, mid, lo = split3(v)
    return dot(a, hi) + dot(a, mid) + dot(a, lo)


def dot_sel(v, ones):
    hi = v.astype(BF16)
    lo = (v - hi.astype(F32)).astype(BF16)
    return dot(hi, ones, NT) + dot(lo, ones, NT)


def kernel(
    zn, hn, bn, heads, split,
    u_h, x_h, g_h, wbc_h, wdt_h, bias_h, alog_h,
    gin, gval, gwbc, gwdt, gbias, galog,
    u, x, g, wbc, wdt, bias, alog, in_s,
    wpad, ut, uto, rows, proj, l_t, l_b, e1_b, e1_p, e2_p, ends_b, sel, xs, gs, own_f, own_b, gxi, st, dst, col_e, erows,
    direct, qd, gl, tails, gacc_b, gacc_c, smid, gmid,
    sf, rf, sb, rb, wx, px, gpx, psend, precv, plocal, zsend, zrecv, fsend, frecv,
    wsend, wrecv, wsum, wzsend, wzrecv, wgrecv, wfsend, wfrecv, smsend, smrecv, smzsend, smzrecv,
    f_ss, f_rs, b_ss, b_rs, h_ss, h_rs, c_ss, c_rs, z_ss, z_rs,
):
    z, hx, bt = lax.axis_index("tm"), lax.axis_index("head"), lax.axis_index("batch")
    tokens, width = u.shape
    pairs = heads // 2
    groups = pairs // 2
    stride = 4
    state = LANES
    sh = tokens // 2
    rpad = wx.shape[1]
    half = width // bn
    units, unit_rows, unit = wzsend.shape
    unit_cols = half // unit

    loads = [
        pltpu.make_async_copy(src, to, in_s.at[i])
        for i, (src, to) in enumerate((
            (wdt_h, wdt), (bias_h, bias), (alog_h, alog), (u_h, u), (wbc_h, wbc), (x_h, x), (g_h, g)
        ))
    ]
    for load in loads[:3]:
        load.start()
    for j, (src, to, n) in enumerate(((u_h, u, 4), (wbc_h, wbc, 4), (x_h, x, 2), (g_h, g, 2))):
        step = src.shape[0] // n
        for i in range(n):
            at = pl.ds(i * step, step)
            pltpu.make_async_copy(src.at[at], to.at[at], in_s.at[3 + j]).start()

    barrier = pltpu.get_barrier_semaphore()
    for k in range(1, zn):
        pl.semaphore_signal(barrier, inc=1, device_id={"tm": lax.rem(z + k, zn)}, device_id_type=MESH)
    for k in range(1, hn):
        pl.semaphore_signal(barrier, inc=1, device_id={"head": lax.rem(hx + k, hn)}, device_id_type=MESH)
    for k in range(1, bn):
        pl.semaphore_signal(barrier, inc=1, device_id={"batch": lax.rem(bt + k, bn)}, device_id_type=MESH)

    lane = lax.broadcasted_iota(jnp.int32, (tokens, LANES), 1)
    low = lax.broadcasted_iota(jnp.int32, (sh, LANES), 1) < 64
    lm = low.astype(F32).astype(BF16)
    hm = 1.0 - lm
    ti = lax.broadcasted_iota(jnp.int32, (tokens, tokens), 0)
    si = lax.broadcasted_iota(jnp.int32, (tokens, tokens), 1)
    lower = (ti >= si).astype(F32).astype(BF16)
    causal = ti[:sh, :sh] <= si[:sh, :sh]

    with jax.named_scope("initial"):
        wpad[...] = jnp.zeros_like(wpad)
        rows[...] = jnp.zeros_like(rows)
        which = lax.broadcasted_iota(jnp.int32, (LANES, LANES), 0)
        head_of = lax.shift_right_logical(lax.broadcasted_iota(jnp.int32, (LANES, LANES), 1), 6)
        used = jnp.where(which < 96, which & 31, -1)
        for p in range(pairs):
            sel[:, p * LANES:(p + 1) * LANES] = (used == head_of + 2 * p).astype(F32).astype(BF16)
        dst[...] = jnp.zeros_like(dst)
        direct[...] = jnp.zeros_like(direct)
        gl[...] = jnp.zeros_like(gl)
        qd[...] = jnp.zeros_like(qd)
        gacc_b[...] = jnp.zeros_like(gacc_b)
        gacc_c[...] = jnp.zeros_like(gacc_c)
        tails[...] = jnp.zeros_like(tails)
        erows[...] = jnp.zeros_like(erows)

        @pl.when(z == 0)
        def _():
            rf[...] = jnp.zeros_like(rf)

        @pl.when(z == zn - 1)
        def _():
            rb[...] = jnp.zeros_like(rb)

    def packed(v):
        hi, mid, lo = split3(v)
        at = lane[:v.shape[0]]
        mid, lo = pltpu.roll(mid.astype(F32), 32, 1), pltpu.roll(lo.astype(F32), 64, 1)
        return jnp.where(at < 32, hi.astype(F32), jnp.where(at < 64, mid, jnp.where(at < 96, lo, 0.0))).astype(BF16)

    with jax.named_scope("wait for u"):
        for load in loads[:5]:
            load.wait()
    wpad[:heads, :] = wdt[...]
    rows[0:1, :heads] = bias[...]
    rows[1:2, :heads] = alog[...]
    wx[hx] = wpad[:rpad, :]
    uu = u[...]
    proj[...] = dot(uu, wbc[...]).astype(BF16)
    b_all, c_all = proj[:, :state], proj[:, state:]
    b_t = b_all.astype(F32).T.astype(BF16)
    c_t = c_all.astype(F32).T.astype(BF16)
    pre = dot(uu, wpad[...], NT) + rows[0:1, :]
    small = jnp.exp(-jnp.abs(pre))
    delta = jnp.maximum(pre, 0.0) + jnp.log1p(small)
    rate = -jnp.exp(rows[1:2, :])
    log_decay = dot_ones(lower, delta * rate)
    l_rows = log_decay.T
    for h in range(heads):
        l_t[h] = l_rows[h:h + 1, :]
    mid_l, last_l = log_decay[sh - 1:sh, :], log_decay[tokens - 1:tokens, :]
    first = lax.broadcasted_iota(jnp.int32, (tokens, LANES), 0) < sh
    e1 = packed(jnp.exp(jnp.where(first, mid_l, last_l) - log_decay) * delta)
    e2 = packed(jnp.exp(jnp.where(first, log_decay, log_decay - mid_l)))
    lc = packed(log_decay - jnp.log(jnp.maximum(delta, 1e-37)))
    e1_p[...] = e1
    e2_p[...] = e2
    ends = jnp.concatenate([jnp.exp(mid_l), jnp.exp(last_l - mid_l), jnp.zeros((6, LANES), F32)], axis=0)
    ends_b[...] = dot(packed(ends), sel[...])
    with jax.named_scope("wait for values"):
        loads[5].wait()
        loads[6].wait()
    with jax.named_scope("wait for devices"):
        pl.semaphore_wait(barrier, zn + hn + bn - 3)

    def head_copy(i, ref, k):
        return pltpu.make_async_remote_copy(
            ref, ref, h_ss.at[i, k - 1], h_rs.at[i, k - 1],
            device_id={"head": lax.rem(hx + k, hn)}, device_id_type=MESH,
        )

    def weights_copy(k):
        return head_copy(0, wx.at[hx], k)

    def steps_copy(k):
        return head_copy(1, gpx.at[hx], k)

    def maps_copy(part, k):
        return head_copy(2 + part, px.at[hx, part], k)

    def chain_f(p):
        return pltpu.make_async_remote_copy(
            sf.at[p], rf.at[p], f_ss, f_rs.at[p],
            device_id={"tm": lax.rem(z + 1, zn)}, device_id_type=MESH,
        )

    def chain_b(p):
        return pltpu.make_async_remote_copy(
            sb.at[p], rb.at[p], b_ss, b_rs.at[p],
            device_id={"tm": lax.rem(z + zn - 1, zn)}, device_id_type=MESH,
        )

    def columns(p, n=1):
        return pl.ds(pl.multiple_of(p * n * LANES, LANES), n * LANES)

    def forward(p):
        cols = columns(p)
        middle = ends_b[0:1, cols] * rf[p].astype(F32) + own_f[0, p]
        smid[p] = middle.astype(BF16)
        sf[p] = (ends_b[1:2, cols] * middle + own_f[1, p]).astype(BF16)

        @pl.when(z < zn - 1)
        def _():
            chain_f(p).start()

    def backward(p):
        cols = columns(p)
        middle = ends_b[1:2, cols] * rb[p].astype(F32) + own_b[1, p]
        gmid[p] = middle.astype(BF16)
        sb[p] = (ends_b[0:1, cols] * middle + own_b[0, p]).astype(BF16)

        @pl.when(z > 0)
        def _():
            chain_b(p).start()

    def summarize(q, carry):
        cols = columns(q, 2)
        spread = dot(e1_p[...], sel[:, cols])
        e1_b[:, cols] = spread
        xv = (spread * x[:, cols].astype(F32)).astype(BF16)
        gv = (dot(e2_p[...], sel[:, cols]) * g[:, cols].astype(F32)).astype(BF16)
        xs[:, cols] = xv
        gs[:, cols] = gv
        for k in range(2):
            part = slice(k * sh, (k + 1) * sh)
            of, ob = dot(b_t[:, part], xv[part]), dot(c_t[:, part], gv[part])
            for j in range(2):
                own_f[k, 2 * q + j] = of[:, j * LANES:(j + 1) * LANES]
                own_b[k, 2 * q + j] = ob[:, j * LANES:(j + 1) * LANES]

        @pl.when(z == 0)
        def _():
            forward(2 * q)
            forward(2 * q + 1)

        @pl.when(z == zn - 1)
        def _():
            backward(2 * q)
            backward(2 * q + 1)

        return carry

    with jax.named_scope("summaries"):
        lax.fori_loop(0, groups, summarize, 0)

    for k in range(1, hn):
        weights_copy(k).start()

    with jax.named_scope("scores"):
        l_b[...] = dot(lc, sel[...])
        for k in range(2):
            part = slice(k * sh, (k + 1) * sh)
            st[k] = jnp.where(causal, dot(b_all[part], c_all[part], NT), 0.0)
    other = {"batch": lax.rem(bt + 1, bn)}

    def core_copy(i, src, to):
        return pltpu.make_async_remote_copy(src, to, c_ss.at[i], c_rs.at[i], device_id=other, device_id_type=MESH)

    block = uto.shape[1]
    chunk = math.lcm(block, LANES)
    for c in range(width // chunk):
        turned = u[:, c * chunk:(c + 1) * chunk].astype(F32).T
        for i in range(chunk // block):
            k, b = divmod(c * (chunk // block) + i, bn)
            ut[b, k] = turned[i * block:(i + 1) * block].astype(BF16)
    core_u = core_copy(5, ut.at[lax.rem(bt + 1, bn)], uto)
    core_u.start()

    def local_pair(p):
        cols = columns(p)
        for k in range(2):
            part = slice(k * sh, (k + 1) * sh)
            gt = g[part, cols]
            xb = x[part, cols]
            sm = st[k]
            dm = dot(jnp.concatenate([xb * lm, xb * hm], axis=0), gt, NT)
            add = None
            mixed = []
            dr = direct[part]
            for j in range(2):
                lr = l_t[2 * p + j][:, part]
                lcol = l_b[part, cols][:, 64 * j:64 * j + 1]
                decay = jnp.exp(jnp.minimum(lr - lcol, 30.0))
                mixed.append((decay * sm).astype(BF16))
                a = dm[j * sh:(j + 1) * sh] * decay
                add = a if add is None else add + a
                w = a * sm
                col_e[2 * p + j, :, part] = jnp.sum(w, axis=0, keepdims=True)
                dr = dr + jnp.where(lane[:sh] == 2 * p + j, jnp.sum(w, axis=1, keepdims=True), 0.0)
            direct[part] = dr
            dst[k] += add
            gx = dot(jnp.concatenate(mixed, axis=0), gt)
            gxi[part, cols] = jnp.where(low, gx[:sh], gx[sh:])

    def two(ref, q):
        return jnp.concatenate([ref[2 * q], ref[2 * q + 1]], axis=1)

    def from_before(q):
        cols = columns(q, 2)
        for k, ref in enumerate((rf, smid)):
            part = slice(k * sh, (k + 1) * sh)
            s_in = two(ref, q)
            car = gs[part, cols].astype(F32) * dot(c_all[part], s_in)
            gl[part] += dot_sel(car, sel[:, cols])
            gacc_c[part] += dot(gs[part, cols], s_in, NT)

    def from_after(q):
        cols = columns(q, 2)
        for k, ref in enumerate((gmid, rb)):
            part = slice(k * sh, (k + 1) * sh)
            s_out = two(ref, q)
            br = e1_b[part, cols] * dot(b_all[part], s_out)
            gval[part, cols] = (gxi[part, cols] + br).astype(BF16)
            qd[part] += dot_sel(x[part, cols].astype(F32) * br, sel[:, cols])
            gacc_b[part] += dot(xs[part, cols], s_out, NT)

    def through(q):
        cols = columns(q, 2)
        for k, (before, after) in enumerate(((rf, gmid), (smid, rb))):
            both_ends = two(before, q).astype(F32) * two(after, q).astype(F32)
            tails[k:k + 1, cols] = ends_b[k:k + 1, cols] * jnp.sum(both_ends, axis=0, keepdims=True)

    def turn(i, carry):
        pf = i - z * stride
        pb = i - (zn - 1 - z) * stride
        in_f, in_b = (pf >= 0) & (pf < pairs), (pb >= 0) & (pb < pairs)

        @pl.when(in_f & (z > 0))
        def _():
            with jax.named_scope("forward"):
                chain_f(pf).wait_recv()
                forward(pf)

        @pl.when(in_b & (z < zn - 1))
        def _():
            with jax.named_scope("backward"):
                chain_b(pb).wait_recv()
                backward(pb)

        @pl.when(i < pairs)
        def _():
            with jax.named_scope("local"):
                local_pair(i)

        kf = i - jnp.where(z == 0, 1, jnp.maximum(z * stride + 1, pairs))
        kb = i - jnp.where(z == zn - 1, 1, jnp.maximum((zn - 1 - z) * stride + 1, pairs))

        @pl.when((kf >= 0) & (kf < pairs) & (kf % 2 == 0))
        def _():
            with jax.named_scope("before"):
                from_before(kf // 2)

        @pl.when((kb >= 0) & (kb < pairs) & (kb % 2 == 0))
        def _():
            with jax.named_scope("after"):
                from_after(kb // 2)

        kt = i - jnp.maximum(z, zn - 1 - z) * stride - 1

        @pl.when((kt >= 0) & (kt < pairs) & (kt % 2 == 0))
        def _():
            with jax.named_scope("through"):
                through(kt // 2)

        return carry

    lax.fori_loop(0, pairs + max((zn - 1) * stride + 1, pairs), turn, 0)

    with jax.named_scope("state map gradients"):
        d_masked = [jnp.where(causal, dst[k], 0.0).astype(BF16) for k in range(2)]
        for k in range(2):
            part = slice(k * sh, (k + 1) * sh)
            px[hx, 0, part] = (gacc_b[part] + dot(d_masked[k], c_all[part])).astype(BF16)
            px[hx, 1, part] = (gacc_c[part] + dot(d_masked[k], b_all[part], TN)).astype(BF16)
        first_part = 1 - hx if split else 0
        for k in range(1, hn):
            maps_copy(first_part, k).start()

    with jax.named_scope("step gradients"):
        upper = ((ti <= si) & ((ti < sh) == (si < sh))).astype(F32).astype(BF16)
        carried = qd[...]
        weighted = direct[...] + carried
        for h in range(heads):
            erows[h:h + 1, :] = col_e[h]
        g_log = gl[...] + erows[...].T - weighted
        ends_sum = sum(dot(part, sel[...], NT) for part in split3(tails[...]))
        tail = [
            jnp.sum(carried[k * sh:(k + 1) * sh], axis=0, keepdims=True) + ends_sum[k:k + 1] for k in range(2)
        ]
        back = dot_ones(upper, g_log) + jnp.where(first, tail[0], tail[1])
        gate = jax.nn.sigmoid(pre)
        per_delta = jnp.where(delta > 1e-30, gate / jnp.maximum(delta, 1e-30), 1.0)
        g_pre = weighted * per_delta + rate * back * gate
        smsend[...] = jnp.zeros_like(smsend)
        smsend[0:1, :] = jnp.sum(g_pre, axis=0, keepdims=True)
        smsend[1:2, :] = jnp.sum(delta * back, axis=0, keepdims=True) * rate
    gpx[hx] = g_pre.T[:rpad, :].astype(BF16)
    for k in range(1, hn):
        maps_copy(1 - first_part, k).start()
        steps_copy(k).start()
    with jax.named_scope("step weight product"):
        wsend[...] = dot(gpx[hx], uu).astype(BF16)

    core_w = core_copy(0, wsend, wrecv)
    core_s = core_copy(1, smsend, smrecv)
    core_p = core_copy(2, psend, precv)
    core_f = core_copy(3, wfsend, wfrecv)
    core_w.start()
    core_s.start()

    def along(i, src, to, k):
        there = lax.rem(z + k, zn)
        return pltpu.make_async_remote_copy(
            src, to.at[z], z_ss.at[i, k - 1], z_rs.at[i, k - 1], device_id={"tm": there}, device_id_type=MESH
        )

    def each_z(body):
        def turn(k, carry):
            body(k)
            return carry

        lax.fori_loop(1, zn, turn, 0)

    def z_start_small(k):
        along(0, wzsend.at[lax.rem(z + k, zn) if units > 1 else 0], wzrecv, k).start()
        along(1, smzsend, smzrecv, k).start()

    def z_start_large(k):
        along(2, zsend.at[lax.rem(z + k, zn)], zrecv, k).start()

    def z_wait_small(k):
        along(0, wzsend.at[lax.rem(z + k, zn) if units > 1 else 0], wzrecv, k).wait()
        along(1, smzsend, smzrecv, k).wait()

    def z_start_sums(k):
        along(3, wgrecv.at[z], wgrecv, k).start()

    def z_wait_sums(k):
        along(3, wgrecv.at[z], wgrecv, k).wait()

    def z_wait_large(k):
        along(2, zsend.at[lax.rem(z + k, zn)], zrecv, k).wait()

    with jax.named_scope("core w"):
        core_w.wait()
    core_s.wait()
    wsum[...] = wsend[...].astype(F32) + wrecv[...].astype(F32)
    mine = pl.ds(pl.multiple_of(bt * half, LANES), half)
    theirs = pl.ds(pl.multiple_of(lax.rem(bt + 1, bn) * half, LANES), half)
    for k in range(units):
        r, c = divmod(k, unit_cols)
        cols = pl.ds(pl.multiple_of(bt * half + c * unit, LANES), unit)
        wzsend[k] = wsum[r * unit_rows:(r + 1) * unit_rows, cols].astype(BF16)
    own_unit = z if units > 1 else 0
    wzrecv[z] = wzsend[own_unit]
    sz = smsend[...] + smrecv[...]
    smzsend[...] = sz
    smzrecv[z] = sz
    each_z(z_start_small)

    def both_heads(part):
        total = px[0, part].astype(F32)
        for k in range(1, hn):
            total = total + px[k, part].astype(F32)
        return total.astype(BF16)

    wide = zrecv.shape[2]
    with jax.named_scope("wait for heads"):
        for k in range(1, hn):
            maps_copy(first_part, k).wait_send()
            maps_copy(1 - first_part, k).wait_recv()
            if not split:
                maps_copy(first_part, k).wait_recv()
    if split:
        piece = both_heads(hx)
    else:
        piece = jnp.concatenate([both_heads(0), both_heads(1)], axis=1)
    psend[...] = piece
    core_p.start()

    def product(ref, values):
        if block % 16 == 0:
            return dot(ref[...].reshape(zn * block, tokens), values).reshape(zn, block, wide)
        return jnp.stack([dot(ref[k], values) for k in range(zn)])

    with jax.named_scope("weight product"):
        plocal[...] = product(ut.at[bt], piece)
    core_u.wait()
    with jax.named_scope("core p"):
        core_p.wait()
    with jax.named_scope("weight product"):
        zsend[...] = (plocal[...] + product(uto, precv[...])).astype(BF16)
    zrecv[z] = zsend[z]
    each_z(z_start_large)

    with jax.named_scope("small along z"):
        each_z(z_wait_small)
    total_w = wzrecv[0].astype(F32)
    total_s = smzrecv[0]
    for k in range(1, zn):
        total_w = total_w + wzrecv[k].astype(F32)
        total_s = total_s + smzrecv[k]
    wgrecv[own_unit] = total_w.astype(BF16)
    if units > 1:
        each_z(z_start_sums)
    gbias[...] = total_s[0:1, :heads]
    galog[...] = total_s[1:2, :heads]

    for k in range(1, hn):
        weights_copy(k).wait()
        steps_copy(k).wait()
        maps_copy(1 - first_part, k).wait_send()
        if split:
            maps_copy(first_part, k).wait_recv()
    gp = jnp.concatenate([both_heads(0), both_heads(1)], axis=1)
    gpa = gpx[...].reshape(hn * rpad, tokens).astype(F32).T.astype(BF16)
    wa = wx[...].reshape(hn * rpad, width)
    with jax.named_scope("input gradient"):
        gin[...] = (dot(gp, wbc[...], NT) + dot(gpa, wa)).astype(BF16)

    with jax.named_scope("large along z"):
        each_z(z_wait_large)
    total = zrecv[0].astype(F32)
    for k in range(1, zn):
        total = total + zrecv[k].astype(F32)
    if split:
        fsend[...] = total.astype(BF16)
        final = pltpu.make_async_remote_copy(
            fsend, frecv, c_ss.at[4], c_rs.at[4], device_id={"head": lax.rem(hx + 1, hn)}, device_id_type=MESH
        )
        final.start()

    with jax.named_scope("sums along z"):
        if units > 1:
            each_z(z_wait_sums)
    for k in range(units):
        r, c = divmod(k, unit_cols)
        wfsend[r * unit_rows:(r + 1) * unit_rows, c * unit:(c + 1) * unit] = wgrecv[k]
    core_f.start()
    gwdt[:, mine] = wfsend[...].astype(F32)[:heads, :]

    if split:
        gwbc[:, pl.ds(pl.multiple_of(hx * wide, LANES), wide)] = fsend[...].astype(F32)
        with jax.named_scope("last exchange"):
            final.wait()
        gwbc[:, pl.ds(pl.multiple_of((1 - hx) * wide, LANES), wide)] = frecv[...].astype(F32)
    else:
        gwbc[...] = total
    with jax.named_scope("core f"):
        core_f.wait()
    gwdt[:, theirs] = wfrecv[...].astype(F32)[:heads, :]

    @pl.when(z < zn - 1)
    def _():
        pltpu.make_async_remote_copy(
            sf, rf, f_ss, f_rs.at[0], device_id={"tm": lax.rem(z + 1, zn)}, device_id_type=MESH
        ).wait_send()

    @pl.when(z > 0)
    def _():
        pltpu.make_async_remote_copy(
            sb, rb, b_ss, b_rs.at[0], device_id={"tm": lax.rem(z + zn - 1, zn)}, device_id_type=MESH
        ).wait_send()


def on_device(sizes, u_input, head_values, grad_output, w_bc, w_dt, dt_bias, a_log):
    zn, hn, bn = sizes
    seqs, tokens, width = u_input.shape
    assert seqs == 1 and bn == 2
    heads = w_dt.shape[1]
    values = head_values.shape[2]
    both = w_bc.shape[1]
    pairs = heads // 2
    assert values == heads * 64 and both == 2 * LANES and heads % 4 == 0 and heads <= 32 and tokens == 2 * LANES
    split = hn == 2
    wide = both // 2 if split else both
    block = width // (zn * bn)
    rpad = -(-heads // 16) * 16
    half = width // bn
    sh = tokens // 2
    unit_rows, unit = 16, half * rpad // (16 * zn)
    if (half * rpad) % (16 * zn) or unit == 0 or unit % LANES or half % unit:
        unit_rows, unit = rpad, half
    units = (rpad // unit_rows) * (half // unit)
    vm = pltpu.VMEM
    dma = pltpu.SemaphoreType.DMA
    scratch = [
        vm((tokens, width), BF16), vm((tokens, values), BF16), vm((tokens, values), BF16), vm((width, both), BF16),
        vm((heads, width), BF16), vm((1, heads), F32), vm((1, heads), F32), dma((7,)),
        vm((LANES, width), BF16), vm((bn, zn, block, tokens), BF16), vm((zn, block, tokens), BF16), vm((8, LANES), F32), vm((tokens, both), BF16),
        vm((heads, 1, tokens), F32), vm((tokens, values), F32), vm((tokens, values), F32),
        vm((tokens, LANES), BF16), vm((tokens, LANES), BF16),
        vm((8, values), F32), vm((LANES, values), BF16), vm((tokens, values), BF16), vm((tokens, values), BF16),
        vm((2, pairs, LANES, LANES), F32), vm((2, pairs, LANES, LANES), F32), vm((tokens, values), F32),
        vm((2, sh, sh), F32), vm((2, sh, sh), F32), vm((heads, 1, tokens), F32), vm((LANES, tokens), F32),
        vm((tokens, LANES), F32), vm((tokens, LANES), F32), vm((tokens, LANES), F32), vm((8, values), F32),
        vm((tokens, LANES), F32), vm((tokens, LANES), F32),
        vm((pairs, LANES, LANES), BF16), vm((pairs, LANES, LANES), BF16),
        vm((pairs, LANES, LANES), BF16), vm((pairs, LANES, LANES), BF16),
        vm((pairs, LANES, LANES), BF16), vm((pairs, LANES, LANES), BF16),
        vm((hn, rpad, width), BF16), vm((hn, 2, tokens, LANES), BF16), vm((hn, rpad, tokens), BF16),
        vm((tokens, wide), BF16), vm((tokens, wide), BF16), vm((zn, block, wide), F32),
        vm((zn, block, wide), BF16), vm((zn, block, wide), BF16), vm((block, wide), BF16), vm((block, wide), BF16),
        vm((rpad, width), BF16), vm((rpad, width), BF16), vm((rpad, width), F32),
        vm((units, unit_rows, unit), BF16), vm((zn, unit_rows, unit), BF16), vm((units, unit_rows, unit), BF16),
        vm((rpad, half), BF16), vm((rpad, half), BF16),
        vm((8, LANES), F32), vm((8, LANES), F32), vm((8, LANES), F32), vm((zn, 8, LANES), F32),
        dma, dma((pairs,)), dma, dma((pairs,)),
        dma((4, hn - 1)), dma((4, hn - 1)), dma((6,)), dma((6,)), dma((4, zn - 1)), dma((4, zn - 1)),
    ]
    spec = pl.BlockSpec(memory_space=pltpu.VMEM)
    shapes = (
        ((tokens, width), BF16), ((tokens, values), BF16), ((block, both), F32),
        ((heads, width), F32), ((1, heads), F32), ((1, heads), F32),
    )
    kept = pl.pallas_call(
        functools.partial(kernel, zn, hn, bn, heads, split),
        out_shape=tuple(vm(*s) for s in shapes),
        in_specs=[pl.BlockSpec(memory_space=pl.ANY)] * 7,
        out_specs=[spec] * 6,
        scratch_shapes=scratch,
        compiler_params=pltpu.CompilerParams(
            collective_id=0, has_side_effects=True, vmem_limit_bytes=56 << 20
        ),
    )(
        u_input.reshape(tokens, width), head_values.reshape(tokens, values), grad_output.reshape(tokens, values),
        w_bc, w_dt.T, dt_bias.reshape(1, heads), a_log.reshape(1, heads),
    )
    gin, gval, gwbc, gwdt, gbias, galog = pl.pallas_call(
        write,
        out_shape=tuple(jax.ShapeDtypeStruct(*s) for s in shapes),
        in_specs=[spec] * 6,
        out_specs=[pl.BlockSpec(memory_space=pl.ANY)] * 6,
        scratch_shapes=[dma((6,))],
        compiler_params=pltpu.CompilerParams(vmem_limit_bytes=1 << 20),
    )(*kept)
    return (
        gin.reshape(1, tokens, width), gval.reshape(1, tokens, values), gwbc,
        gwdt.T, gbias.reshape(heads), galog.reshape(heads),
    )


def write(*refs):
    sems = refs[12]
    copies = [pltpu.make_async_copy(refs[i], refs[6 + i], sems.at[i]) for i in range(6)]
    for copy in copies:
        copy.start()
    for copy in copies:
        copy.wait()


def solution(mesh):
    sizes = (mesh.shape["tm"], mesh.shape["head"], mesh.shape["batch"])
    return jax.shard_map(
        functools.partial(on_device, sizes),
        mesh=mesh,
        in_specs=(
            P(("groups", "batch"), "tm", None),
            P(("groups", "batch"), "tm", "head"),
            P(("groups", "batch"), "tm", "head"),
            P(),
            P(None, "head"),
            P("head"),
            P("head"),
        ),
        out_specs=(
            P(("groups", "batch"), "tm", None),
            P(("groups", "batch"), "tm", "head"),
            P(("groups", "tm", "batch"), None),
            P("groups", "head"),
            P(("groups", "head")),
            P(("groups", "head")),
        ),
        check_vma=False,
    )
```

```python
import functools
import math

import jax
import jax.numpy as jnp
from jax import lax
from jax.experimental import pallas as pl
from jax.experimental.pallas import tpu as pltpu
from jax.sharding import PartitionSpec as P

MESH = pl.DeviceIdType.MESH
F32 = jnp.float32
BF16 = jnp.bfloat16
LANES = 128
NT = (((1,), (1,)), ((), ()))
TN = (((0,), (0,)), ((), ()))


def dot(a, b, dims=(((1,), (0,)), ((), ()))):
    return lax.dot_general(a, b, dims, preferred_element_type=F32)


def split3(v):
    hi = v.astype(BF16)
    rest = v - hi.astype(F32)
    mid = rest.astype(BF16)
    return hi, mid, (rest - mid.astype(F32)).astype(BF16)


def dot_ones(a, v):
    hi, mid, lo = split3(v)
    return dot(a, hi) + dot(a, mid) + dot(a, lo)


def dot_sel(v, ones):
    hi = v.astype(BF16)
    lo = (v - hi.astype(F32)).astype(BF16)
    return dot(hi, ones, NT) + dot(lo, ones, NT)


def kernel(
    zn, hn, bn, heads, split,
    u_h, x_h, g_h, wbc_h, wdt_h, bias_h, alog_h,
    gin, gval, gwbc, gwdt, gbias, galog,
    u, x, g, wbc, wdt, bias, alog, in_s,
    wpad, ut, uto, rows, proj, l_t, l_b, e1_b, e1_p, e2_p, ends_b, sel, xs, gs, own_f, own_b, gxi, st, dst, col_e, erows,
    direct, qd, gl, net, gates, tails, gacc_b, gacc_c, smid, gmid,
    sf, rf, sb, rb, wx, px, gpx, psend, precv, plocal, zsend, zrecv, fsend, frecv,
    wsend, wrecv, wsum, wzsend, wzrecv, wgrecv, wfsend, wfrecv, smsend, smrecv, smzsend, smzrecv,
    f_ss, f_rs, b_ss, b_rs, h_ss, h_rs, c_ss, c_rs, z_ss, z_rs,
):
    z, hx, bt = lax.axis_index("tm"), lax.axis_index("head"), lax.axis_index("batch")
    tokens, width = u.shape
    pairs = heads // 2
    groups = pairs // 2
    state = LANES
    sh = tokens // 2
    rpad = wx.shape[1]
    half = width // bn
    units, unit_rows, unit = wzsend.shape
    unit_cols = half // unit

    loads = [
        pltpu.make_async_copy(src, to, in_s.at[i])
        for i, (src, to) in enumerate((
            (wdt_h, wdt), (bias_h, bias), (alog_h, alog), (u_h, u), (wbc_h, wbc), (x_h, x), (g_h, g)
        ))
    ]
    for load in loads[:3]:
        load.start()
    for j, (src, to, n) in enumerate(((u_h, u, 4), (wbc_h, wbc, 4), (x_h, x, 2), (g_h, g, 2))):
        step = src.shape[0] // n
        for i in range(n):
            at = pl.ds(i * step, step)
            pltpu.make_async_copy(src.at[at], to.at[at], in_s.at[3 + j]).start()

    barrier = pltpu.get_barrier_semaphore()
    for k in range(1, zn):
        pl.semaphore_signal(barrier, inc=1, device_id={"tm": lax.rem(z + k, zn)}, device_id_type=MESH)
    for k in range(1, hn):
        pl.semaphore_signal(barrier, inc=1, device_id={"head": lax.rem(hx + k, hn)}, device_id_type=MESH)
    for k in range(1, bn):
        pl.semaphore_signal(barrier, inc=1, device_id={"batch": lax.rem(bt + k, bn)}, device_id_type=MESH)

    lane = lax.broadcasted_iota(jnp.int32, (tokens, LANES), 1)
    low = lax.broadcasted_iota(jnp.int32, (sh, LANES), 1) < 64
    lm = low.astype(F32).astype(BF16)
    hm = 1.0 - lm
    ti = lax.broadcasted_iota(jnp.int32, (tokens, tokens), 0)
    si = lax.broadcasted_iota(jnp.int32, (tokens, tokens), 1)
    lower = (ti >= si).astype(F32).astype(BF16)
    causal = ti[:sh, :sh] <= si[:sh, :sh]

    with jax.named_scope("initial"):
        wpad[...] = jnp.zeros_like(wpad)
        rows[...] = jnp.zeros_like(rows)
        which = lax.broadcasted_iota(jnp.int32, (LANES, LANES), 0)
        head_of = lax.shift_right_logical(lax.broadcasted_iota(jnp.int32, (LANES, LANES), 1), 6)
        used = jnp.where(which < 96, which & 31, -1)
        for p in range(pairs):
            sel[:, p * LANES:(p + 1) * LANES] = (used == head_of + 2 * p).astype(F32).astype(BF16)
        dst[...] = jnp.zeros_like(dst)
        direct[...] = jnp.zeros_like(direct)
        gl[...] = jnp.zeros_like(gl)
        qd[...] = jnp.zeros_like(qd)
        gacc_b[...] = jnp.zeros_like(gacc_b)
        gacc_c[...] = jnp.zeros_like(gacc_c)
        tails[...] = jnp.zeros_like(tails)
        erows[...] = jnp.zeros_like(erows)

        @pl.when(z == 0)
        def _():
            rf[...] = jnp.zeros_like(rf)

        @pl.when(z == zn - 1)
        def _():
            rb[...] = jnp.zeros_like(rb)

    def packed(v):
        hi, mid, lo = split3(v)
        at = lane[:v.shape[0]]
        mid, lo = pltpu.roll(mid.astype(F32), 32, 1), pltpu.roll(lo.astype(F32), 64, 1)
        return jnp.where(at < 32, hi.astype(F32), jnp.where(at < 64, mid, jnp.where(at < 96, lo, 0.0))).astype(BF16)

    with jax.named_scope("wait for u"):
        for load in loads[:5]:
            load.wait()
    wpad[:heads, :] = wdt[...]
    rows[0:1, :heads] = bias[...]
    rows[1:2, :heads] = alog[...]
    wx[hx] = wpad[:rpad, :]
    uu = u[...]
    proj[...] = dot(uu, wbc[...]).astype(BF16)
    b_all, c_all = proj[:, :state], proj[:, state:]
    b_t = b_all.astype(F32).T.astype(BF16)
    c_t = c_all.astype(F32).T.astype(BF16)
    pre = dot(uu, wpad[...], NT) + rows[0:1, :]
    small = jnp.exp(-jnp.abs(pre))
    delta = jnp.maximum(pre, 0.0) + jnp.log1p(small)
    rate = -jnp.exp(rows[1:2, :])
    log_decay = dot_ones(lower, delta * rate)
    mid_l, last_l = log_decay[sh - 1:sh, :], log_decay[tokens - 1:tokens, :]
    first = lax.broadcasted_iota(jnp.int32, (tokens, LANES), 0) < sh
    e1 = packed(jnp.exp(jnp.where(first, mid_l, last_l) - log_decay) * delta)
    e2 = packed(jnp.exp(jnp.where(first, log_decay, log_decay - mid_l)))
    e1_p[...] = e1
    e2_p[...] = e2
    ends = jnp.concatenate([jnp.exp(mid_l), jnp.exp(last_l - mid_l), jnp.zeros((6, LANES), F32)], axis=0)
    ends_b[...] = dot(packed(ends), sel[...])
    with jax.named_scope("wait for values"):
        loads[5].wait()
        loads[6].wait()
    with jax.named_scope("wait for devices"):
        pl.semaphore_wait(barrier, zn + hn + bn - 3)

    def head_copy(i, ref, k):
        return pltpu.make_async_remote_copy(
            ref, ref, h_ss.at[i, k - 1], h_rs.at[i, k - 1],
            device_id={"head": lax.rem(hx + k, hn)}, device_id_type=MESH,
        )

    def weights_copy(k):
        return head_copy(0, wx.at[hx], k)

    def steps_copy(k):
        return head_copy(1, gpx.at[hx], k)

    def maps_copy(part, k):
        return head_copy(2 + part, px.at[hx, part], k)

    def chain_f(p):
        return pltpu.make_async_remote_copy(
            sf.at[p], rf.at[p], f_ss, f_rs.at[p],
            device_id={"tm": lax.rem(z + 1, zn)}, device_id_type=MESH,
        )

    def chain_b(p):
        return pltpu.make_async_remote_copy(
            sb.at[p], rb.at[p], b_ss, b_rs.at[p],
            device_id={"tm": lax.rem(z + zn - 1, zn)}, device_id_type=MESH,
        )

    def columns(p, n=1):
        return pl.ds(pl.multiple_of(p * n * LANES, LANES), n * LANES)

    def forward(p):
        cols = columns(p)
        middle = ends_b[0:1, cols] * rf[p].astype(F32) + own_f[0, p]
        smid[p] = middle.astype(BF16)
        sf[p] = (ends_b[1:2, cols] * middle + own_f[1, p]).astype(BF16)

        @pl.when(z < zn - 1)
        def _():
            chain_f(p).start()

    def backward(p):
        cols = columns(p)
        middle = ends_b[1:2, cols] * rb[p].astype(F32) + own_b[1, p]
        gmid[p] = middle.astype(BF16)
        sb[p] = (ends_b[0:1, cols] * middle + own_b[0, p]).astype(BF16)

        @pl.when(z > 0)
        def _():
            chain_b(p).start()

    def summarize(q, carry):
        cols = columns(q, 2)
        spread = dot(e1_p[...], sel[:, cols])
        e1_b[:, cols] = spread
        xv = (spread * x[:, cols].astype(F32)).astype(BF16)
        gv = (dot(e2_p[...], sel[:, cols]) * g[:, cols].astype(F32)).astype(BF16)
        xs[:, cols] = xv
        gs[:, cols] = gv
        for k in range(2):
            part = slice(k * sh, (k + 1) * sh)
            of, ob = dot(b_t[:, part], xv[part]), dot(c_t[:, part], gv[part])
            for j in range(2):
                own_f[k, 2 * q + j] = of[:, j * LANES:(j + 1) * LANES]
                own_b[k, 2 * q + j] = ob[:, j * LANES:(j + 1) * LANES]

        @pl.when(z == 0)
        def _():
            forward(2 * q)
            forward(2 * q + 1)

        @pl.when(z == zn - 1)
        def _():
            @pl.when(q > 0)
            def _():
                backward(2 * q)

            backward(2 * q + 1)

        return carry

    @pl.when(z == zn - 1)
    def _():
        with jax.named_scope("first pair"):
            gv = (dot(e2_p[...], sel[:, :LANES]) * g[:, :LANES].astype(F32)).astype(BF16)
            for k in range(2):
                part = slice(k * sh, (k + 1) * sh)
                own_b[k, 0] = dot(c_t[:, part], gv[part])
            backward(0)

    with jax.named_scope("summaries"):
        lax.fori_loop(0, groups, summarize, 0)

    for k in range(1, hn):
        weights_copy(k).start()

    with jax.named_scope("scores"):
        l_rows = log_decay.T
        for h in range(heads):
            l_t[h] = l_rows[h:h + 1, :]
        l_b[...] = dot(packed(log_decay - jnp.log(jnp.maximum(delta, 1e-37))), sel[...])
        gate = jax.nn.sigmoid(pre)
        gates[0] = gate
        gates[1] = jnp.where(delta > 1e-30, gate / jnp.maximum(delta, 1e-30), 1.0)
        for k in range(2):
            part = slice(k * sh, (k + 1) * sh)
            st[k] = jnp.where(causal, dot(b_all[part], c_all[part], NT), 0.0)
    other = {"batch": lax.rem(bt + 1, bn)}

    def core_copy(i, src, to):
        return pltpu.make_async_remote_copy(src, to, c_ss.at[i], c_rs.at[i], device_id=other, device_id_type=MESH)

    block = uto.shape[1]
    chunk = math.lcm(block, LANES)
    for c in range(width // chunk):
        turned = u[:, c * chunk:(c + 1) * chunk].astype(F32).T
        for i in range(chunk // block):
            k, b = divmod(c * (chunk // block) + i, bn)
            ut[b, k] = turned[i * block:(i + 1) * block].astype(BF16)
    core_u = core_copy(5, ut.at[lax.rem(bt + 1, bn)], uto)
    core_u.start()

    def local_pair(p):
        cols = columns(p)
        for k in range(2):
            part = slice(k * sh, (k + 1) * sh)
            gt = g[part, cols]
            xb = x[part, cols]
            sm = st[k]
            dm = dot(jnp.concatenate([xb * lm, xb * hm], axis=0), gt, NT)
            add = None
            mixed = []
            dr = direct[part]
            for j in range(2):
                lr = l_t[2 * p + j][:, part]
                lcol = l_b[part, cols][:, 64 * j:64 * j + 1]
                decay = jnp.exp(jnp.minimum(lr - lcol, 30.0))
                mixed.append((decay * sm).astype(BF16))
                a = dm[j * sh:(j + 1) * sh] * decay
                add = a if add is None else add + a
                w = a * sm
                col_e[2 * p + j, :, part] = jnp.sum(w, axis=0, keepdims=True)
                dr = dr + jnp.where(lane[:sh] == 2 * p + j, jnp.sum(w, axis=1, keepdims=True), 0.0)
            direct[part] = dr
            dst[k] += add
            gx = dot(jnp.concatenate(mixed, axis=0), gt)
            gxi[part, cols] = jnp.where(low, gx[:sh], gx[sh:])

    def two(ref, q):
        return jnp.concatenate([ref[2 * q], ref[2 * q + 1]], axis=1)

    halves = [slice(k * sh, (k + 1) * sh) for k in range(2)]

    def maps_before(q):
        for part, ref in zip(halves, (rf, smid)):
            gacc_c[part] += dot(gs[part, columns(q, 2)], two(ref, q), NT)

    def maps_after(q):
        for part, ref in zip(halves, (gmid, rb)):
            gacc_b[part] += dot(xs[part, columns(q, 2)], two(ref, q), NT)

    def values_before(q):
        cols = columns(q, 2)
        cs = [dot(c_all[part], two(ref, q)) for part, ref in zip(halves, (rf, smid))]
        gl[...] += dot_sel(gs[:, cols].astype(F32) * jnp.concatenate(cs, axis=0), sel[:, cols])

    def values_after(q):
        cols = columns(q, 2)
        bs = [dot(b_all[part], two(ref, q)) for part, ref in zip(halves, (gmid, rb))]
        br = e1_b[:, cols] * jnp.concatenate(bs, axis=0)
        gval[:, cols] = (gxi[:, cols] + br).astype(BF16)
        qd[...] += dot_sel(x[:, cols].astype(F32) * br, sel[:, cols])

    def through(q):
        cols = columns(q, 2)
        both = [
            jnp.sum(two(before, q).astype(F32) * two(after, q).astype(F32), axis=0, keepdims=True)
            for before, after in ((rf, gmid), (smid, rb))
        ]
        row = lax.broadcasted_iota(jnp.int32, (8, 2 * LANES), 0)
        both = ends_b[:, cols] * jnp.where(row == 0, both[0], both[1])
        tails[...] += sum(dot(part, sel[:, cols], NT) for part in split3(both))

    late_f = jnp.maximum(4 * z - 2, 0)
    late_b = jnp.maximum(6 * (zn - 1 - z) - 4, 0)

    def turn(i, carry):
        pf = i - late_f
        pb = i - late_b
        in_f, in_b = (pf >= 0) & (pf < pairs), (pb >= 0) & (pb < pairs)

        @pl.when(in_f & (z > 0))
        def _():
            with jax.named_scope("forward"):
                chain_f(pf).wait_recv()
                forward(pf)

        @pl.when(in_b & (z < zn - 1))
        def _():
            with jax.named_scope("backward"):
                chain_b(pb).wait_recv()
                backward(pb)

        @pl.when(i < pairs)
        def _():
            with jax.named_scope("local"):
                local_pair(i)

        kf = i - jnp.where(z == 0, 1, jnp.maximum(late_f + 1, pairs))
        kb = i - jnp.where(z == zn - 1, 1, jnp.maximum(late_b + 1, pairs))

        @pl.when(kf == 0)
        def _():
            maps_before(0)

        @pl.when((kf > 0) & (kf < pairs) & (kf % 2 == 0))
        def _():
            with jax.named_scope("before"):
                maps_before(kf // 2)
                values_before(kf // 2 - 1)

        @pl.when(kb == 0)
        def _():
            maps_after(0)

        @pl.when((kb > 0) & (kb < pairs) & (kb % 2 == 0))
        def _():
            with jax.named_scope("after"):
                maps_after(kb // 2)
                values_after(kb // 2 - 1)

        kt = i - jnp.maximum(late_f, late_b) - 2

        @pl.when((kt >= 0) & (kt < pairs - 2) & (kt % 2 == 0))
        def _():
            with jax.named_scope("through"):
                through(kt // 2)

        @pl.when(i == pairs)
        def _():
            with jax.named_scope("local sums"):
                for h in range(heads):
                    erows[h:h + 1, :] = col_e[h]
                net[...] = erows[...].T - direct[...]

        return carry

    lax.fori_loop(0, pairs + max(6 * (zn - 1) - 3, pairs), turn, 0)

    with jax.named_scope("state map gradients"):
        d_masked = [jnp.where(causal, dst[k], 0.0).astype(BF16) for k in range(2)]
        for k in range(2):
            part = slice(k * sh, (k + 1) * sh)
            px[hx, 0, part] = (gacc_b[part] + dot(d_masked[k], c_all[part])).astype(BF16)
            px[hx, 1, part] = (gacc_c[part] + dot(d_masked[k], b_all[part], TN)).astype(BF16)
        first_part = 1 - hx if split else 0
        for k in range(1, hn):
            maps_copy(first_part, k).start()

    with jax.named_scope("last values"):
        values_before(groups - 1)
        values_after(groups - 1)
        through(groups - 1)

    with jax.named_scope("step gradients"):
        upper = ((ti <= si) & ((ti < sh) == (si < sh))).astype(F32).astype(BF16)
        carried = qd[...]
        weighted = direct[...] + carried
        g_log = net[...] + gl[...] - carried
        ends_sum = tails[...]
        tail = [
            jnp.sum(carried[k * sh:(k + 1) * sh], axis=0, keepdims=True) + ends_sum[k:k + 1] for k in range(2)
        ]
        back = dot_ones(upper, g_log) + jnp.where(first, tail[0], tail[1])
        gate, per_delta = gates[0], gates[1]
        g_pre = weighted * per_delta + rate * back * gate
        smsend[...] = jnp.zeros_like(smsend)
        smsend[0:1, :] = jnp.sum(g_pre, axis=0, keepdims=True)
        smsend[1:2, :] = jnp.sum(delta * back, axis=0, keepdims=True) * rate
    gpx[hx] = g_pre.T[:rpad, :].astype(BF16)
    for k in range(1, hn):
        maps_copy(1 - first_part, k).start()
        steps_copy(k).start()
    with jax.named_scope("step weight product"):
        wsend[...] = dot(gpx[hx], uu).astype(BF16)

    core_w = core_copy(0, wsend, wrecv)
    core_s = core_copy(1, smsend, smrecv)
    core_p = core_copy(2, psend, precv)
    core_f = core_copy(3, wfsend, wfrecv)
    core_w.start()
    core_s.start()

    def along(i, src, to, k):
        there = lax.rem(z + k, zn)
        return pltpu.make_async_remote_copy(
            src, to.at[z], z_ss.at[i, k - 1], z_rs.at[i, k - 1], device_id={"tm": there}, device_id_type=MESH
        )

    def each_z(body):
        def turn(k, carry):
            body(k)
            return carry

        lax.fori_loop(1, zn, turn, 0)

    def z_start_small(k):
        along(0, wzsend.at[lax.rem(z + k, zn) if units > 1 else 0], wzrecv, k).start()
        along(1, smzsend, smzrecv, k).start()

    def z_start_large(k):
        along(2, zsend.at[lax.rem(z + k, zn)], zrecv, k).start()

    def z_wait_small(k):
        along(0, wzsend.at[lax.rem(z + k, zn) if units > 1 else 0], wzrecv, k).wait()
        along(1, smzsend, smzrecv, k).wait()

    def z_start_sums(k):
        along(3, wgrecv.at[z], wgrecv, k).start()

    def z_wait_sums(k):
        along(3, wgrecv.at[z], wgrecv, k).wait()

    def z_wait_large(k):
        along(2, zsend.at[lax.rem(z + k, zn)], zrecv, k).wait()

    with jax.named_scope("core w"):
        core_w.wait()
    core_s.wait()
    wsum[...] = wsend[...].astype(F32) + wrecv[...].astype(F32)
    mine = pl.ds(pl.multiple_of(bt * half, LANES), half)
    theirs = pl.ds(pl.multiple_of(lax.rem(bt + 1, bn) * half, LANES), half)
    for k in range(units):
        r, c = divmod(k, unit_cols)
        cols = pl.ds(pl.multiple_of(bt * half + c * unit, LANES), unit)
        wzsend[k] = wsum[r * unit_rows:(r + 1) * unit_rows, cols].astype(BF16)
    own_unit = z if units > 1 else 0
    wzrecv[z] = wzsend[own_unit]
    sz = smsend[...] + smrecv[...]
    smzsend[...] = sz
    smzrecv[z] = sz
    each_z(z_start_small)

    def both_heads(part):
        total = px[0, part].astype(F32)
        for k in range(1, hn):
            total = total + px[k, part].astype(F32)
        return total.astype(BF16)

    wide = zrecv.shape[2]
    with jax.named_scope("wait for heads"):
        for k in range(1, hn):
            maps_copy(first_part, k).wait_send()
            maps_copy(1 - first_part, k).wait_recv()
            if not split:
                maps_copy(first_part, k).wait_recv()
    if split:
        piece = both_heads(hx)
    else:
        piece = jnp.concatenate([both_heads(0), both_heads(1)], axis=1)
    psend[...] = piece
    core_p.start()

    def product(ref, values):
        if block % 16 == 0:
            return dot(ref[...].reshape(zn * block, tokens), values).reshape(zn, block, wide)
        return jnp.stack([dot(ref[k], values) for k in range(zn)])

    with jax.named_scope("weight product"):
        plocal[...] = product(ut.at[bt], piece)
    core_u.wait()
    with jax.named_scope("core p"):
        core_p.wait()
    with jax.named_scope("weight product"):
        zsend[...] = (plocal[...] + product(uto, precv[...])).astype(BF16)
    zrecv[z] = zsend[z]
    each_z(z_start_large)

    with jax.named_scope("small along z"):
        each_z(z_wait_small)
    total_w = wzrecv[0].astype(F32)
    total_s = smzrecv[0]
    for k in range(1, zn):
        total_w = total_w + wzrecv[k].astype(F32)
        total_s = total_s + smzrecv[k]
    wgrecv[own_unit] = total_w.astype(BF16)
    if units > 1:
        each_z(z_start_sums)
    gbias[...] = total_s[0:1, :heads]
    galog[...] = total_s[1:2, :heads]

    for k in range(1, hn):
        weights_copy(k).wait()
        steps_copy(k).wait()
        maps_copy(1 - first_part, k).wait_send()
        if split:
            maps_copy(first_part, k).wait_recv()
    gp = jnp.concatenate([both_heads(0), both_heads(1)], axis=1)
    gpa = gpx[...].reshape(hn * rpad, tokens).astype(F32).T.astype(BF16)
    wa = wx[...].reshape(hn * rpad, width)
    with jax.named_scope("input gradient"):
        gin[...] = (dot(gp, wbc[...], NT) + dot(gpa, wa)).astype(BF16)

    with jax.named_scope("large along z"):
        each_z(z_wait_large)
    total = zrecv[0].astype(F32)
    for k in range(1, zn):
        total = total + zrecv[k].astype(F32)
    if split:
        fsend[...] = total.astype(BF16)
        final = pltpu.make_async_remote_copy(
            fsend, frecv, c_ss.at[4], c_rs.at[4], device_id={"head": lax.rem(hx + 1, hn)}, device_id_type=MESH
        )
        final.start()

    with jax.named_scope("sums along z"):
        if units > 1:
            each_z(z_wait_sums)
    for k in range(units):
        r, c = divmod(k, unit_cols)
        wfsend[r * unit_rows:(r + 1) * unit_rows, c * unit:(c + 1) * unit] = wgrecv[k]
    core_f.start()
    gwdt[:, mine] = wfsend[...].astype(F32)[:heads, :]

    if split:
        gwbc[:, pl.ds(pl.multiple_of(hx * wide, LANES), wide)] = fsend[...].astype(F32)
        with jax.named_scope("last exchange"):
            final.wait()
        gwbc[:, pl.ds(pl.multiple_of((1 - hx) * wide, LANES), wide)] = frecv[...].astype(F32)
    else:
        gwbc[...] = total
    with jax.named_scope("core f"):
        core_f.wait()
    gwdt[:, theirs] = wfrecv[...].astype(F32)[:heads, :]

    @pl.when(z < zn - 1)
    def _():
        pltpu.make_async_remote_copy(
            sf, rf, f_ss, f_rs.at[0], device_id={"tm": lax.rem(z + 1, zn)}, device_id_type=MESH
        ).wait_send()

    @pl.when(z > 0)
    def _():
        pltpu.make_async_remote_copy(
            sb, rb, b_ss, b_rs.at[0], device_id={"tm": lax.rem(z + zn - 1, zn)}, device_id_type=MESH
        ).wait_send()


def on_device(sizes, u_input, head_values, grad_output, w_bc, w_dt, dt_bias, a_log):
    zn, hn, bn = sizes
    seqs, tokens, width = u_input.shape
    assert seqs == 1 and bn == 2
    heads = w_dt.shape[1]
    values = head_values.shape[2]
    both = w_bc.shape[1]
    pairs = heads // 2
    assert values == heads * 64 and both == 2 * LANES and heads % 4 == 0 and heads <= 32 and tokens == 2 * LANES
    split = hn == 2
    wide = both // 2 if split else both
    block = width // (zn * bn)
    rpad = -(-heads // 16) * 16
    half = width // bn
    sh = tokens // 2
    unit_rows, unit = 16, half * rpad // (16 * zn)
    if (half * rpad) % (16 * zn) or unit == 0 or unit % LANES or half % unit:
        unit_rows, unit = rpad, half
    units = (rpad // unit_rows) * (half // unit)
    vm = pltpu.VMEM
    dma = pltpu.SemaphoreType.DMA
    scratch = [
        vm((tokens, width), BF16), vm((tokens, values), BF16), vm((tokens, values), BF16), vm((width, both), BF16),
        vm((heads, width), BF16), vm((1, heads), F32), vm((1, heads), F32), dma((7,)),
        vm((LANES, width), BF16), vm((bn, zn, block, tokens), BF16), vm((zn, block, tokens), BF16), vm((8, LANES), F32), vm((tokens, both), BF16),
        vm((heads, 1, tokens), F32), vm((tokens, values), F32), vm((tokens, values), F32),
        vm((tokens, LANES), BF16), vm((tokens, LANES), BF16),
        vm((8, values), F32), vm((LANES, values), BF16), vm((tokens, values), BF16), vm((tokens, values), BF16),
        vm((2, pairs, LANES, LANES), F32), vm((2, pairs, LANES, LANES), F32), vm((tokens, values), F32),
        vm((2, sh, sh), F32), vm((2, sh, sh), F32), vm((heads, 1, tokens), F32), vm((LANES, tokens), F32),
        vm((tokens, LANES), F32), vm((tokens, LANES), F32), vm((tokens, LANES), F32), vm((tokens, LANES), F32),
        vm((2, tokens, LANES), F32), vm((8, LANES), F32),
        vm((tokens, LANES), F32), vm((tokens, LANES), F32),
        vm((pairs, LANES, LANES), BF16), vm((pairs, LANES, LANES), BF16),
        vm((pairs, LANES, LANES), BF16), vm((pairs, LANES, LANES), BF16),
        vm((pairs, LANES, LANES), BF16), vm((pairs, LANES, LANES), BF16),
        vm((hn, rpad, width), BF16), vm((hn, 2, tokens, LANES), BF16), vm((hn, rpad, tokens), BF16),
        vm((tokens, wide), BF16), vm((tokens, wide), BF16), vm((zn, block, wide), F32),
        vm((zn, block, wide), BF16), vm((zn, block, wide), BF16), vm((block, wide), BF16), vm((block, wide), BF16),
        vm((rpad, width), BF16), vm((rpad, width), BF16), vm((rpad, width), F32),
        vm((units, unit_rows, unit), BF16), vm((zn, unit_rows, unit), BF16), vm((units, unit_rows, unit), BF16),
        vm((rpad, half), BF16), vm((rpad, half), BF16),
        vm((8, LANES), F32), vm((8, LANES), F32), vm((8, LANES), F32), vm((zn, 8, LANES), F32),
        dma, dma((pairs,)), dma, dma((pairs,)),
        dma((4, hn - 1)), dma((4, hn - 1)), dma((6,)), dma((6,)), dma((4, zn - 1)), dma((4, zn - 1)),
    ]
    spec = pl.BlockSpec(memory_space=pltpu.VMEM)
    shapes = (
        ((tokens, width), BF16), ((tokens, values), BF16), ((block, both), F32),
        ((heads, width), F32), ((1, heads), F32), ((1, heads), F32),
    )
    kept = pl.pallas_call(
        functools.partial(kernel, zn, hn, bn, heads, split),
        out_shape=tuple(vm(*s) for s in shapes),
        in_specs=[pl.BlockSpec(memory_space=pl.ANY)] * 7,
        out_specs=[spec] * 6,
        scratch_shapes=scratch,
        compiler_params=pltpu.CompilerParams(
            collective_id=0, has_side_effects=True, vmem_limit_bytes=56 << 20
        ),
    )(
        u_input.reshape(tokens, width), head_values.reshape(tokens, values), grad_output.reshape(tokens, values),
        w_bc, w_dt.T, dt_bias.reshape(1, heads), a_log.reshape(1, heads),
    )
    gin, gval, gwbc, gwdt, gbias, galog = pl.pallas_call(
        write,
        out_shape=tuple(jax.ShapeDtypeStruct(*s) for s in shapes),
        in_specs=[spec] * 6,
        out_specs=[pl.BlockSpec(memory_space=pl.ANY)] * 6,
        scratch_shapes=[dma((6,))],
        compiler_params=pltpu.CompilerParams(vmem_limit_bytes=1 << 20),
    )(*kept)
    return (
        gin.reshape(1, tokens, width), gval.reshape(1, tokens, values), gwbc,
        gwdt.T, gbias.reshape(heads), galog.reshape(heads),
    )


def write(*refs):
    sems = refs[12]
    copies = [pltpu.make_async_copy(refs[i], refs[6 + i], sems.at[i]) for i in range(6)]
    for copy in copies:
        copy.start()
    for copy in copies:
        copy.wait()


def solution(mesh):
    sizes = (mesh.shape["tm"], mesh.shape["head"], mesh.shape["batch"])
    return jax.shard_map(
        functools.partial(on_device, sizes),
        mesh=mesh,
        in_specs=(
            P(("groups", "batch"), "tm", None),
            P(("groups", "batch"), "tm", "head"),
            P(("groups", "batch"), "tm", "head"),
            P(),
            P(None, "head"),
            P("head"),
            P("head"),
        ),
        out_specs=(
            P(("groups", "batch"), "tm", None),
            P(("groups", "batch"), "tm", "head"),
            P(("groups", "tm", "batch"), None),
            P("groups", "head"),
            P(("groups", "head")),
            P(("groups", "head")),
        ),
        check_vma=False,
    )
```

```python
import functools
import math

import jax
import jax.numpy as jnp
from jax import lax
from jax.experimental import pallas as pl
from jax.experimental.pallas import tpu as pltpu
from jax.sharding import PartitionSpec as P

MESH = pl.DeviceIdType.MESH
F32 = jnp.float32
BF16 = jnp.bfloat16
LANES = 128
NT = (((1,), (1,)), ((), ()))
TN = (((0,), (0,)), ((), ()))


def dot(a, b, dims=(((1,), (0,)), ((), ()))):
    return lax.dot_general(a, b, dims, preferred_element_type=F32)


def split3(v):
    hi = v.astype(BF16)
    rest = v - hi.astype(F32)
    mid = rest.astype(BF16)
    return hi, mid, (rest - mid.astype(F32)).astype(BF16)


def dot_ones(a, v):
    hi, mid, lo = split3(v)
    return dot(a, hi) + dot(a, mid) + dot(a, lo)


def dot_sel(v, ones):
    hi = v.astype(BF16)
    lo = (v - hi.astype(F32)).astype(BF16)
    return dot(hi, ones, NT) + dot(lo, ones, NT)


def kernel(
    zn, hn, bn, heads, split,
    u_h, x_h, g_h, wbc_h, wdt_h, bias_h, alog_h,
    gin, gval, gwbc, gwdt, gbias, galog,
    u, x, g, wbc, wdt, bias, alog, in_s,
    wpad, ut, uto, rows, proj, l_t, l_b, e1_b, e1_p, e2_p, ends_b, sel, xs, gs, own_f, own_b, gxi, st, dst, col_e, erows,
    direct, qd, gl, net, gates, tails, gacc, mixers, mates, smid, gmid,
    sf, rf, sb, rb, wx, px, gpx, psend, precv, plocal, zsend, zrecv, fsend, frecv,
    wsend, wrecv, wsum, wzsend, wzrecv, wgrecv, wfsend, wfrecv, smsend, smrecv, smzsend, smzrecv,
    f_ss, f_rs, b_ss, b_rs, h_ss, h_rs, c_ss, c_rs, z_ss, z_rs,
):
    z, hx, bt = lax.axis_index("tm"), lax.axis_index("head"), lax.axis_index("batch")
    tokens, width = u.shape
    pairs = heads // 2
    groups = pairs // 2
    state = LANES
    sh = tokens // 2
    rpad = wx.shape[1]
    half = width // bn
    units, unit_rows, unit = wzsend.shape
    unit_cols = half // unit

    loads = [
        pltpu.make_async_copy(src, to, in_s.at[i])
        for i, (src, to) in enumerate((
            (wdt_h, wdt), (bias_h, bias), (alog_h, alog), (u_h, u), (wbc_h, wbc), (x_h, x), (g_h, g)
        ))
    ]
    for load in loads[:3]:
        load.start()
    for j, (src, to, n) in enumerate(((u_h, u, 4), (wbc_h, wbc, 4), (x_h, x, 2), (g_h, g, 2))):
        step = src.shape[0] // n
        for i in range(n):
            at = pl.ds(i * step, step)
            pltpu.make_async_copy(src.at[at], to.at[at], in_s.at[3 + j]).start()

    barrier = pltpu.get_barrier_semaphore()
    for k in range(1, zn):
        pl.semaphore_signal(barrier, inc=1, device_id={"tm": lax.rem(z + k, zn)}, device_id_type=MESH)
    for k in range(1, hn):
        pl.semaphore_signal(barrier, inc=1, device_id={"head": lax.rem(hx + k, hn)}, device_id_type=MESH)
    for k in range(1, bn):
        pl.semaphore_signal(barrier, inc=1, device_id={"batch": lax.rem(bt + k, bn)}, device_id_type=MESH)

    lane = lax.broadcasted_iota(jnp.int32, (tokens, LANES), 1)
    low = lax.broadcasted_iota(jnp.int32, (sh, LANES), 1) < 64
    lm = low.astype(F32).astype(BF16)
    hm = 1.0 - lm
    ti = lax.broadcasted_iota(jnp.int32, (tokens, tokens), 0)
    si = lax.broadcasted_iota(jnp.int32, (tokens, tokens), 1)
    lower = (ti >= si).astype(F32).astype(BF16)
    causal = ti[:sh, :sh] <= si[:sh, :sh]

    with jax.named_scope("initial"):
        wpad[...] = jnp.zeros_like(wpad)
        rows[...] = jnp.zeros_like(rows)
        which = lax.broadcasted_iota(jnp.int32, (LANES, LANES), 0)
        head_of = lax.shift_right_logical(lax.broadcasted_iota(jnp.int32, (LANES, LANES), 1), 6)
        used = jnp.where(which < 96, which & 31, -1)
        for p in range(pairs):
            sel[:, p * LANES:(p + 1) * LANES] = (used == head_of + 2 * p).astype(F32).astype(BF16)
        dst[...] = jnp.zeros_like(dst)
        direct[...] = jnp.zeros_like(direct)
        gl[...] = jnp.zeros_like(gl)
        qd[...] = jnp.zeros_like(qd)
        gacc[...] = jnp.zeros_like(gacc)
        tails[...] = jnp.zeros_like(tails)
        erows[...] = jnp.zeros_like(erows)

        @pl.when(z == 0)
        def _():
            rf[...] = jnp.zeros_like(rf)

        @pl.when(z == zn - 1)
        def _():
            rb[...] = jnp.zeros_like(rb)

    def packed(v):
        hi, mid, lo = split3(v)
        at = lane[:v.shape[0]]
        mid, lo = pltpu.roll(mid.astype(F32), 32, 1), pltpu.roll(lo.astype(F32), 64, 1)
        return jnp.where(at < 32, hi.astype(F32), jnp.where(at < 64, mid, jnp.where(at < 96, lo, 0.0))).astype(BF16)

    with jax.named_scope("wait for u"):
        for load in loads[:5]:
            load.wait()
    wpad[:heads, :] = wdt[...]
    rows[0:1, :heads] = bias[...]
    rows[1:2, :heads] = alog[...]
    wx[hx] = wpad[:rpad, :]
    uu = u[...]
    proj[...] = dot(uu, wbc[...]).astype(BF16)
    b_all, c_all = proj[:, :state], proj[:, state:]
    b_t = b_all.astype(F32).T.astype(BF16)
    c_t = c_all.astype(F32).T.astype(BF16)
    pre = dot(uu, wpad[...], NT) + rows[0:1, :]
    small = jnp.exp(-jnp.abs(pre))
    delta = jnp.maximum(pre, 0.0) + jnp.log1p(small)
    rate = -jnp.exp(rows[1:2, :])
    log_decay = dot_ones(lower, delta * rate)
    mid_l, last_l = log_decay[sh - 1:sh, :], log_decay[tokens - 1:tokens, :]
    first = lax.broadcasted_iota(jnp.int32, (tokens, LANES), 0) < sh
    e1 = packed(jnp.exp(jnp.where(first, mid_l, last_l) - log_decay) * delta)
    e2 = packed(jnp.exp(jnp.where(first, log_decay, log_decay - mid_l)))
    e1_p[...] = e1
    e2_p[...] = e2
    ends = jnp.concatenate([jnp.exp(mid_l), jnp.exp(last_l - mid_l), jnp.zeros((6, LANES), F32)], axis=0)
    ends_b[...] = dot(packed(ends), sel[...])
    with jax.named_scope("wait for values"):
        loads[5].wait()
        loads[6].wait()
    with jax.named_scope("wait for devices"):
        pl.semaphore_wait(barrier, zn + hn + bn - 3)

    def head_copy(i, ref, k):
        return pltpu.make_async_remote_copy(
            ref, ref, h_ss.at[i, k - 1], h_rs.at[i, k - 1],
            device_id={"head": lax.rem(hx + k, hn)}, device_id_type=MESH,
        )

    def weights_copy(k):
        return head_copy(0, wx.at[hx], k)

    def steps_copy(k):
        return head_copy(1, gpx.at[hx], k)

    early = jnp.where(2 * z < zn, 1, 0)

    def maps_copy(role, k):
        return head_copy(2 + role, px.at[hx, early if role == 0 else 1 - early], k)

    def chain_f(p):
        return pltpu.make_async_remote_copy(
            sf.at[p], rf.at[p], f_ss, f_rs.at[p],
            device_id={"tm": lax.rem(z + 1, zn)}, device_id_type=MESH,
        )

    def chain_b(p):
        return pltpu.make_async_remote_copy(
            sb.at[p], rb.at[p], b_ss, b_rs.at[p],
            device_id={"tm": lax.rem(z + zn - 1, zn)}, device_id_type=MESH,
        )

    def columns(p, n=1):
        return pl.ds(pl.multiple_of(p * n * LANES, LANES), n * LANES)

    def forward(p):
        cols = columns(p)
        middle = ends_b[0:1, cols] * rf[p].astype(F32) + own_f[0, p]
        smid[p] = middle.astype(BF16)
        sf[p] = (ends_b[1:2, cols] * middle + own_f[1, p]).astype(BF16)

        @pl.when(z < zn - 1)
        def _():
            chain_f(p).start()

    def backward(p):
        cols = columns(p)
        middle = ends_b[1:2, cols] * rb[p].astype(F32) + own_b[1, p]
        gmid[p] = middle.astype(BF16)
        sb[p] = (ends_b[0:1, cols] * middle + own_b[0, p]).astype(BF16)

        @pl.when(z > 0)
        def _():
            chain_b(p).start()

    def summarize(q, carry):
        cols = columns(q, 2)
        spread = dot(e1_p[...], sel[:, cols])
        e1_b[:, cols] = spread
        xv = (spread * x[:, cols].astype(F32)).astype(BF16)
        gv = (dot(e2_p[...], sel[:, cols]) * g[:, cols].astype(F32)).astype(BF16)
        xs[:, cols] = xv
        gs[:, cols] = gv
        for k in range(2):
            part = slice(k * sh, (k + 1) * sh)
            of, ob = dot(b_t[:, part], xv[part]), dot(c_t[:, part], gv[part])
            for j in range(2):
                own_f[k, 2 * q + j] = of[:, j * LANES:(j + 1) * LANES]
                own_b[k, 2 * q + j] = ob[:, j * LANES:(j + 1) * LANES]

        @pl.when(z == 0)
        def _():
            forward(2 * q)
            forward(2 * q + 1)

        @pl.when(z == zn - 1)
        def _():
            @pl.when(q > 0)
            def _():
                backward(2 * q)

            backward(2 * q + 1)

        return carry

    @pl.when(z == zn - 1)
    def _():
        with jax.named_scope("first pair"):
            gv = (dot(e2_p[...], sel[:, :LANES]) * g[:, :LANES].astype(F32)).astype(BF16)
            for k in range(2):
                part = slice(k * sh, (k + 1) * sh)
                own_b[k, 0] = dot(c_t[:, part], gv[part])
            backward(0)

    with jax.named_scope("summaries"):
        lax.fori_loop(0, groups, summarize, 0)

    for k in range(1, hn):
        weights_copy(k).start()

    with jax.named_scope("scores"):
        l_rows = log_decay.T
        for h in range(heads):
            l_t[h] = l_rows[h:h + 1, :]
        l_b[...] = dot(packed(log_decay - jnp.log(jnp.maximum(delta, 1e-37))), sel[...])
        gate = jax.nn.sigmoid(pre)
        gates[0] = gate
        gates[1] = jnp.where(delta > 1e-30, gate / jnp.maximum(delta, 1e-30), 1.0)
        for k in range(2):
            part = slice(k * sh, (k + 1) * sh)
            st[k] = jnp.where(causal, dot(b_all[part], c_all[part], NT), 0.0)
    other = {"batch": lax.rem(bt + 1, bn)}

    def core_copy(i, src, to):
        return pltpu.make_async_remote_copy(src, to, c_ss.at[i], c_rs.at[i], device_id=other, device_id_type=MESH)

    share = ut.shape[1]
    part_rows = uto.shape[1]
    block = share * part_rows
    my_rows = hx if split else 0
    chunk = math.lcm(block, LANES)
    for c in range(width // chunk):
        turned = u[:, c * chunk:(c + 1) * chunk].astype(F32).T
        for i in range(chunk // block):
            k, b = divmod(c * (chunk // block) + i, bn)
            for r in range(share):
                at = i * block + r * part_rows
                ut[b, r, k] = turned[at:at + part_rows].astype(BF16)
    core_u = core_copy(5, ut.at[lax.rem(bt + 1, bn), my_rows], uto)
    core_u.start()

    def local_pair(p):
        cols = columns(p)
        for k in range(2):
            part = slice(k * sh, (k + 1) * sh)
            gt = g[part, cols]
            xb = x[part, cols]
            sm = st[k]
            dm = dot(jnp.concatenate([xb * lm, xb * hm], axis=0), gt, NT)
            add = None
            mixed = []
            dr = direct[part]
            for j in range(2):
                lr = l_t[2 * p + j][:, part]
                lcol = l_b[part, cols][:, 64 * j:64 * j + 1]
                decay = jnp.exp(jnp.minimum(lr - lcol, 30.0))
                mixed.append((decay * sm).astype(BF16))
                a = dm[j * sh:(j + 1) * sh] * decay
                add = a if add is None else add + a
                w = a * sm
                col_e[2 * p + j, :, part] = jnp.sum(w, axis=0, keepdims=True)
                dr = dr + jnp.where(lane[:sh] == 2 * p + j, jnp.sum(w, axis=1, keepdims=True), 0.0)
            direct[part] = dr
            dst[k] += add
            gx = dot(jnp.concatenate(mixed, axis=0), gt)
            gxi[part, cols] = jnp.where(low, gx[:sh], gx[sh:])

    def two(ref, q):
        return jnp.concatenate([ref[2 * q], ref[2 * q + 1]], axis=1)

    halves = [slice(k * sh, (k + 1) * sh) for k in range(2)]

    def maps_before(q):
        for part, ref in zip(halves, (rf, smid)):
            gacc[1, part] += dot(gs[part, columns(q, 2)], two(ref, q), NT)

    def maps_after(q):
        for part, ref in zip(halves, (gmid, rb)):
            gacc[0, part] += dot(xs[part, columns(q, 2)], two(ref, q), NT)

    def values_before(q):
        cols = columns(q, 2)
        cs = [dot(c_all[part], two(ref, q)) for part, ref in zip(halves, (rf, smid))]
        gl[...] += dot_sel(gs[:, cols].astype(F32) * jnp.concatenate(cs, axis=0), sel[:, cols])

    def values_after(q):
        cols = columns(q, 2)
        bs = [dot(b_all[part], two(ref, q)) for part, ref in zip(halves, (gmid, rb))]
        br = e1_b[:, cols] * jnp.concatenate(bs, axis=0)
        gval[:, cols] = (gxi[:, cols] + br).astype(BF16)
        qd[...] += dot_sel(x[:, cols].astype(F32) * br, sel[:, cols])

    def through(q):
        cols = columns(q, 2)
        both = [
            jnp.sum(two(before, q).astype(F32) * two(after, q).astype(F32), axis=0, keepdims=True)
            for before, after in ((rf, gmid), (smid, rb))
        ]
        row = lax.broadcasted_iota(jnp.int32, (8, 2 * LANES), 0)
        both = ends_b[:, cols] * jnp.where(row == 0, both[0], both[1])
        tails[...] += sum(dot(part, sel[:, cols], NT) for part in split3(both))

    late_f = jnp.maximum(4 * z - 2, 0)
    late_b = jnp.maximum(6 * (zn - 1 - z) - 4, 0)

    first_base = jnp.maximum(pairs, jnp.where(early == 1, late_f, late_b) + 1 + groups)
    second_base = jnp.maximum(first_base + groups, jnp.where(early == 1, late_b, late_f) + 1 + groups)

    def base_of(edge, far_edge, first, late):
        return jnp.where(edge, 1, jnp.where(far_edge, late + 1, jnp.where(first, first_base, second_base)))

    base_f = base_of(z == 0, z == zn - 1, early == 1, late_f)
    base_b = base_of(z == zn - 1, z == 0, early == 0, late_b)
    at_end = (z == 0) | (z == zn - 1)
    send_at = jnp.where(at_end, jnp.maximum(2 * groups, pairs) + 1, first_base + groups)

    def step_of(i, edge, base):
        k = i - base
        return k, jnp.where(at_end, k // 2, k), (k >= 0) & (jnp.logical_not(at_end) | (k % 2 == 0))

    def send_maps(role):
        part = early if role == 0 else 1 - early
        for k, rows_of in enumerate(halves):
            px[hx, part, rows_of] = (gacc[part, rows_of] + dot(mixers[part, k], mates[part, rows_of])).astype(BF16)
        for k in range(1, hn):
            maps_copy(role, k).start()

    def turn(i, carry):
        pf = i - late_f
        pb = i - late_b
        in_f, in_b = (pf >= 0) & (pf < pairs), (pb >= 0) & (pb < pairs)

        @pl.when(in_f & (z > 0))
        def _():
            with jax.named_scope("forward"):
                chain_f(pf).wait_recv()
                forward(pf)

        @pl.when(in_b & (z < zn - 1))
        def _():
            with jax.named_scope("backward"):
                chain_b(pb).wait_recv()
                backward(pb)

        @pl.when(i < pairs)
        def _():
            with jax.named_scope("local"):
                local_pair(i)

        kf, qf, on_f = step_of(i, z == 0, base_f)
        kb, qb, on_b = step_of(i, z == zn - 1, base_b)

        @pl.when(kf == 0)
        def _():
            maps_before(0)

        @pl.when(on_f & (qf > 0) & (qf < groups))
        def _():
            with jax.named_scope("before"):
                maps_before(qf)
                values_before(qf - 1)

        @pl.when(kb == 0)
        def _():
            maps_after(0)

        @pl.when(on_b & (qb > 0) & (qb < groups))
        def _():
            with jax.named_scope("after"):
                maps_after(qb)
                values_after(qb - 1)

        kt = i - jnp.maximum(late_f, late_b) - 2

        @pl.when((kt >= 0) & (kt < pairs - 2) & (kt % 2 == 0))
        def _():
            with jax.named_scope("through"):
                through(kt // 2)

        @pl.when(i == send_at)
        def _():
            with jax.named_scope("first map gradient"):
                send_maps(0)

        @pl.when(i == pairs)
        def _():
            with jax.named_scope("local sums"):
                for h in range(heads):
                    erows[h:h + 1, :] = col_e[h]
                net[...] = erows[...].T - direct[...]
                for k in range(2):
                    masked = jnp.where(causal, dst[k], 0.0)
                    mixers[0, k] = masked.astype(BF16)
                    mixers[1, k] = masked.T.astype(BF16)
                mates[0] = c_all
                mates[1] = b_all

        return carry

    lax.fori_loop(0, max(6 * (zn - 1) - 3, pairs) + 2 * groups + 1, turn, 0)

    with jax.named_scope("last map gradient"):
        send_maps(1)

    def along(i, src, to, k):
        there = lax.rem(z + k, zn)
        return pltpu.make_async_remote_copy(
            src, to.at[z], z_ss.at[i, k - 1], z_rs.at[i, k - 1], device_id={"tm": there}, device_id_type=MESH
        )

    def each_z(body):
        def turn(k, carry):
            body(k)
            return carry

        lax.fori_loop(1, zn, turn, 0)

    def both_heads(part):
        total = px[0, part].astype(F32)
        for k in range(1, hn):
            total = total + px[k, part].astype(F32)
        return total.astype(BF16)

    def product(ref, values):
        if part_rows % 16 == 0:
            return dot(ref[...].reshape(zn * part_rows, tokens), values).reshape(zn, part_rows, LANES)
        return jnp.stack([dot(ref[k], values) for k in range(zn)])

    def core_maps(role):
        return core_copy(2 if role == 0 else 6, psend.at[role], precv.at[role])

    def share_maps(role):
        for k in range(1, hn):
            maps_copy(role, k).wait()
        piece = both_heads(early if role == 0 else 1 - early)
        psend[role] = piece
        core_maps(role).start()
        plocal[role] = product(ut.at[bt, my_rows], piece)

    def z_copy_maps(role, k):
        part = early if role == 0 else 1 - early
        return along(2 if role == 0 else 4, zsend.at[part, lax.rem(z + k, zn)], zrecv.at[part], k)

    def spread_maps(role):
        part = early if role == 0 else 1 - early
        core_maps(role).wait()
        zsend[part] = (plocal[role] + product(uto, precv[role])).astype(BF16)
        zrecv[part, z] = zsend[part, z]
        each_z(lambda k: z_copy_maps(role, k).start())

    with jax.named_scope("share first maps"):
        core_u.wait()
        share_maps(0)

    with jax.named_scope("last values"):
        values_before(groups - 1)
        values_after(groups - 1)
        through(groups - 1)

    with jax.named_scope("step gradients"):
        upper = ((ti <= si) & ((ti < sh) == (si < sh))).astype(F32).astype(BF16)
        carried = qd[...]
        weighted = direct[...] + carried
        g_log = net[...] + gl[...] - carried
        ends_sum = tails[...]
        tail = [
            jnp.sum(carried[k * sh:(k + 1) * sh], axis=0, keepdims=True) + ends_sum[k:k + 1] for k in range(2)
        ]
        back = dot_ones(upper, g_log) + jnp.where(first, tail[0], tail[1])
        gate, per_delta = gates[0], gates[1]
        g_pre = weighted * per_delta + rate * back * gate
        smsend[...] = jnp.zeros_like(smsend)
        smsend[0:1, :] = jnp.sum(g_pre, axis=0, keepdims=True)
        smsend[1:2, :] = jnp.sum(delta * back, axis=0, keepdims=True) * rate
    gpx[hx] = g_pre.T[:rpad, :].astype(BF16)
    for k in range(1, hn):
        steps_copy(k).start()
    with jax.named_scope("step weight product"):
        wsend[...] = dot(gpx[hx], uu).astype(BF16)

    core_w = core_copy(0, wsend, wrecv)
    core_s = core_copy(1, smsend, smrecv)
    core_f = core_copy(3, wfsend, wfrecv)
    core_w.start()
    core_s.start()

    def z_start_small(k):
        along(0, wzsend.at[lax.rem(z + k, zn) if units > 1 else 0], wzrecv, k).start()
        along(1, smzsend, smzrecv, k).start()

    def z_wait_small(k):
        along(0, wzsend.at[lax.rem(z + k, zn) if units > 1 else 0], wzrecv, k).wait()
        along(1, smzsend, smzrecv, k).wait()

    def z_start_sums(k):
        along(3, wgrecv.at[z], wgrecv, k).start()

    def z_wait_sums(k):
        along(3, wgrecv.at[z], wgrecv, k).wait()

    with jax.named_scope("spread first maps"):
        spread_maps(0)
    with jax.named_scope("core w"):
        core_w.wait()
    core_s.wait()
    wsum[...] = wsend[...].astype(F32) + wrecv[...].astype(F32)
    mine = pl.ds(pl.multiple_of(bt * half, LANES), half)
    theirs = pl.ds(pl.multiple_of(lax.rem(bt + 1, bn) * half, LANES), half)
    for k in range(units):
        r, c = divmod(k, unit_cols)
        cols = pl.ds(pl.multiple_of(bt * half + c * unit, LANES), unit)
        wzsend[k] = wsum[r * unit_rows:(r + 1) * unit_rows, cols].astype(BF16)
    own_unit = z if units > 1 else 0
    wzrecv[z] = wzsend[own_unit]
    sz = smsend[...] + smrecv[...]
    smzsend[...] = sz
    smzrecv[z] = sz
    each_z(z_start_small)

    with jax.named_scope("share last maps"):
        share_maps(1)
    with jax.named_scope("spread last maps"):
        spread_maps(1)

    with jax.named_scope("small along z"):
        each_z(z_wait_small)
    total_w = wzrecv[0].astype(F32)
    total_s = smzrecv[0]
    for k in range(1, zn):
        total_w = total_w + wzrecv[k].astype(F32)
        total_s = total_s + smzrecv[k]
    wgrecv[own_unit] = total_w.astype(BF16)
    if units > 1:
        each_z(z_start_sums)
    gbias[...] = total_s[0:1, :heads]
    galog[...] = total_s[1:2, :heads]

    for k in range(1, hn):
        weights_copy(k).wait()
        steps_copy(k).wait()
    gp = jnp.concatenate([both_heads(0), both_heads(1)], axis=1)
    gpa = gpx[...].reshape(hn * rpad, tokens).astype(F32).T.astype(BF16)
    wa = wx[...].reshape(hn * rpad, width)
    with jax.named_scope("input gradient"):
        gin[...] = (dot(gp, wbc[...], NT) + dot(gpa, wa)).astype(BF16)

    with jax.named_scope("large along z"):
        for role in range(2):
            each_z(lambda k: z_copy_maps(role, k).wait())
    total = [sum(zrecv[part, k].astype(F32) for k in range(zn)) for part in range(2)]
    if split:
        fsend[...] = jnp.concatenate(total, axis=1).astype(BF16)
        final = pltpu.make_async_remote_copy(
            fsend, frecv, c_ss.at[4], c_rs.at[4], device_id={"head": lax.rem(hx + 1, hn)}, device_id_type=MESH
        )
        final.start()

    with jax.named_scope("sums along z"):
        if units > 1:
            each_z(z_wait_sums)
    for k in range(units):
        r, c = divmod(k, unit_cols)
        wfsend[r * unit_rows:(r + 1) * unit_rows, c * unit:(c + 1) * unit] = wgrecv[k]
    core_f.start()
    gwdt[:, mine] = wfsend[...].astype(F32)[:heads, :]

    if split:
        gwbc[pl.ds(pl.multiple_of(hx * part_rows, 16), part_rows), :] = fsend[...].astype(F32)
        with jax.named_scope("last exchange"):
            final.wait()
        gwbc[pl.ds(pl.multiple_of((1 - hx) * part_rows, 16), part_rows), :] = frecv[...].astype(F32)
    else:
        gwbc[...] = jnp.concatenate(total, axis=1)
    with jax.named_scope("core f"):
        core_f.wait()
    gwdt[:, theirs] = wfrecv[...].astype(F32)[:heads, :]

    @pl.when(z < zn - 1)
    def _():
        pltpu.make_async_remote_copy(
            sf, rf, f_ss, f_rs.at[0], device_id={"tm": lax.rem(z + 1, zn)}, device_id_type=MESH
        ).wait_send()

    @pl.when(z > 0)
    def _():
        pltpu.make_async_remote_copy(
            sb, rb, b_ss, b_rs.at[0], device_id={"tm": lax.rem(z + zn - 1, zn)}, device_id_type=MESH
        ).wait_send()


def on_device(sizes, u_input, head_values, grad_output, w_bc, w_dt, dt_bias, a_log):
    zn, hn, bn = sizes
    seqs, tokens, width = u_input.shape
    assert seqs == 1 and bn == 2
    heads = w_dt.shape[1]
    values = head_values.shape[2]
    both = w_bc.shape[1]
    pairs = heads // 2
    assert values == heads * 64 and both == 2 * LANES and heads % 4 == 0 and heads <= 32 and tokens == 2 * LANES
    block = width // (zn * bn)
    split = hn == 2 and block % 32 == 0
    share = hn if split else 1
    part_rows = block // share
    rpad = -(-heads // 16) * 16
    half = width // bn
    sh = tokens // 2
    unit_rows, unit = 16, half * rpad // (16 * zn)
    if (half * rpad) % (16 * zn) or unit == 0 or unit % LANES or half % unit:
        unit_rows, unit = rpad, half
    units = (rpad // unit_rows) * (half // unit)
    vm = pltpu.VMEM
    dma = pltpu.SemaphoreType.DMA
    scratch = [
        vm((tokens, width), BF16), vm((tokens, values), BF16), vm((tokens, values), BF16), vm((width, both), BF16),
        vm((heads, width), BF16), vm((1, heads), F32), vm((1, heads), F32), dma((7,)),
        vm((LANES, width), BF16), vm((bn, share, zn, part_rows, tokens), BF16), vm((zn, part_rows, tokens), BF16), vm((8, LANES), F32), vm((tokens, both), BF16),
        vm((heads, 1, tokens), F32), vm((tokens, values), F32), vm((tokens, values), F32),
        vm((tokens, LANES), BF16), vm((tokens, LANES), BF16),
        vm((8, values), F32), vm((LANES, values), BF16), vm((tokens, values), BF16), vm((tokens, values), BF16),
        vm((2, pairs, LANES, LANES), F32), vm((2, pairs, LANES, LANES), F32), vm((tokens, values), F32),
        vm((2, sh, sh), F32), vm((2, sh, sh), F32), vm((heads, 1, tokens), F32), vm((LANES, tokens), F32),
        vm((tokens, LANES), F32), vm((tokens, LANES), F32), vm((tokens, LANES), F32), vm((tokens, LANES), F32),
        vm((2, tokens, LANES), F32), vm((8, LANES), F32),
        vm((2, tokens, LANES), F32), vm((2, 2, sh, sh), BF16), vm((2, tokens, LANES), BF16),
        vm((pairs, LANES, LANES), BF16), vm((pairs, LANES, LANES), BF16),
        vm((pairs, LANES, LANES), BF16), vm((pairs, LANES, LANES), BF16),
        vm((pairs, LANES, LANES), BF16), vm((pairs, LANES, LANES), BF16),
        vm((hn, rpad, width), BF16), vm((hn, 2, tokens, LANES), BF16), vm((hn, rpad, tokens), BF16),
        vm((2, tokens, LANES), BF16), vm((2, tokens, LANES), BF16), vm((2, zn, part_rows, LANES), F32),
        vm((2, zn, part_rows, LANES), BF16), vm((2, zn, part_rows, LANES), BF16),
        vm((part_rows, both), BF16), vm((part_rows, both), BF16),
        vm((rpad, width), BF16), vm((rpad, width), BF16), vm((rpad, width), F32),
        vm((units, unit_rows, unit), BF16), vm((zn, unit_rows, unit), BF16), vm((units, unit_rows, unit), BF16),
        vm((rpad, half), BF16), vm((rpad, half), BF16),
        vm((8, LANES), F32), vm((8, LANES), F32), vm((8, LANES), F32), vm((zn, 8, LANES), F32),
        dma, dma((pairs,)), dma, dma((pairs,)),
        dma((4, hn - 1)), dma((4, hn - 1)), dma((7,)), dma((7,)), dma((5, zn - 1)), dma((5, zn - 1)),
    ]
    spec = pl.BlockSpec(memory_space=pltpu.VMEM)
    shapes = (
        ((tokens, width), BF16), ((tokens, values), BF16), ((block, both), F32),
        ((heads, width), F32), ((1, heads), F32), ((1, heads), F32),
    )
    kept = pl.pallas_call(
        functools.partial(kernel, zn, hn, bn, heads, split),
        out_shape=tuple(vm(*s) for s in shapes),
        in_specs=[pl.BlockSpec(memory_space=pl.ANY)] * 7,
        out_specs=[spec] * 6,
        scratch_shapes=scratch,
        compiler_params=pltpu.CompilerParams(
            collective_id=0, has_side_effects=True, vmem_limit_bytes=56 << 20
        ),
    )(
        u_input.reshape(tokens, width), head_values.reshape(tokens, values), grad_output.reshape(tokens, values),
        w_bc, w_dt.T, dt_bias.reshape(1, heads), a_log.reshape(1, heads),
    )
    gin, gval, gwbc, gwdt, gbias, galog = pl.pallas_call(
        write,
        out_shape=tuple(jax.ShapeDtypeStruct(*s) for s in shapes),
        in_specs=[spec] * 6,
        out_specs=[pl.BlockSpec(memory_space=pl.ANY)] * 6,
        scratch_shapes=[dma((6,))],
        compiler_params=pltpu.CompilerParams(vmem_limit_bytes=1 << 20),
    )(*kept)
    return (
        gin.reshape(1, tokens, width), gval.reshape(1, tokens, values), gwbc,
        gwdt.T, gbias.reshape(heads), galog.reshape(heads),
    )


def write(*refs):
    sems = refs[12]
    copies = [pltpu.make_async_copy(refs[i], refs[6 + i], sems.at[i]) for i in range(6)]
    for copy in copies:
        copy.start()
    for copy in copies:
        copy.wait()


def solution(mesh):
    sizes = (mesh.shape["tm"], mesh.shape["head"], mesh.shape["batch"])
    return jax.shard_map(
        functools.partial(on_device, sizes),
        mesh=mesh,
        in_specs=(
            P(("groups", "batch"), "tm", None),
            P(("groups", "batch"), "tm", "head"),
            P(("groups", "batch"), "tm", "head"),
            P(),
            P(None, "head"),
            P("head"),
            P("head"),
        ),
        out_specs=(
            P(("groups", "batch"), "tm", None),
            P(("groups", "batch"), "tm", "head"),
            P(("groups", "tm", "batch"), None),
            P("groups", "head"),
            P(("groups", "head")),
            P(("groups", "head")),
        ),
        check_vma=False,
    )
```

```python
import functools
import math

import jax
import jax.numpy as jnp
from jax import lax
from jax.experimental import pallas as pl
from jax.experimental.pallas import tpu as pltpu
from jax.sharding import PartitionSpec as P

MESH = pl.DeviceIdType.MESH
F32 = jnp.float32
BF16 = jnp.bfloat16
LANES = 128
NT = (((1,), (1,)), ((), ()))
TN = (((0,), (0,)), ((), ()))


def dot(a, b, dims=(((1,), (0,)), ((), ()))):
    return lax.dot_general(a, b, dims, preferred_element_type=F32)


def split3(v):
    hi = v.astype(BF16)
    rest = v - hi.astype(F32)
    mid = rest.astype(BF16)
    return hi, mid, (rest - mid.astype(F32)).astype(BF16)


def dot_ones(a, v):
    hi, mid, lo = split3(v)
    return dot(a, hi) + dot(a, mid) + dot(a, lo)


def dot_sel(v, ones):
    hi = v.astype(BF16)
    lo = (v - hi.astype(F32)).astype(BF16)
    return dot(hi, ones, NT) + dot(lo, ones, NT)


def kernel(
    zn, hn, bn, heads, split,
    u_h, x_h, g_h, wbc_h, wdt_h, bias_h, alog_h,
    gin, gval, gwbc, gwdt, gbias, galog,
    u, x, g, wbc, wdt, bias, alog,
    wpad, ut, uto, rows, proj, l_t, l_b, e1_b, e1_p, e2_p, ends_b, sel, xs, gs, own_f, own_b, gxi, st, dst, col_e, erows,
    direct, qd, gl, net, gates, tails, gacc, mixers, mates, smid, gmid,
    sf, rf, sb, rb, wx, px, gpx, psend, precv, plocal, zsend, zrecv, fsend, frecv,
    wsend, wrecv, wsum, wzsend, wzrecv, wgrecv, wfsend, wfrecv, smsend, smrecv, smzsend, smzrecv,
    f_ss, f_rs, b_ss, b_rs, h_ss, h_rs, c_ss, c_rs, z_ss, z_rs,
):
    z, hx, bt = lax.axis_index("tm"), lax.axis_index("head"), lax.axis_index("batch")
    tokens, width = u.shape
    pairs = heads // 2
    groups = pairs // 2
    state = LANES
    sh = tokens // 2
    rpad = wx.shape[1]
    half = width // bn
    units, unit_rows, unit = wzsend.shape
    unit_cols = half // unit

    loads = [
        pltpu.make_async_copy(src, to, c_ss.at[i])
        for i, (src, to) in enumerate((
            (wdt_h, wdt), (bias_h, bias), (alog_h, alog), (u_h, u), (wbc_h, wbc), (x_h, x), (g_h, g)
        ))
    ]
    for load in loads[:3]:
        load.start()
    for j, (src, to, n) in enumerate(((u_h, u, 4), (wbc_h, wbc, 4), (x_h, x, 2), (g_h, g, 2))):
        step = src.shape[0] // n
        for i in range(n):
            at = pl.ds(i * step, step)
            pltpu.make_async_copy(src.at[at], to.at[at], c_ss.at[3 + j]).start()

    barrier = pltpu.get_barrier_semaphore()
    for k in range(1, zn):
        pl.semaphore_signal(barrier, inc=1, device_id={"tm": lax.rem(z + k, zn)}, device_id_type=MESH)
    for k in range(1, hn):
        pl.semaphore_signal(barrier, inc=1, device_id={"head": lax.rem(hx + k, hn)}, device_id_type=MESH)
    for k in range(1, bn):
        pl.semaphore_signal(barrier, inc=1, device_id={"batch": lax.rem(bt + k, bn)}, device_id_type=MESH)

    lane = lax.broadcasted_iota(jnp.int32, (tokens, LANES), 1)
    low = lax.broadcasted_iota(jnp.int32, (sh, LANES), 1) < 64
    lm = low.astype(F32).astype(BF16)
    hm = 1.0 - lm
    ti = lax.broadcasted_iota(jnp.int32, (tokens, tokens), 0)
    si = lax.broadcasted_iota(jnp.int32, (tokens, tokens), 1)
    lower = (ti >= si).astype(F32).astype(BF16)
    causal = ti[:sh, :sh] <= si[:sh, :sh]

    with jax.named_scope("initial"):
        wpad[...] = jnp.zeros_like(wpad)
        rows[...] = jnp.zeros_like(rows)
        which = lax.broadcasted_iota(jnp.int32, (LANES, LANES), 0)
        head_of = lax.shift_right_logical(lax.broadcasted_iota(jnp.int32, (LANES, LANES), 1), 6)
        used = jnp.where(which < 96, which & 31, -1)
        for p in range(pairs):
            sel[:, p * LANES:(p + 1) * LANES] = (used == head_of + 2 * p).astype(F32).astype(BF16)
        dst[...] = jnp.zeros_like(dst)
        direct[...] = jnp.zeros_like(direct)
        gl[...] = jnp.zeros_like(gl)
        qd[...] = jnp.zeros_like(qd)
        gacc[...] = jnp.zeros_like(gacc)
        tails[...] = jnp.zeros_like(tails)
        erows[...] = jnp.zeros_like(erows)

        @pl.when(z == 0)
        def _():
            rf[...] = jnp.zeros_like(rf)

        @pl.when(z == zn - 1)
        def _():
            rb[...] = jnp.zeros_like(rb)

    def packed(v):
        hi, mid, lo = split3(v)
        at = lane[:v.shape[0]]
        mid, lo = pltpu.roll(mid.astype(F32), 32, 1), pltpu.roll(lo.astype(F32), 64, 1)
        return jnp.where(at < 32, hi.astype(F32), jnp.where(at < 64, mid, jnp.where(at < 96, lo, 0.0))).astype(BF16)

    with jax.named_scope("wait for u"):
        for load in loads[:5]:
            load.wait()
    wpad[:heads, :] = wdt[...]
    rows[0:1, :heads] = bias[...]
    rows[1:2, :heads] = alog[...]
    wx[hx] = wpad[:rpad, :]
    uu = u[...]
    proj[...] = dot(uu, wbc[...]).astype(BF16)
    b_all, c_all = proj[:, :state], proj[:, state:]
    b_t = b_all.astype(F32).T.astype(BF16)
    c_t = c_all.astype(F32).T.astype(BF16)
    pre = dot(uu, wpad[...], NT) + rows[0:1, :]
    small = jnp.exp(-jnp.abs(pre))
    delta = jnp.maximum(pre, 0.0) + jnp.log1p(small)
    rate = -jnp.exp(rows[1:2, :])
    log_decay = dot_ones(lower, delta * rate)
    mid_l, last_l = log_decay[sh - 1:sh, :], log_decay[tokens - 1:tokens, :]
    first = lax.broadcasted_iota(jnp.int32, (tokens, LANES), 0) < sh
    e1 = packed(jnp.exp(jnp.where(first, mid_l, last_l) - log_decay) * delta)
    e2 = packed(jnp.exp(jnp.where(first, log_decay, log_decay - mid_l)))
    e1_p[...] = e1
    e2_p[...] = e2
    ends = jnp.concatenate([jnp.exp(mid_l), jnp.exp(last_l - mid_l), jnp.zeros((6, LANES), F32)], axis=0)
    ends_b[...] = dot(packed(ends), sel[...])
    with jax.named_scope("wait for values"):
        loads[5].wait()
        loads[6].wait()
    with jax.named_scope("wait for devices"):
        pl.semaphore_wait(barrier, zn + hn + bn - 3)

    def head_copy(i, ref, k):
        return pltpu.make_async_remote_copy(
            ref, ref, h_ss.at[i, k - 1], h_rs.at[i, k - 1],
            device_id={"head": lax.rem(hx + k, hn)}, device_id_type=MESH,
        )

    def weights_copy(k):
        return head_copy(0, wx.at[hx], k)

    def steps_copy(k):
        return head_copy(1, gpx.at[hx], k)

    early = jnp.where(2 * z < zn, 1, 0)

    def maps_copy(role, k):
        return head_copy(2 + role, px.at[hx, early if role == 0 else 1 - early], k)

    def chain_f(p, piece):
        at, size, sem = piece
        return pltpu.make_async_remote_copy(
            sf.at[p, pl.ds(at, size)], rf.at[p, pl.ds(at, size)], f_ss, f_rs.at[sem],
            device_id={"tm": lax.rem(z + 1, zn)}, device_id_type=MESH,
        )

    def chain_b(p, piece):
        at, size, sem = piece
        return pltpu.make_async_remote_copy(
            sb.at[p, pl.ds(at, size)], rb.at[p, pl.ds(at, size)], b_ss, b_rs.at[sem],
            device_id={"tm": lax.rem(z + zn - 1, zn)}, device_id_type=MESH,
        )

    def pieces(p, body):
        @pl.when(p < pairs - 1)
        def _():
            body((0, state, p))

        @pl.when(p == pairs - 1)
        def _():
            body((0, state // 2, pairs - 1))
            body((state // 2, state // 2, pairs))

    def columns(p, n=1):
        return pl.ds(pl.multiple_of(p * n * LANES, LANES), n * LANES)

    def forward(p, arrives):
        cols = columns(p)

        def body(piece):
            at, size, _ = piece
            if arrives:
                chain_f(p, piece).wait_recv()
            part = slice(at, at + size)
            middle = ends_b[0:1, cols] * rf[p, part].astype(F32) + own_f[0, p, part]
            smid[p, part] = middle.astype(BF16)
            sf[p, part] = (ends_b[1:2, cols] * middle + own_f[1, p, part]).astype(BF16)

            @pl.when(z < zn - 1)
            def _():
                chain_f(p, piece).start()

        pieces(p, body)

    def backward(p, arrives):
        cols = columns(p)

        def body(piece):
            at, size, _ = piece
            if arrives:
                chain_b(p, piece).wait_recv()
            part = slice(at, at + size)
            middle = ends_b[1:2, cols] * rb[p, part].astype(F32) + own_b[1, p, part]
            gmid[p, part] = middle.astype(BF16)
            sb[p, part] = (ends_b[0:1, cols] * middle + own_b[0, p, part]).astype(BF16)

            @pl.when(z > 0)
            def _():
                chain_b(p, piece).start()

        pieces(p, body)

    def summarize(q, carry):
        cols = columns(q, 2)
        spread = dot(e1_p[...], sel[:, cols])
        e1_b[:, cols] = spread
        xv = (spread * x[:, cols].astype(F32)).astype(BF16)
        gv = (dot(e2_p[...], sel[:, cols]) * g[:, cols].astype(F32)).astype(BF16)
        xs[:, cols] = xv
        gs[:, cols] = gv
        for k in range(2):
            part = slice(k * sh, (k + 1) * sh)
            of, ob = dot(b_t[:, part], xv[part]), dot(c_t[:, part], gv[part])
            for j in range(2):
                own_f[k, 2 * q + j] = of[:, j * LANES:(j + 1) * LANES]
                own_b[k, 2 * q + j] = ob[:, j * LANES:(j + 1) * LANES]

        @pl.when(z == 0)
        def _():
            forward(2 * q, False)
            forward(2 * q + 1, False)

        @pl.when(z == zn - 1)
        def _():
            @pl.when(q > 0)
            def _():
                backward(2 * q, False)

            backward(2 * q + 1, False)

        return carry

    @pl.when(z == zn - 1)
    def _():
        with jax.named_scope("first pair"):
            gv = (dot(e2_p[...], sel[:, :LANES]) * g[:, :LANES].astype(F32)).astype(BF16)
            for k in range(2):
                part = slice(k * sh, (k + 1) * sh)
                own_b[k, 0] = dot(c_t[:, part], gv[part])
            backward(0, False)

    with jax.named_scope("summaries"):
        lax.fori_loop(0, groups, summarize, 0)

    for k in range(1, hn):
        weights_copy(k).start()

    with jax.named_scope("scores"):
        l_rows = log_decay.T
        for h in range(heads):
            l_t[h] = l_rows[h:h + 1, :]
        l_b[...] = dot(packed(log_decay - jnp.log(jnp.maximum(delta, 1e-37))), sel[...])
        gate = jax.nn.sigmoid(pre)
        gates[0] = gate
        gates[1] = jnp.where(delta > 1e-30, gate / jnp.maximum(delta, 1e-30), 1.0)
        for k in range(2):
            part = slice(k * sh, (k + 1) * sh)
            st[k] = jnp.where(causal, dot(b_all[part], c_all[part], NT), 0.0)
    other = {"batch": lax.rem(bt + 1, bn)}

    def core_copy(i, src, to):
        return pltpu.make_async_remote_copy(src, to, c_ss.at[i], c_rs.at[i], device_id=other, device_id_type=MESH)

    share = ut.shape[1]
    part_rows = uto.shape[1]
    block = share * part_rows
    my_rows = hx if split else 0
    chunk = math.lcm(block, LANES)
    for c in range(width // chunk):
        turned = u[:, c * chunk:(c + 1) * chunk].astype(F32).T
        for i in range(chunk // block):
            k, b = divmod(c * (chunk // block) + i, bn)
            for r in range(share):
                at = i * block + r * part_rows
                ut[b, r, k] = turned[at:at + part_rows].astype(BF16)
    core_u = core_copy(5, ut.at[lax.rem(bt + 1, bn), my_rows], uto)
    core_u.start()

    def local_pair(p):
        cols = columns(p)
        for k in range(2):
            part = slice(k * sh, (k + 1) * sh)
            gt = g[part, cols]
            xb = x[part, cols]
            sm = st[k]
            dm = dot(jnp.concatenate([xb * lm, xb * hm], axis=0), gt, NT)
            add = None
            mixed = []
            dr = direct[part]
            for j in range(2):
                lr = l_t[2 * p + j][:, part]
                lcol = l_b[part, cols][:, 64 * j:64 * j + 1]
                decay = jnp.exp(jnp.minimum(lr - lcol, 30.0))
                mixed.append((decay * sm).astype(BF16))
                a = dm[j * sh:(j + 1) * sh] * decay
                add = a if add is None else add + a
                w = a * sm
                col_e[2 * p + j, :, part] = jnp.sum(w, axis=0, keepdims=True)
                dr = dr + jnp.where(lane[:sh] == 2 * p + j, jnp.sum(w, axis=1, keepdims=True), 0.0)
            direct[part] = dr
            dst[k] += add
            gx = dot(jnp.concatenate(mixed, axis=0), gt)
            gxi[part, cols] = jnp.where(low, gx[:sh], gx[sh:])

    def two(ref, q):
        return jnp.concatenate([ref[2 * q], ref[2 * q + 1]], axis=1)

    halves = [slice(k * sh, (k + 1) * sh) for k in range(2)]

    def maps_before(q):
        for part, ref in zip(halves, (rf, smid)):
            gacc[1, part] += dot(gs[part, columns(q, 2)], two(ref, q), NT)

    def maps_after(q):
        for part, ref in zip(halves, (gmid, rb)):
            gacc[0, part] += dot(xs[part, columns(q, 2)], two(ref, q), NT)

    def values_before(q):
        cols = columns(q, 2)
        cs = [dot(c_all[part], two(ref, q)) for part, ref in zip(halves, (rf, smid))]
        gl[...] += dot_sel(gs[:, cols].astype(F32) * jnp.concatenate(cs, axis=0), sel[:, cols])

    def values_after(q):
        cols = columns(q, 2)
        bs = [dot(b_all[part], two(ref, q)) for part, ref in zip(halves, (gmid, rb))]
        br = e1_b[:, cols] * jnp.concatenate(bs, axis=0)
        gval[:, cols] = (gxi[:, cols] + br).astype(BF16)
        qd[...] += dot_sel(x[:, cols].astype(F32) * br, sel[:, cols])

    def through(q):
        cols = columns(q, 2)
        both = [
            jnp.sum(two(before, q).astype(F32) * two(after, q).astype(F32), axis=0, keepdims=True)
            for before, after in ((rf, gmid), (smid, rb))
        ]
        row = lax.broadcasted_iota(jnp.int32, (8, 2 * LANES), 0)
        both = ends_b[:, cols] * jnp.where(row == 0, both[0], both[1])
        tails[...] += sum(dot(part, sel[:, cols], NT) for part in split3(both))

    late_f = jnp.maximum(4 * z - 2, 0)
    late_b = jnp.maximum(6 * (zn - 1 - z) - 4, 0)

    first_base = jnp.maximum(pairs, jnp.where(early == 1, late_f, late_b) + 1 + groups)
    second_base = jnp.maximum(first_base + groups, jnp.where(early == 1, late_b, late_f) + 1 + groups)

    def base_of(edge, far_edge, first, late):
        return jnp.where(edge, 1, jnp.where(far_edge, late + 1, jnp.where(first, first_base, second_base)))

    base_f = base_of(z == 0, z == zn - 1, early == 1, late_f)
    base_b = base_of(z == zn - 1, z == 0, early == 0, late_b)
    at_end = (z == 0) | (z == zn - 1)
    send_at = jnp.where(at_end, jnp.maximum(2 * groups, pairs) + 1, first_base + groups)

    def step_of(i, edge, base):
        k = i - base
        return k, jnp.where(at_end, k // 2, k), (k >= 0) & (jnp.logical_not(at_end) | (k % 2 == 0))

    def send_maps(role):
        part = early if role == 0 else 1 - early
        for k, rows_of in enumerate(halves):
            px[hx, part, rows_of] = (gacc[part, rows_of] + dot(mixers[part, k], mates[part, rows_of])).astype(BF16)
        for k in range(1, hn):
            maps_copy(role, k).start()

    def along(i, src, to, k):
        there = lax.rem(z + k, zn)
        return pltpu.make_async_remote_copy(
            src, to.at[z], z_ss.at[i], z_rs.at[i, k - 1], device_id={"tm": there}, device_id_type=MESH
        )

    def all_sent(i, blocks):
        pltpu.make_async_remote_copy(
            blocks.at[pl.ds(0, zn - 1)], blocks.at[pl.ds(0, zn - 1)], z_ss.at[i], z_rs.at[i, 0],
            device_id={"tm": lax.rem(z + 1, zn)}, device_id_type=MESH,
        ).wait_send()

    def each_z(body):
        def turn(k, carry):
            body(k)
            return carry

        lax.fori_loop(1, zn, turn, 0)

    def both_heads(part):
        total = px[0, part].astype(F32)
        for k in range(1, hn):
            total = total + px[k, part].astype(F32)
        return total.astype(BF16)

    def product(ref, values):
        if part_rows % 16 == 0:
            return dot(ref[...].reshape(zn * part_rows, tokens), values).reshape(zn, part_rows, LANES)
        return jnp.stack([dot(ref[k], values) for k in range(zn)])

    def core_maps(role):
        return core_copy(2 if role == 0 else 6, psend.at[role], precv.at[role])

    def share_maps(role):
        for k in range(1, hn):
            maps_copy(role, k).wait()
        piece = both_heads(early if role == 0 else 1 - early)
        psend[role] = piece
        core_maps(role).start()
        plocal[role] = product(ut.at[bt, my_rows], piece)

    def z_copy_maps(role, k):
        part = early if role == 0 else 1 - early
        return along(2 if role == 0 else 4, zsend.at[part, lax.rem(z + k, zn)], zrecv.at[part], k)

    def spread_maps(role):
        part = early if role == 0 else 1 - early
        if role == 0:
            core_u.wait()
        core_maps(role).wait()
        zsend[part] = (plocal[role] + product(uto, precv[role])).astype(BF16)
        zrecv[part, z] = zsend[part, z]
        each_z(lambda k: z_copy_maps(role, k).start())

    def turn(i, carry):
        pf = i - late_f
        pb = i - late_b
        in_f, in_b = (pf >= 0) & (pf < pairs), (pb >= 0) & (pb < pairs)

        @pl.when(in_f & (z > 0))
        def _():
            with jax.named_scope("forward"):
                forward(pf, True)

        @pl.when(in_b & (z < zn - 1))
        def _():
            with jax.named_scope("backward"):
                backward(pb, True)

        @pl.when(i < pairs)
        def _():
            with jax.named_scope("local"):
                local_pair(i)

        kf, qf, on_f = step_of(i, z == 0, base_f)
        kb, qb, on_b = step_of(i, z == zn - 1, base_b)

        @pl.when(kf == 0)
        def _():
            maps_before(0)

        @pl.when(on_f & (qf == groups - 1))
        def _():
            maps_before(groups - 1)

        @pl.when(on_b & (qb == groups - 1))
        def _():
            maps_after(groups - 1)

        @pl.when(on_f & (qf > 0) & (qf < groups - 1))
        def _():
            with jax.named_scope("before"):
                maps_before(qf)
                values_before(qf - 1)

        @pl.when(kb == 0)
        def _():
            maps_after(0)

        @pl.when(on_b & (qb > 0) & (qb < groups - 1))
        def _():
            with jax.named_scope("after"):
                maps_after(qb)
                values_after(qb - 1)

        kt = i - jnp.maximum(late_f, late_b) - 2

        @pl.when((kt >= 0) & (kt < pairs - 2) & (kt % 2 == 0))
        def _():
            with jax.named_scope("through"):
                through(kt // 2)

        @pl.when(i == send_at)
        def _():
            with jax.named_scope("first map gradient"):
                send_maps(0)

        @pl.when(at_end & (i == send_at + 6))
        def _():
            with jax.named_scope("share first maps"):
                share_maps(0)

        @pl.when(at_end & (i == send_at + 8))
        def _():
            with jax.named_scope("spread first maps"):
                spread_maps(0)

        @pl.when(i == pairs)
        def _():
            with jax.named_scope("local sums"):
                for h in range(heads):
                    erows[h:h + 1, :] = col_e[h]
                net[...] = erows[...].T - direct[...]
                for k in range(2):
                    masked = jnp.where(causal, dst[k], 0.0)
                    mixers[0, k] = masked.astype(BF16)
                    mixers[1, k] = masked.T.astype(BF16)
                mates[0] = c_all
                mates[1] = b_all

        return carry

    lax.fori_loop(0, max(6 * (zn - 1) - 3, pairs, 10) + 2 * groups + 1, turn, 0)

    with jax.named_scope("last map gradient"):
        send_maps(1)

    @pl.when(jnp.logical_not(at_end))
    def _():
        with jax.named_scope("share first maps"):
            share_maps(0)

    with jax.named_scope("last values"):
        for q in range(max(groups - 2, 0), groups):
            values_before(q)
            values_after(q)
        through(groups - 1)

    with jax.named_scope("step gradients"):
        upper = ((ti <= si) & ((ti < sh) == (si < sh))).astype(F32).astype(BF16)
        carried = qd[...]
        weighted = direct[...] + carried
        g_log = net[...] + gl[...] - carried
        ends_sum = tails[...]
        tail = [
            jnp.sum(carried[k * sh:(k + 1) * sh], axis=0, keepdims=True) + ends_sum[k:k + 1] for k in range(2)
        ]
        back = dot_ones(upper, g_log) + jnp.where(first, tail[0], tail[1])
        gate, per_delta = gates[0], gates[1]
        g_pre = weighted * per_delta + rate * back * gate
        smsend[...] = jnp.zeros_like(smsend)
        smsend[0:1, :] = jnp.sum(g_pre, axis=0, keepdims=True)
        smsend[1:2, :] = jnp.sum(delta * back, axis=0, keepdims=True) * rate
    gpx[hx] = g_pre.T[:rpad, :].astype(BF16)
    for k in range(1, hn):
        steps_copy(k).start()
    with jax.named_scope("step weight product"):
        wsend[...] = dot(gpx[hx], uu).astype(BF16)

    core_w = core_copy(0, wsend, wrecv)
    core_s = core_copy(1, smsend, smrecv)
    core_f = core_copy(3, wfsend, wfrecv)
    core_w.start()
    core_s.start()

    def z_start_small(k):
        along(0, wzsend.at[lax.rem(z + k, zn) if units > 1 else 0], wzrecv, k).start()
        along(1, smzsend, smzrecv, k).start()

    def z_wait_small(k):
        along(0, wzsend.at[lax.rem(z + k, zn) if units > 1 else 0], wzrecv, k).wait_recv()
        along(1, smzsend, smzrecv, k).wait_recv()

    def z_start_sums(k):
        along(3, wgrecv.at[z], wgrecv, k).start()

    def z_wait_sums(k):
        along(3, wgrecv.at[z], wgrecv, k).wait_recv()

    @pl.when(jnp.logical_not(at_end))
    def _():
        with jax.named_scope("spread first maps"):
            spread_maps(0)

    with jax.named_scope("core w"):
        core_w.wait()
    core_s.wait()
    wsum[...] = wsend[...].astype(F32) + wrecv[...].astype(F32)
    mine = pl.ds(pl.multiple_of(bt * half, LANES), half)
    theirs = pl.ds(pl.multiple_of(lax.rem(bt + 1, bn) * half, LANES), half)
    for k in range(units):
        r, c = divmod(k, unit_cols)
        cols = pl.ds(pl.multiple_of(bt * half + c * unit, LANES), unit)
        wzsend[k] = wsum[r * unit_rows:(r + 1) * unit_rows, cols].astype(BF16)
    own_unit = z if units > 1 else 0
    wzrecv[z] = wzsend[own_unit]
    sz = smsend[...] + smrecv[...]
    smzsend[...] = sz
    smzrecv[z] = sz
    each_z(z_start_small)

    with jax.named_scope("share last maps"):
        share_maps(1)
    with jax.named_scope("spread last maps"):
        spread_maps(1)

    with jax.named_scope("small along z"):
        each_z(z_wait_small)
    total_w = wzrecv[0].astype(F32)
    total_s = smzrecv[0]
    for k in range(1, zn):
        total_w = total_w + wzrecv[k].astype(F32)
        total_s = total_s + smzrecv[k]
    wgrecv[own_unit] = total_w.astype(BF16)
    if units > 1:
        each_z(z_start_sums)
    gbias[...] = total_s[0:1, :heads]
    galog[...] = total_s[1:2, :heads]

    for k in range(1, hn):
        weights_copy(k).wait()
        steps_copy(k).wait()
    gp = jnp.concatenate([both_heads(0), both_heads(1)], axis=1)
    gpa = gpx[...].reshape(hn * rpad, tokens).astype(F32).T.astype(BF16)
    wa = wx[...].reshape(hn * rpad, width)
    with jax.named_scope("input gradient"):
        gin[...] = (dot(gp, wbc[...], NT) + dot(gpa, wa)).astype(BF16)

    with jax.named_scope("large along z"):
        for role in range(2):
            each_z(lambda k: z_copy_maps(role, k).wait_recv())
    total = [sum(zrecv[part, k].astype(F32) for k in range(zn)) for part in range(2)]
    if split:
        fsend[...] = jnp.concatenate(total, axis=1).astype(BF16)
        final = pltpu.make_async_remote_copy(
            fsend, frecv, c_ss.at[4], c_rs.at[4], device_id={"head": lax.rem(hx + 1, hn)}, device_id_type=MESH
        )
        final.start()

    with jax.named_scope("sums along z"):
        if units > 1:
            each_z(z_wait_sums)
    for k in range(units):
        r, c = divmod(k, unit_cols)
        wfsend[r * unit_rows:(r + 1) * unit_rows, c * unit:(c + 1) * unit] = wgrecv[k]
    core_f.start()
    gwdt[:, mine] = wfsend[...].astype(F32)[:heads, :]

    if split:
        gwbc[pl.ds(pl.multiple_of(hx * part_rows, 16), part_rows), :] = fsend[...].astype(F32)
        with jax.named_scope("last exchange"):
            final.wait()
        gwbc[pl.ds(pl.multiple_of((1 - hx) * part_rows, 16), part_rows), :] = frecv[...].astype(F32)
    else:
        gwbc[...] = jnp.concatenate(total, axis=1)
    with jax.named_scope("core f"):
        core_f.wait()
    gwdt[:, theirs] = wfrecv[...].astype(F32)[:heads, :]

    all_sent(0, wzrecv)
    all_sent(1, smzrecv)
    all_sent(2, zrecv.at[0])
    all_sent(4, zrecv.at[0])
    if units > 1:
        all_sent(3, wgrecv)

    @pl.when(z < zn - 1)
    def _():
        pltpu.make_async_remote_copy(
            sf, rf, f_ss, f_rs.at[0], device_id={"tm": lax.rem(z + 1, zn)}, device_id_type=MESH
        ).wait_send()

    @pl.when(z > 0)
    def _():
        pltpu.make_async_remote_copy(
            sb, rb, b_ss, b_rs.at[0], device_id={"tm": lax.rem(z + zn - 1, zn)}, device_id_type=MESH
        ).wait_send()


def on_device(sizes, u_input, head_values, grad_output, w_bc, w_dt, dt_bias, a_log):
    zn, hn, bn = sizes
    seqs, tokens, width = u_input.shape
    assert seqs == 1 and bn == 2
    heads = w_dt.shape[1]
    values = head_values.shape[2]
    both = w_bc.shape[1]
    pairs = heads // 2
    assert values == heads * 64 and both == 2 * LANES and heads % 4 == 0 and heads <= 32 and tokens == 2 * LANES
    block = width // (zn * bn)
    split = hn == 2 and block % 32 == 0
    share = hn if split else 1
    part_rows = block // share
    rpad = -(-heads // 16) * 16
    half = width // bn
    sh = tokens // 2
    unit_rows, unit = 16, half * rpad // (16 * zn)
    if (half * rpad) % (16 * zn) or unit == 0 or unit % LANES or half % unit:
        unit_rows, unit = rpad, half
    units = (rpad // unit_rows) * (half // unit)
    vm = pltpu.VMEM
    dma = pltpu.SemaphoreType.DMA
    scratch = [
        vm((tokens, width), BF16), vm((tokens, values), BF16), vm((tokens, values), BF16), vm((width, both), BF16),
        vm((heads, width), BF16), vm((1, heads), F32), vm((1, heads), F32),
        vm((LANES, width), BF16), vm((bn, share, zn, part_rows, tokens), BF16), vm((zn, part_rows, tokens), BF16), vm((8, LANES), F32), vm((tokens, both), BF16),
        vm((heads, 1, tokens), F32), vm((tokens, values), F32), vm((tokens, values), F32),
        vm((tokens, LANES), BF16), vm((tokens, LANES), BF16),
        vm((8, values), F32), vm((LANES, values), BF16), vm((tokens, values), BF16), vm((tokens, values), BF16),
        vm((2, pairs, LANES, LANES), F32), vm((2, pairs, LANES, LANES), F32), vm((tokens, values), F32),
        vm((2, sh, sh), F32), vm((2, sh, sh), F32), vm((heads, 1, tokens), F32), vm((LANES, tokens), F32),
        vm((tokens, LANES), F32), vm((tokens, LANES), F32), vm((tokens, LANES), F32), vm((tokens, LANES), F32),
        vm((2, tokens, LANES), F32), vm((8, LANES), F32),
        vm((2, tokens, LANES), F32), vm((2, 2, sh, sh), BF16), vm((2, tokens, LANES), BF16),
        vm((pairs, LANES, LANES), BF16), vm((pairs, LANES, LANES), BF16),
        vm((pairs, LANES, LANES), BF16), vm((pairs, LANES, LANES), BF16),
        vm((pairs, LANES, LANES), BF16), vm((pairs, LANES, LANES), BF16),
        vm((hn, rpad, width), BF16), vm((hn, 2, tokens, LANES), BF16), vm((hn, rpad, tokens), BF16),
        vm((2, tokens, LANES), BF16), vm((2, tokens, LANES), BF16), vm((2, zn, part_rows, LANES), F32),
        vm((2, zn, part_rows, LANES), BF16), vm((2, zn, part_rows, LANES), BF16),
        vm((part_rows, both), BF16), vm((part_rows, both), BF16),
        vm((rpad, width), BF16), vm((rpad, width), BF16), vm((rpad, width), F32),
        vm((units, unit_rows, unit), BF16), vm((zn, unit_rows, unit), BF16), vm((units, unit_rows, unit), BF16),
        vm((rpad, half), BF16), vm((rpad, half), BF16),
        vm((8, LANES), F32), vm((8, LANES), F32), vm((8, LANES), F32), vm((zn, 8, LANES), F32),
        dma, dma((pairs + 1,)), dma, dma((pairs + 1,)),
        dma((4, hn - 1)), dma((4, hn - 1)), dma((7,)), dma((7,)), dma((5,)), dma((5, zn - 1)),
    ]
    spec = pl.BlockSpec(memory_space=pltpu.VMEM)
    shapes = (
        ((tokens, width), BF16), ((tokens, values), BF16), ((block, both), F32),
        ((heads, width), F32), ((1, heads), F32), ((1, heads), F32),
    )
    kept = pl.pallas_call(
        functools.partial(kernel, zn, hn, bn, heads, split),
        out_shape=tuple(vm(*s) for s in shapes),
        in_specs=[pl.BlockSpec(memory_space=pl.ANY)] * 7,
        out_specs=[spec] * 6,
        scratch_shapes=scratch,
        compiler_params=pltpu.CompilerParams(
            collective_id=0, has_side_effects=True, vmem_limit_bytes=56 << 20
        ),
    )(
        u_input.reshape(tokens, width), head_values.reshape(tokens, values), grad_output.reshape(tokens, values),
        w_bc, w_dt.T, dt_bias.reshape(1, heads), a_log.reshape(1, heads),
    )
    gin, gval, gwbc, gwdt, gbias, galog = pl.pallas_call(
        write,
        out_shape=tuple(jax.ShapeDtypeStruct(*s) for s in shapes),
        in_specs=[spec] * 6,
        out_specs=[pl.BlockSpec(memory_space=pl.ANY)] * 6,
        scratch_shapes=[dma((6,))],
        compiler_params=pltpu.CompilerParams(vmem_limit_bytes=1 << 20),
    )(*kept)
    return (
        gin.reshape(1, tokens, width), gval.reshape(1, tokens, values), gwbc,
        gwdt.T, gbias.reshape(heads), galog.reshape(heads),
    )


def write(*refs):
    sems = refs[12]
    copies = [pltpu.make_async_copy(refs[i], refs[6 + i], sems.at[i]) for i in range(6)]
    for copy in copies:
        copy.start()
    for copy in copies:
        copy.wait()


def solution(mesh):
    sizes = (mesh.shape["tm"], mesh.shape["head"], mesh.shape["batch"])
    return jax.shard_map(
        functools.partial(on_device, sizes),
        mesh=mesh,
        in_specs=(
            P(("groups", "batch"), "tm", None),
            P(("groups", "batch"), "tm", "head"),
            P(("groups", "batch"), "tm", "head"),
            P(),
            P(None, "head"),
            P("head"),
            P("head"),
        ),
        out_specs=(
            P(("groups", "batch"), "tm", None),
            P(("groups", "batch"), "tm", "head"),
            P(("groups", "tm", "batch"), None),
            P("groups", "head"),
            P(("groups", "head")),
            P(("groups", "head")),
        ),
        check_vma=False,
    )
```

```python
import functools
import math

import jax
import jax.numpy as jnp
from jax import lax
from jax.experimental import pallas as pl
from jax.experimental.pallas import tpu as pltpu
from jax.sharding import PartitionSpec as P

MESH = pl.DeviceIdType.MESH
F32 = jnp.float32
BF16 = jnp.bfloat16
LANES = 128
NT = (((1,), (1,)), ((), ()))
TN = (((0,), (0,)), ((), ()))


def dot(a, b, dims=(((1,), (0,)), ((), ()))):
    return lax.dot_general(a, b, dims, preferred_element_type=F32)


def split3(v):
    hi = v.astype(BF16)
    rest = v - hi.astype(F32)
    mid = rest.astype(BF16)
    return hi, mid, (rest - mid.astype(F32)).astype(BF16)


def dot_ones(a, v):
    hi, mid, lo = split3(v)
    return dot(a, hi) + dot(a, mid) + dot(a, lo)


def dot_sel(v, ones):
    hi = v.astype(BF16)
    lo = (v - hi.astype(F32)).astype(BF16)
    return dot(hi, ones, NT) + dot(lo, ones, NT)


def kernel(
    zn, hn, bn, heads, split,
    u_h, x_h, g_h, wbc_h, wdt_h, bias_h, alog_h,
    gin, gval, gwbc, gwdt, gbias, galog,
    u, x, g, wbc, wdt, bias, alog,
    wpad, ut, uto, rows, proj, l_t, l_b, e1_b, e1_p, e2_p, ends_b, sel, xs, gs, own_f, own_b, gxi, st, dst, col_e, erows,
    direct, qd, gl, net, gates, tails, gacc, mixers, mates, smid, gmid,
    sf, rf, sb, rb, wx, px, gpx, psend, precv, plocal, zsend, zrecv, fsend, frecv,
    wsend, wrecv, wsum, wzsend, wzrecv, wgrecv, wfsend, wfrecv, smsend, smrecv, smzsend, smzrecv,
    f_ss, f_rs, b_ss, b_rs, h_ss, h_rs, c_ss, c_rs, z_ss, z_rs,
):
    z, hx, bt = lax.axis_index("tm"), lax.axis_index("head"), lax.axis_index("batch")
    tokens, width = u.shape
    pairs = heads // 2
    groups = pairs // 2
    state = LANES
    sh = tokens // 2
    rpad = wx.shape[1]
    half = width // bn
    units, unit_rows, unit = wzsend.shape
    unit_cols = half // unit

    loads = [
        pltpu.make_async_copy(src, to, c_ss.at[i])
        for i, (src, to) in enumerate((
            (wdt_h, wdt), (bias_h, bias), (alog_h, alog), (u_h, u), (wbc_h, wbc), (x_h, x), (g_h, g)
        ))
    ]
    for load in loads[:3]:
        load.start()
    for j, (src, to, n) in enumerate(((u_h, u, 4), (wbc_h, wbc, 4), (x_h, x, 2), (g_h, g, 2))):
        step = src.shape[0] // n
        for i in range(n):
            at = pl.ds(i * step, step)
            pltpu.make_async_copy(src.at[at], to.at[at], c_ss.at[3 + j]).start()

    barrier = pltpu.get_barrier_semaphore()
    @pl.when(z > 0)
    def _():
        pl.semaphore_signal(barrier, inc=1, device_id={"tm": lax.rem(z + zn - 1, zn)}, device_id_type=MESH)

    @pl.when(z < zn - 1)
    def _():
        pl.semaphore_signal(barrier, inc=1, device_id={"tm": lax.rem(z + 1, zn)}, device_id_type=MESH)

    for k in range(1, hn):
        pl.semaphore_signal(barrier, inc=1, device_id={"head": lax.rem(hx + k, hn)}, device_id_type=MESH)
    for k in range(1, bn):
        pl.semaphore_signal(barrier, inc=1, device_id={"batch": lax.rem(bt + k, bn)}, device_id_type=MESH)

    lane = lax.broadcasted_iota(jnp.int32, (tokens, LANES), 1)
    low = lax.broadcasted_iota(jnp.int32, (sh, LANES), 1) < 64
    lm = low.astype(F32).astype(BF16)
    hm = 1.0 - lm
    ti = lax.broadcasted_iota(jnp.int32, (tokens, tokens), 0)
    si = lax.broadcasted_iota(jnp.int32, (tokens, tokens), 1)
    lower = (ti >= si).astype(F32).astype(BF16)
    causal = ti[:sh, :sh] <= si[:sh, :sh]

    with jax.named_scope("initial"):
        wpad[...] = jnp.zeros_like(wpad)
        rows[...] = jnp.zeros_like(rows)
        which = lax.broadcasted_iota(jnp.int32, (LANES, LANES), 0)
        head_of = lax.shift_right_logical(lax.broadcasted_iota(jnp.int32, (LANES, LANES), 1), 6)
        used = jnp.where(which < 96, which & 31, -1)
        for p in range(pairs):
            sel[:, p * LANES:(p + 1) * LANES] = (used == head_of + 2 * p).astype(F32).astype(BF16)
        dst[...] = jnp.zeros_like(dst)
        direct[...] = jnp.zeros_like(direct)
        gl[...] = jnp.zeros_like(gl)
        qd[...] = jnp.zeros_like(qd)
        gacc[...] = jnp.zeros_like(gacc)
        tails[...] = jnp.zeros_like(tails)
        erows[...] = jnp.zeros_like(erows)

        @pl.when(z == 0)
        def _():
            rf[...] = jnp.zeros_like(rf)

        @pl.when(z == zn - 1)
        def _():
            rb[...] = jnp.zeros_like(rb)

    def packed(v):
        hi, mid, lo = split3(v)
        at = lane[:v.shape[0]]
        mid, lo = pltpu.roll(mid.astype(F32), 32, 1), pltpu.roll(lo.astype(F32), 64, 1)
        return jnp.where(at < 32, hi.astype(F32), jnp.where(at < 64, mid, jnp.where(at < 96, lo, 0.0))).astype(BF16)

    with jax.named_scope("wait for u"):
        for load in loads[:5]:
            load.wait()
    wpad[:heads, :] = wdt[...]
    rows[0:1, :heads] = bias[...]
    rows[1:2, :heads] = alog[...]
    wx[hx] = wpad[:rpad, :]
    uu = u[...]
    proj[...] = dot(uu, wbc[...]).astype(BF16)
    b_all, c_all = proj[:, :state], proj[:, state:]
    b_t = b_all.astype(F32).T.astype(BF16)
    c_t = c_all.astype(F32).T.astype(BF16)
    pre = dot(uu, wpad[...], NT) + rows[0:1, :]
    small = jnp.exp(-jnp.abs(pre))
    delta = jnp.maximum(pre, 0.0) + jnp.log1p(small)
    rate = -jnp.exp(rows[1:2, :])
    log_decay = dot_ones(lower, delta * rate)
    mid_l, last_l = log_decay[sh - 1:sh, :], log_decay[tokens - 1:tokens, :]
    first = lax.broadcasted_iota(jnp.int32, (tokens, LANES), 0) < sh
    e1 = packed(jnp.exp(jnp.where(first, mid_l, last_l) - log_decay) * delta)
    e2 = packed(jnp.exp(jnp.where(first, log_decay, log_decay - mid_l)))
    e1_p[...] = e1
    e2_p[...] = e2
    ends = jnp.concatenate([jnp.exp(mid_l), jnp.exp(last_l - mid_l), jnp.zeros((6, LANES), F32)], axis=0)
    ends_b[...] = dot(packed(ends), sel[...])
    with jax.named_scope("wait for values"):
        loads[5].wait()
        loads[6].wait()
    with jax.named_scope("wait for devices"):
        pl.semaphore_wait(barrier, jnp.where((z == 0) | (z == zn - 1), 1, 2) + hn + bn - 2)

    def head_copy(i, ref, k):
        return pltpu.make_async_remote_copy(
            ref, ref, h_ss.at[i, k - 1], h_rs.at[i, k - 1],
            device_id={"head": lax.rem(hx + k, hn)}, device_id_type=MESH,
        )

    def weights_copy(k):
        return head_copy(0, wx.at[hx], k)

    def steps_copy(k):
        return head_copy(1, gpx.at[hx], k)

    early = jnp.where(2 * z < zn, 1, 0)

    def maps_copy(role, k):
        return head_copy(2 + role, px.at[hx, early if role == 0 else 1 - early], k)

    def chain_f(p, piece):
        at, size, sem = piece
        return pltpu.make_async_remote_copy(
            sf.at[p, pl.ds(at, size)], rf.at[p, pl.ds(at, size)], f_ss, f_rs.at[sem],
            device_id={"tm": lax.rem(z + 1, zn)}, device_id_type=MESH,
        )

    def chain_b(p, piece):
        at, size, sem = piece
        return pltpu.make_async_remote_copy(
            sb.at[p, pl.ds(at, size)], rb.at[p, pl.ds(at, size)], b_ss, b_rs.at[sem],
            device_id={"tm": lax.rem(z + zn - 1, zn)}, device_id_type=MESH,
        )

    def pieces(p, body):
        @pl.when(p < pairs - 1)
        def _():
            body((0, state, p))

        @pl.when(p == pairs - 1)
        def _():
            body((0, state // 2, pairs - 1))
            body((state // 2, state // 2, pairs))

    def columns(p, n=1):
        return pl.ds(pl.multiple_of(p * n * LANES, LANES), n * LANES)

    def forward(p, arrives):
        cols = columns(p)

        def body(piece):
            at, size, _ = piece
            if arrives:
                chain_f(p, piece).wait_recv()
            part = slice(at, at + size)
            middle = ends_b[0:1, cols] * rf[p, part].astype(F32) + own_f[0, p, part]
            smid[p, part] = middle.astype(BF16)
            sf[p, part] = (ends_b[1:2, cols] * middle + own_f[1, p, part]).astype(BF16)

            @pl.when(z < zn - 1)
            def _():
                chain_f(p, piece).start()

        pieces(p, body)

    def backward(p, arrives):
        cols = columns(p)

        def body(piece):
            at, size, _ = piece
            if arrives:
                chain_b(p, piece).wait_recv()
            part = slice(at, at + size)
            middle = ends_b[1:2, cols] * rb[p, part].astype(F32) + own_b[1, p, part]
            gmid[p, part] = middle.astype(BF16)
            sb[p, part] = (ends_b[0:1, cols] * middle + own_b[0, p, part]).astype(BF16)

            @pl.when(z > 0)
            def _():
                chain_b(p, piece).start()

        pieces(p, body)

    def summarize(q, carry):
        cols = columns(q, 2)
        spread = dot(e1_p[...], sel[:, cols])
        e1_b[:, cols] = spread
        xv = (spread * x[:, cols].astype(F32)).astype(BF16)
        gv = (dot(e2_p[...], sel[:, cols]) * g[:, cols].astype(F32)).astype(BF16)
        xs[:, cols] = xv
        gs[:, cols] = gv
        for k in range(2):
            part = slice(k * sh, (k + 1) * sh)
            of, ob = dot(b_t[:, part], xv[part]), dot(c_t[:, part], gv[part])
            for j in range(2):
                own_f[k, 2 * q + j] = of[:, j * LANES:(j + 1) * LANES]
                own_b[k, 2 * q + j] = ob[:, j * LANES:(j + 1) * LANES]

        @pl.when(z == 0)
        def _():
            forward(2 * q, False)
            forward(2 * q + 1, False)

        @pl.when(z == zn - 1)
        def _():
            @pl.when(q > 0)
            def _():
                backward(2 * q, False)

            backward(2 * q + 1, False)

        return carry

    @pl.when(z == zn - 1)
    def _():
        with jax.named_scope("first pair"):
            gv = (dot(e2_p[...], sel[:, :LANES]) * g[:, :LANES].astype(F32)).astype(BF16)
            for k in range(2):
                part = slice(k * sh, (k + 1) * sh)
                own_b[k, 0] = dot(c_t[:, part], gv[part])
            backward(0, False)

    with jax.named_scope("summaries"):
        lax.fori_loop(0, groups, summarize, 0)

    for k in range(1, hn):
        weights_copy(k).start()

    with jax.named_scope("scores"):
        l_rows = log_decay.T
        for h in range(heads):
            l_t[h] = l_rows[h:h + 1, :]
        l_b[...] = dot(packed(log_decay - jnp.log(jnp.maximum(delta, 1e-37))), sel[...])
        gate = jax.nn.sigmoid(pre)
        gates[0] = gate
        gates[1] = jnp.where(delta > 1e-30, gate / jnp.maximum(delta, 1e-30), 1.0)
        for k in range(2):
            part = slice(k * sh, (k + 1) * sh)
            st[k] = jnp.where(causal, dot(b_all[part], c_all[part], NT), 0.0)
    other = {"batch": lax.rem(bt + 1, bn)}

    def core_copy(i, src, to):
        return pltpu.make_async_remote_copy(src, to, c_ss.at[i], c_rs.at[i], device_id=other, device_id_type=MESH)

    share = ut.shape[1]
    part_rows = uto.shape[1]
    block = share * part_rows
    my_rows = hx if split else 0
    chunk = math.lcm(block, LANES)
    for c in range(width // chunk):
        turned = u[:, c * chunk:(c + 1) * chunk].astype(F32).T
        for i in range(chunk // block):
            k, b = divmod(c * (chunk // block) + i, bn)
            for r in range(share):
                at = i * block + r * part_rows
                ut[b, r, k] = turned[at:at + part_rows].astype(BF16)
    core_u = core_copy(5, ut.at[lax.rem(bt + 1, bn), my_rows], uto)
    core_u.start()

    def local_pair(p):
        cols = columns(p)
        for k in range(2):
            part = slice(k * sh, (k + 1) * sh)
            gt = g[part, cols]
            xb = x[part, cols]
            sm = st[k]
            dm = dot(jnp.concatenate([xb * lm, xb * hm], axis=0), gt, NT)
            add = None
            mixed = []
            dr = direct[part]
            for j in range(2):
                lr = l_t[2 * p + j][:, part]
                lcol = l_b[part, cols][:, 64 * j:64 * j + 1]
                decay = jnp.exp(jnp.minimum(lr - lcol, 30.0))
                mixed.append((decay * sm).astype(BF16))
                a = dm[j * sh:(j + 1) * sh] * decay
                add = a if add is None else add + a
                w = a * sm
                col_e[2 * p + j, :, part] = jnp.sum(w, axis=0, keepdims=True)
                dr = dr + jnp.where(lane[:sh] == 2 * p + j, jnp.sum(w, axis=1, keepdims=True), 0.0)
            direct[part] = dr
            dst[k] += add
            gx = dot(jnp.concatenate(mixed, axis=0), gt)
            gxi[part, cols] = jnp.where(low, gx[:sh], gx[sh:])

    def two(ref, q):
        return jnp.concatenate([ref[2 * q], ref[2 * q + 1]], axis=1)

    kept = max(groups - 3, 0)
    halves = [slice(k * sh, (k + 1) * sh) for k in range(2)]

    def maps_before(q):
        for part, ref in zip(halves, (rf, smid)):
            gacc[1, part] += dot(gs[part, columns(q, 2)], two(ref, q), NT)

    def maps_after(q):
        for part, ref in zip(halves, (gmid, rb)):
            gacc[0, part] += dot(xs[part, columns(q, 2)], two(ref, q), NT)

    def values_before(q):
        cols = columns(q, 2)
        cs = [dot(c_all[part], two(ref, q)) for part, ref in zip(halves, (rf, smid))]
        gl[...] += dot_sel(gs[:, cols].astype(F32) * jnp.concatenate(cs, axis=0), sel[:, cols])

    def values_after(q):
        cols = columns(q, 2)
        bs = [dot(b_all[part], two(ref, q)) for part, ref in zip(halves, (gmid, rb))]
        br = e1_b[:, cols] * jnp.concatenate(bs, axis=0)
        gval[:, cols] = (gxi[:, cols] + br).astype(BF16)
        qd[...] += dot_sel(x[:, cols].astype(F32) * br, sel[:, cols])

    def through(q):
        cols = columns(q, 2)
        both = [
            jnp.sum(two(before, q).astype(F32) * two(after, q).astype(F32), axis=0, keepdims=True)
            for before, after in ((rf, gmid), (smid, rb))
        ]
        row = lax.broadcasted_iota(jnp.int32, (8, 2 * LANES), 0)
        both = ends_b[:, cols] * jnp.where(row == 0, both[0], both[1])
        tails[...] += sum(dot(part, sel[:, cols], NT) for part in split3(both))

    late_f = jnp.maximum(4 * z - 2, 0)
    late_b = jnp.maximum(6 * (zn - 1 - z) - 4, 0)

    first_base = jnp.maximum(pairs, jnp.where(early == 1, late_f, late_b) + 1 + groups)
    second_base = jnp.maximum(first_base + groups, jnp.where(early == 1, late_b, late_f) + 1 + groups)

    def base_of(edge, far_edge, first, late):
        return jnp.where(edge, 1, jnp.where(far_edge, late + 1, jnp.where(first, first_base, second_base)))

    base_f = base_of(z == 0, z == zn - 1, early == 1, late_f)
    base_b = base_of(z == zn - 1, z == 0, early == 0, late_b)
    at_end = (z == 0) | (z == zn - 1)
    send_at = jnp.where(at_end, jnp.maximum(2 * groups, pairs) + 1, first_base + groups)

    def step_of(i, edge, base):
        k = i - base
        return k, jnp.where(at_end, k // 2, k), (k >= 0) & (jnp.logical_not(at_end) | (k % 2 == 0))

    def send_maps(role):
        part = early if role == 0 else 1 - early
        for k, rows_of in enumerate(halves):
            px[hx, part, rows_of] = (gacc[part, rows_of] + dot(mixers[part, k], mates[part, rows_of])).astype(BF16)
        for k in range(1, hn):
            maps_copy(role, k).start()

    def along(i, src, to, k):
        there = lax.rem(z + k, zn)
        return pltpu.make_async_remote_copy(
            src, to.at[z], z_ss.at[i], z_rs.at[i, k - 1], device_id={"tm": there}, device_id_type=MESH
        )

    def all_sent(i, blocks):
        pltpu.make_async_remote_copy(
            blocks.at[pl.ds(0, zn - 1)], blocks.at[pl.ds(0, zn - 1)], z_ss.at[i], z_rs.at[i, 0],
            device_id={"tm": lax.rem(z + 1, zn)}, device_id_type=MESH,
        ).wait_send()

    def each_z(body):
        def turn(k, carry):
            body(k)
            return carry

        lax.fori_loop(1, zn, turn, 0)

    def both_heads(part):
        total = px[0, part].astype(F32)
        for k in range(1, hn):
            total = total + px[k, part].astype(F32)
        return total.astype(BF16)

    def product(ref, values):
        if part_rows % 16 == 0:
            return dot(ref[...].reshape(zn * part_rows, tokens), values).reshape(zn, part_rows, LANES)
        return jnp.stack([dot(ref[k], values) for k in range(zn)])

    def core_maps(role):
        return core_copy(2 if role == 0 else 6, psend.at[role], precv.at[role])

    def share_maps(role):
        for k in range(1, hn):
            maps_copy(role, k).wait()
        piece = both_heads(early if role == 0 else 1 - early)
        psend[role] = piece
        core_maps(role).start()
        plocal[role] = product(ut.at[bt, my_rows], piece)

    def z_copy_maps(role, k):
        part = early if role == 0 else 1 - early
        return along(2 if role == 0 else 4, zsend.at[part, lax.rem(z + k, zn)], zrecv.at[part], k)

    def spread_maps(role):
        part = early if role == 0 else 1 - early
        if role == 0:
            core_u.wait()
        core_maps(role).wait()
        zsend[part] = (plocal[role] + product(uto, precv[role])).astype(BF16)
        zrecv[part, z] = zsend[part, z]
        each_z(lambda k: z_copy_maps(role, k).start())

    def turn(i, carry):
        pf = i - late_f
        pb = i - late_b
        in_f, in_b = (pf >= 0) & (pf < pairs), (pb >= 0) & (pb < pairs)

        @pl.when(in_f & (z > 0))
        def _():
            with jax.named_scope("forward"):
                forward(pf, True)

        @pl.when(in_b & (z < zn - 1))
        def _():
            with jax.named_scope("backward"):
                backward(pb, True)

        @pl.when(i < pairs)
        def _():
            with jax.named_scope("local"):
                local_pair(i)

        kf, qf, on_f = step_of(i, z == 0, base_f)
        kb, qb, on_b = step_of(i, z == zn - 1, base_b)

        @pl.when(kf == 0)
        def _():
            maps_before(0)

        @pl.when(on_f & (qf == groups - 1))
        def _():
            maps_before(groups - 1)

        @pl.when(on_b & (qb == groups - 1))
        def _():
            maps_after(groups - 1)

        @pl.when(on_f & (qf > 0) & (qf < groups - 1))
        def _():
            with jax.named_scope("before"):
                maps_before(qf)
                values_before(qf - 1)

        @pl.when(kb == 0)
        def _():
            maps_after(0)

        @pl.when(on_b & (qb > 0) & (qb < groups - 1))
        def _():
            with jax.named_scope("after"):
                maps_after(qb)
                values_after(qb - 1)

        kt = i - jnp.maximum(late_f, late_b) - 2

        @pl.when((kt >= 0) & (kt < jnp.where(at_end, 2 * kept, pairs - 2)) & (kt % 2 == 0))
        def _():
            with jax.named_scope("through"):
                through(kt // 2)

        @pl.when(i == send_at)
        def _():
            with jax.named_scope("first map gradient"):
                send_maps(0)

        @pl.when(at_end & (i == send_at + 6))
        def _():
            with jax.named_scope("share first maps"):
                share_maps(0)

        @pl.when(at_end & (i == send_at + 8))
        def _():
            with jax.named_scope("spread first maps"):
                spread_maps(0)

        @pl.when(i == pairs)
        def _():
            with jax.named_scope("local sums"):
                for h in range(heads):
                    erows[h:h + 1, :] = col_e[h]
                net[...] = erows[...].T - direct[...]
                for k in range(2):
                    masked = jnp.where(causal, dst[k], 0.0)
                    mixers[0, k] = masked.astype(BF16)
                    mixers[1, k] = masked.T.astype(BF16)
                mates[0] = c_all
                mates[1] = b_all

        return carry

    lax.fori_loop(0, max(6 * (zn - 1) - 3, pairs, 10) + 2 * groups + 1, turn, 0)

    with jax.named_scope("last map gradient"):
        send_maps(1)

    @pl.when(jnp.logical_not(at_end))
    def _():
        with jax.named_scope("share first maps"):
            share_maps(0)

    with jax.named_scope("last values"):
        for q in range(max(groups - 2, 0), groups):
            values_before(q)
            values_after(q)
        @pl.when(at_end)
        def _():
            for q in range(kept, groups):
                through(q)

        @pl.when(jnp.logical_not(at_end))
        def _():
            through(groups - 1)

    with jax.named_scope("step gradients"):
        upper = ((ti <= si) & ((ti < sh) == (si < sh))).astype(F32).astype(BF16)
        carried = qd[...]
        weighted = direct[...] + carried
        g_log = net[...] + gl[...] - carried
        ends_sum = tails[...]
        tail = [
            jnp.sum(carried[k * sh:(k + 1) * sh], axis=0, keepdims=True) + ends_sum[k:k + 1] for k in range(2)
        ]
        back = dot_ones(upper, g_log) + jnp.where(first, tail[0], tail[1])
        gate, per_delta = gates[0], gates[1]
        g_pre = weighted * per_delta + rate * back * gate
        smsend[...] = jnp.zeros_like(smsend)
        smsend[0:1, :] = jnp.sum(g_pre, axis=0, keepdims=True)
        smsend[1:2, :] = jnp.sum(delta * back, axis=0, keepdims=True) * rate
    gpx[hx] = g_pre.T[:rpad, :].astype(BF16)
    for k in range(1, hn):
        steps_copy(k).start()
    with jax.named_scope("step weight product"):
        wsend[...] = dot(gpx[hx], uu).astype(BF16)

    core_w = core_copy(0, wsend, wrecv)
    core_s = core_copy(1, smsend, smrecv)
    core_f = core_copy(3, wfsend, wfrecv)
    core_w.start()
    core_s.start()

    def z_start_small(k):
        along(0, wzsend.at[lax.rem(z + k, zn) if units > 1 else 0], wzrecv, k).start()
        along(1, smzsend, smzrecv, k).start()

    def z_wait_small(k):
        along(0, wzsend.at[lax.rem(z + k, zn) if units > 1 else 0], wzrecv, k).wait_recv()
        along(1, smzsend, smzrecv, k).wait_recv()

    def z_start_sums(k):
        along(3, wgrecv.at[z], wgrecv, k).start()

    def z_wait_sums(k):
        along(3, wgrecv.at[z], wgrecv, k).wait_recv()

    @pl.when(jnp.logical_not(at_end))
    def _():
        with jax.named_scope("spread first maps"):
            spread_maps(0)

    with jax.named_scope("core w"):
        core_w.wait()
    core_s.wait()
    wsum[...] = wsend[...].astype(F32) + wrecv[...].astype(F32)
    mine = pl.ds(pl.multiple_of(bt * half, LANES), half)
    theirs = pl.ds(pl.multiple_of(lax.rem(bt + 1, bn) * half, LANES), half)
    for k in range(units):
        r, c = divmod(k, unit_cols)
        cols = pl.ds(pl.multiple_of(bt * half + c * unit, LANES), unit)
        wzsend[k] = wsum[r * unit_rows:(r + 1) * unit_rows, cols].astype(BF16)
    own_unit = z if units > 1 else 0
    wzrecv[z] = wzsend[own_unit]
    sz = smsend[...] + smrecv[...]
    smzsend[...] = sz
    smzrecv[z] = sz
    each_z(z_start_small)

    with jax.named_scope("share last maps"):
        share_maps(1)
    with jax.named_scope("spread last maps"):
        spread_maps(1)

    with jax.named_scope("small along z"):
        each_z(z_wait_small)
    total_w = wzrecv[0].astype(F32)
    total_s = smzrecv[0]
    for k in range(1, zn):
        total_w = total_w + wzrecv[k].astype(F32)
        total_s = total_s + smzrecv[k]
    wgrecv[own_unit] = total_w.astype(BF16)
    if units > 1:
        each_z(z_start_sums)
    gbias[...] = total_s[0:1, :heads]
    galog[...] = total_s[1:2, :heads]

    for k in range(1, hn):
        weights_copy(k).wait()
        steps_copy(k).wait()
    gp = jnp.concatenate([both_heads(0), both_heads(1)], axis=1)
    gpa = gpx[...].reshape(hn * rpad, tokens).astype(F32).T.astype(BF16)
    wa = wx[...].reshape(hn * rpad, width)
    with jax.named_scope("input gradient"):
        gin[...] = (dot(gp, wbc[...], NT) + dot(gpa, wa)).astype(BF16)

    with jax.named_scope("large along z"):
        for role in range(2):
            each_z(lambda k: z_copy_maps(role, k).wait_recv())
    total = [sum(zrecv[part, k].astype(F32) for k in range(zn)) for part in range(2)]
    if split:
        fsend[...] = jnp.concatenate(total, axis=1).astype(BF16)
        final = pltpu.make_async_remote_copy(
            fsend, frecv, c_ss.at[4], c_rs.at[4], device_id={"head": lax.rem(hx + 1, hn)}, device_id_type=MESH
        )
        final.start()

    with jax.named_scope("sums along z"):
        if units > 1:
            each_z(z_wait_sums)
    for k in range(units):
        r, c = divmod(k, unit_cols)
        wfsend[r * unit_rows:(r + 1) * unit_rows, c * unit:(c + 1) * unit] = wgrecv[k]
    core_f.start()
    gwdt[:, mine] = wfsend[...].astype(F32)[:heads, :]

    if split:
        gwbc[pl.ds(pl.multiple_of(hx * part_rows, 16), part_rows), :] = fsend[...].astype(F32)
        with jax.named_scope("last exchange"):
            final.wait()
        gwbc[pl.ds(pl.multiple_of((1 - hx) * part_rows, 16), part_rows), :] = frecv[...].astype(F32)
    else:
        gwbc[...] = jnp.concatenate(total, axis=1)
    with jax.named_scope("core f"):
        core_f.wait()
    gwdt[:, theirs] = wfrecv[...].astype(F32)[:heads, :]

    all_sent(0, wzrecv)
    all_sent(1, smzrecv)
    all_sent(2, zrecv.at[0])
    all_sent(4, zrecv.at[0])
    if units > 1:
        all_sent(3, wgrecv)

    @pl.when(z < zn - 1)
    def _():
        pltpu.make_async_remote_copy(
            sf, rf, f_ss, f_rs.at[0], device_id={"tm": lax.rem(z + 1, zn)}, device_id_type=MESH
        ).wait_send()

    @pl.when(z > 0)
    def _():
        pltpu.make_async_remote_copy(
            sb, rb, b_ss, b_rs.at[0], device_id={"tm": lax.rem(z + zn - 1, zn)}, device_id_type=MESH
        ).wait_send()


def on_device(sizes, u_input, head_values, grad_output, w_bc, w_dt, dt_bias, a_log):
    zn, hn, bn = sizes
    seqs, tokens, width = u_input.shape
    assert seqs == 1 and bn == 2
    heads = w_dt.shape[1]
    values = head_values.shape[2]
    both = w_bc.shape[1]
    pairs = heads // 2
    assert values == heads * 64 and both == 2 * LANES and heads % 4 == 0 and heads <= 32 and tokens == 2 * LANES
    block = width // (zn * bn)
    split = hn == 2 and block % 32 == 0
    share = hn if split else 1
    part_rows = block // share
    rpad = -(-heads // 16) * 16
    half = width // bn
    sh = tokens // 2
    unit_rows, unit = 16, half * rpad // (16 * zn)
    if (half * rpad) % (16 * zn) or unit == 0 or unit % LANES or half % unit:
        unit_rows, unit = rpad, half
    units = (rpad // unit_rows) * (half // unit)
    vm = pltpu.VMEM
    dma = pltpu.SemaphoreType.DMA
    scratch = [
        vm((tokens, width), BF16), vm((tokens, values), BF16), vm((tokens, values), BF16), vm((width, both), BF16),
        vm((heads, width), BF16), vm((1, heads), F32), vm((1, heads), F32),
        vm((LANES, width), BF16), vm((bn, share, zn, part_rows, tokens), BF16), vm((zn, part_rows, tokens), BF16), vm((8, LANES), F32), vm((tokens, both), BF16),
        vm((heads, 1, tokens), F32), vm((tokens, values), F32), vm((tokens, values), F32),
        vm((tokens, LANES), BF16), vm((tokens, LANES), BF16),
        vm((8, values), F32), vm((LANES, values), BF16), vm((tokens, values), BF16), vm((tokens, values), BF16),
        vm((2, pairs, LANES, LANES), F32), vm((2, pairs, LANES, LANES), F32), vm((tokens, values), F32),
        vm((2, sh, sh), F32), vm((2, sh, sh), F32), vm((heads, 1, tokens), F32), vm((LANES, tokens), F32),
        vm((tokens, LANES), F32), vm((tokens, LANES), F32), vm((tokens, LANES), F32), vm((tokens, LANES), F32),
        vm((2, tokens, LANES), F32), vm((8, LANES), F32),
        vm((2, tokens, LANES), F32), vm((2, 2, sh, sh), BF16), vm((2, tokens, LANES), BF16),
        vm((pairs, LANES, LANES), BF16), vm((pairs, LANES, LANES), BF16),
        vm((pairs, LANES, LANES), BF16), vm((pairs, LANES, LANES), BF16),
        vm((pairs, LANES, LANES), BF16), vm((pairs, LANES, LANES), BF16),
        vm((hn, rpad, width), BF16), vm((hn, 2, tokens, LANES), BF16), vm((hn, rpad, tokens), BF16),
        vm((2, tokens, LANES), BF16), vm((2, tokens, LANES), BF16), vm((2, zn, part_rows, LANES), F32),
        vm((2, zn, part_rows, LANES), BF16), vm((2, zn, part_rows, LANES), BF16),
        vm((part_rows, both), BF16), vm((part_rows, both), BF16),
        vm((rpad, width), BF16), vm((rpad, width), BF16), vm((rpad, width), F32),
        vm((units, unit_rows, unit), BF16), vm((zn, unit_rows, unit), BF16), vm((units, unit_rows, unit), BF16),
        vm((rpad, half), BF16), vm((rpad, half), BF16),
        vm((8, LANES), F32), vm((8, LANES), F32), vm((8, LANES), F32), vm((zn, 8, LANES), F32),
        dma, dma((pairs + 1,)), dma, dma((pairs + 1,)),
        dma((4, hn - 1)), dma((4, hn - 1)), dma((7,)), dma((7,)), dma((5,)), dma((5, zn - 1)),
    ]
    spec = pl.BlockSpec(memory_space=pltpu.VMEM)
    shapes = (
        ((tokens, width), BF16), ((tokens, values), BF16), ((block, both), F32),
        ((heads, width), F32), ((1, heads), F32), ((1, heads), F32),
    )
    kept = pl.pallas_call(
        functools.partial(kernel, zn, hn, bn, heads, split),
        out_shape=tuple(vm(*s) for s in shapes),
        in_specs=[pl.BlockSpec(memory_space=pl.ANY)] * 7,
        out_specs=[spec] * 6,
        scratch_shapes=scratch,
        compiler_params=pltpu.CompilerParams(
            collective_id=0, has_side_effects=True, vmem_limit_bytes=56 << 20
        ),
    )(
        u_input.reshape(tokens, width), head_values.reshape(tokens, values), grad_output.reshape(tokens, values),
        w_bc, w_dt.T, dt_bias.reshape(1, heads), a_log.reshape(1, heads),
    )
    gin, gval, gwbc, gwdt, gbias, galog = pl.pallas_call(
        write,
        out_shape=tuple(jax.ShapeDtypeStruct(*s) for s in shapes),
        in_specs=[spec] * 6,
        out_specs=[pl.BlockSpec(memory_space=pl.ANY)] * 6,
        scratch_shapes=[dma((6,))],
        compiler_params=pltpu.CompilerParams(vmem_limit_bytes=1 << 20),
    )(*kept)
    return (
        gin.reshape(1, tokens, width), gval.reshape(1, tokens, values), gwbc,
        gwdt.T, gbias.reshape(heads), galog.reshape(heads),
    )


def write(*refs):
    sems = refs[12]
    copies = [pltpu.make_async_copy(refs[i], refs[6 + i], sems.at[i]) for i in range(6)]
    for copy in copies:
        copy.start()
    for copy in copies:
        copy.wait()


def solution(mesh):
    sizes = (mesh.shape["tm"], mesh.shape["head"], mesh.shape["batch"])
    return jax.shard_map(
        functools.partial(on_device, sizes),
        mesh=mesh,
        in_specs=(
            P(("groups", "batch"), "tm", None),
            P(("groups", "batch"), "tm", "head"),
            P(("groups", "batch"), "tm", "head"),
            P(),
            P(None, "head"),
            P("head"),
            P("head"),
        ),
        out_specs=(
            P(("groups", "batch"), "tm", None),
            P(("groups", "batch"), "tm", "head"),
            P(("groups", "tm", "batch"), None),
            P("groups", "head"),
            P(("groups", "head")),
            P(("groups", "head")),
        ),
        check_vma=False,
    )
```

```python
import functools
import math

import jax
import jax.numpy as jnp
from jax import lax
from jax.experimental import pallas as pl
from jax.experimental.pallas import tpu as pltpu
from jax.sharding import PartitionSpec as P

MESH = pl.DeviceIdType.MESH
F32 = jnp.float32
BF16 = jnp.bfloat16
LANES = 128
NT = (((1,), (1,)), ((), ()))
TN = (((0,), (0,)), ((), ()))


def dot(a, b, dims=(((1,), (0,)), ((), ()))):
    return lax.dot_general(a, b, dims, preferred_element_type=F32)


def split3(v):
    hi = v.astype(BF16)
    rest = v - hi.astype(F32)
    mid = rest.astype(BF16)
    return hi, mid, (rest - mid.astype(F32)).astype(BF16)


def dot_ones(a, v):
    hi, mid, lo = split3(v)
    return dot(a, hi) + dot(a, mid) + dot(a, lo)


def dot_sel(v, ones):
    hi = v.astype(BF16)
    lo = (v - hi.astype(F32)).astype(BF16)
    return dot(hi, ones, NT) + dot(lo, ones, NT)


def kernel(
    zn, hn, bn, heads, split,
    u_h, x_h, g_h, wbc_h, wdt_h, bias_h, alog_h,
    gin, gval, gwbc, gwdt, gbias, galog,
    u, x, g, wbc, wdt, bias, alog,
    wpad, ut, uto, rows, proj, l_t, l_b, e1_b, e1_p, e2_p, ends_b, sel, xs, gs, own_f, own_b, gxi, st, dst, col_e, erows,
    direct, qd, gl, net, gates, tails, gacc, mixers, mates, smid, gmid,
    sf, rf, sb, rb, wx, px, gpx, psend, precv, plocal, zsend, zrecv, fsend, frecv,
    wsend, wrecv, wsum, wzsend, wzrecv, wgrecv, wfsend, wfrecv, smsend, smrecv, smzsend, smzrecv,
    f_ss, f_rs, b_ss, b_rs, h_ss, h_rs, c_ss, c_rs, z_ss, z_rs,
):
    z, hx, bt = lax.axis_index("tm"), lax.axis_index("head"), lax.axis_index("batch")
    tokens, width = u.shape
    pairs = heads // 2
    groups = pairs // 2
    state = LANES
    sh = tokens // 2
    rpad = wx.shape[1]
    half = width // bn
    units, unit_rows, unit = wzsend.shape
    unit_cols = half // unit

    loads = [
        pltpu.make_async_copy(src, to, c_ss.at[i])
        for i, (src, to) in enumerate((
            (wdt_h, wdt), (bias_h, bias), (alog_h, alog), (u_h, u), (wbc_h, wbc), (x_h, x), (g_h, g)
        ))
    ]
    for i in (3, 4, 0, 1, 2, 6, 5):
        loads[i].start()

    barrier = pltpu.get_barrier_semaphore()
    @pl.when(z > 0)
    def _():
        pl.semaphore_signal(barrier, inc=1, device_id={"tm": lax.rem(z + zn - 1, zn)}, device_id_type=MESH)

    @pl.when(z < zn - 1)
    def _():
        pl.semaphore_signal(barrier, inc=1, device_id={"tm": lax.rem(z + 1, zn)}, device_id_type=MESH)

    for k in range(1, hn):
        pl.semaphore_signal(barrier, inc=1, device_id={"head": lax.rem(hx + k, hn)}, device_id_type=MESH)
    for k in range(1, bn):
        pl.semaphore_signal(barrier, inc=1, device_id={"batch": lax.rem(bt + k, bn)}, device_id_type=MESH)

    lane = lax.broadcasted_iota(jnp.int32, (tokens, LANES), 1)
    low = lax.broadcasted_iota(jnp.int32, (sh, LANES), 1) < 64
    lm = low.astype(F32).astype(BF16)
    hm = 1.0 - lm
    ti = lax.broadcasted_iota(jnp.int32, (tokens, tokens), 0)
    si = lax.broadcasted_iota(jnp.int32, (tokens, tokens), 1)
    lower = (ti >= si).astype(F32).astype(BF16)
    causal = ti[:sh, :sh] <= si[:sh, :sh]

    with jax.named_scope("initial"):
        wpad[...] = jnp.zeros_like(wpad)
        rows[...] = jnp.zeros_like(rows)
        which = lax.broadcasted_iota(jnp.int32, (LANES, LANES), 0)
        head_of = lax.shift_right_logical(lax.broadcasted_iota(jnp.int32, (LANES, LANES), 1), 6)
        used = jnp.where(which < 96, which & 31, -1)
        for p in range(pairs):
            sel[:, p * LANES:(p + 1) * LANES] = (used == head_of + 2 * p).astype(F32).astype(BF16)
        dst[...] = jnp.zeros_like(dst)
        direct[...] = jnp.zeros_like(direct)
        gl[...] = jnp.zeros_like(gl)
        qd[...] = jnp.zeros_like(qd)
        gacc[...] = jnp.zeros_like(gacc)
        tails[...] = jnp.zeros_like(tails)
        erows[...] = jnp.zeros_like(erows)

        @pl.when(z == 0)
        def _():
            rf[...] = jnp.zeros_like(rf)

        @pl.when(z == zn - 1)
        def _():
            rb[...] = jnp.zeros_like(rb)

    def packed(v):
        hi, mid, lo = split3(v)
        at = lane[:v.shape[0]]
        mid, lo = pltpu.roll(mid.astype(F32), 32, 1), pltpu.roll(lo.astype(F32), 64, 1)
        return jnp.where(at < 32, hi.astype(F32), jnp.where(at < 64, mid, jnp.where(at < 96, lo, 0.0))).astype(BF16)

    with jax.named_scope("wait for u"):
        for load in loads[:5]:
            load.wait()
    wpad[:heads, :] = wdt[...]
    rows[0:1, :heads] = bias[...]
    rows[1:2, :heads] = alog[...]
    wx[hx] = wpad[:rpad, :]
    uu = u[...]
    proj[...] = dot(uu, wbc[...]).astype(BF16)
    b_all, c_all = proj[:, :state], proj[:, state:]
    b_t = b_all.astype(F32).T.astype(BF16)
    c_t = c_all.astype(F32).T.astype(BF16)
    pre = dot(uu, wpad[...], NT) + rows[0:1, :]
    small = jnp.exp(-jnp.abs(pre))
    delta = jnp.maximum(pre, 0.0) + jnp.log1p(small)
    rate = -jnp.exp(rows[1:2, :])
    log_decay = dot_ones(lower, delta * rate)
    mid_l, last_l = log_decay[sh - 1:sh, :], log_decay[tokens - 1:tokens, :]
    first = lax.broadcasted_iota(jnp.int32, (tokens, LANES), 0) < sh
    e1 = packed(jnp.exp(jnp.where(first, mid_l, last_l) - log_decay) * delta)
    e2 = packed(jnp.exp(jnp.where(first, log_decay, log_decay - mid_l)))
    e1_p[...] = e1
    e2_p[...] = e2
    ends = jnp.concatenate([jnp.exp(mid_l), jnp.exp(last_l - mid_l), jnp.zeros((6, LANES), F32)], axis=0)
    ends_b[...] = dot(packed(ends), sel[...])
    with jax.named_scope("wait for values"):
        loads[5].wait()
        loads[6].wait()
    with jax.named_scope("wait for devices"):
        pl.semaphore_wait(barrier, jnp.where((z == 0) | (z == zn - 1), 1, 2) + hn + bn - 2)

    def head_copy(i, ref, k):
        return pltpu.make_async_remote_copy(
            ref, ref, h_ss.at[i, k - 1], h_rs.at[i, k - 1],
            device_id={"head": lax.rem(hx + k, hn)}, device_id_type=MESH,
        )

    def weights_copy(k):
        return head_copy(0, wx.at[hx], k)

    def steps_copy(k):
        return head_copy(1, gpx.at[hx], k)

    early = jnp.where(2 * z < zn, 1, 0)

    def maps_copy(role, k):
        return head_copy(2 + role, px.at[hx, early if role == 0 else 1 - early], k)

    def chain_f(p, piece):
        at, size, sem = piece
        return pltpu.make_async_remote_copy(
            sf.at[p, pl.ds(at, size)], rf.at[p, pl.ds(at, size)], f_ss, f_rs.at[sem],
            device_id={"tm": lax.rem(z + 1, zn)}, device_id_type=MESH,
        )

    def chain_b(p, piece):
        at, size, sem = piece
        return pltpu.make_async_remote_copy(
            sb.at[p, pl.ds(at, size)], rb.at[p, pl.ds(at, size)], b_ss, b_rs.at[sem],
            device_id={"tm": lax.rem(z + zn - 1, zn)}, device_id_type=MESH,
        )

    def pieces(p, body):
        @pl.when(p < pairs - 1)
        def _():
            body((0, state, p))

        @pl.when(p == pairs - 1)
        def _():
            body((0, state // 2, pairs - 1))
            body((state // 2, state // 2, pairs))

    def columns(p, n=1):
        return pl.ds(pl.multiple_of(p * n * LANES, LANES), n * LANES)

    def forward(p, arrives):
        cols = columns(p)

        def body(piece):
            at, size, _ = piece
            if arrives:
                chain_f(p, piece).wait_recv()
            part = slice(at, at + size)
            middle = ends_b[0:1, cols] * rf[p, part].astype(F32) + own_f[0, p, part]
            smid[p, part] = middle.astype(BF16)
            sf[p, part] = (ends_b[1:2, cols] * middle + own_f[1, p, part]).astype(BF16)

            @pl.when(z < zn - 1)
            def _():
                chain_f(p, piece).start()

        pieces(p, body)

    def backward(p, arrives):
        cols = columns(p)

        def body(piece):
            at, size, _ = piece
            if arrives:
                chain_b(p, piece).wait_recv()
            part = slice(at, at + size)
            middle = ends_b[1:2, cols] * rb[p, part].astype(F32) + own_b[1, p, part]
            gmid[p, part] = middle.astype(BF16)
            sb[p, part] = (ends_b[0:1, cols] * middle + own_b[0, p, part]).astype(BF16)

            @pl.when(z > 0)
            def _():
                chain_b(p, piece).start()

        pieces(p, body)

    def summarize(q, carry):
        cols = columns(q, 2)
        spread = dot(e1_p[...], sel[:, cols])
        e1_b[:, cols] = spread
        xv = (spread * x[:, cols].astype(F32)).astype(BF16)
        gv = (dot(e2_p[...], sel[:, cols]) * g[:, cols].astype(F32)).astype(BF16)
        xs[:, cols] = xv
        gs[:, cols] = gv
        for k in range(2):
            part = slice(k * sh, (k + 1) * sh)
            of, ob = dot(b_t[:, part], xv[part]), dot(c_t[:, part], gv[part])
            for j in range(2):
                own_f[k, 2 * q + j] = of[:, j * LANES:(j + 1) * LANES]
                own_b[k, 2 * q + j] = ob[:, j * LANES:(j + 1) * LANES]

        @pl.when(z == 0)
        def _():
            forward(2 * q, False)
            forward(2 * q + 1, False)

        @pl.when(z == zn - 1)
        def _():
            @pl.when(q > 0)
            def _():
                backward(2 * q, False)

            backward(2 * q + 1, False)

        return carry

    @pl.when(z == zn - 1)
    def _():
        with jax.named_scope("first pair"):
            gv = (dot(e2_p[...], sel[:, :LANES]) * g[:, :LANES].astype(F32)).astype(BF16)
            for k in range(2):
                part = slice(k * sh, (k + 1) * sh)
                own_b[k, 0] = dot(c_t[:, part], gv[part])
            backward(0, False)

    with jax.named_scope("summaries"):
        lax.fori_loop(0, groups, summarize, 0)

    for k in range(1, hn):
        weights_copy(k).start()

    with jax.named_scope("scores"):
        l_rows = log_decay.T
        for h in range(heads):
            l_t[h] = l_rows[h:h + 1, :]
        l_b[...] = dot(packed(log_decay - jnp.log(jnp.maximum(delta, 1e-37))), sel[...])
        gate = jax.nn.sigmoid(pre)
        gates[0] = gate
        gates[1] = jnp.where(delta > 1e-30, gate / jnp.maximum(delta, 1e-30), 1.0)
        for k in range(2):
            part = slice(k * sh, (k + 1) * sh)
            st[k] = jnp.where(causal, dot(b_all[part], c_all[part], NT), 0.0)
    other = {"batch": lax.rem(bt + 1, bn)}

    def core_copy(i, src, to):
        return pltpu.make_async_remote_copy(src, to, c_ss.at[i], c_rs.at[i], device_id=other, device_id_type=MESH)

    share = ut.shape[1]
    part_rows = uto.shape[1]
    block = share * part_rows
    my_rows = hx if split else 0
    chunk = math.lcm(block, LANES)
    for c in range(width // chunk):
        turned = u[:, c * chunk:(c + 1) * chunk].astype(F32).T
        for i in range(chunk // block):
            k, b = divmod(c * (chunk // block) + i, bn)
            for r in range(share):
                at = i * block + r * part_rows
                ut[b, r, k] = turned[at:at + part_rows].astype(BF16)
    core_u = core_copy(5, ut.at[lax.rem(bt + 1, bn), my_rows], uto)
    core_u.start()

    def local_pair(p):
        cols = columns(p)
        for k in range(2):
            part = slice(k * sh, (k + 1) * sh)
            gt = g[part, cols]
            xb = x[part, cols]
            sm = st[k]
            dm = dot(jnp.concatenate([xb * lm, xb * hm], axis=0), gt, NT)
            add = None
            mixed = []
            dr = direct[part]
            for j in range(2):
                lr = l_t[2 * p + j][:, part]
                lcol = l_b[part, cols][:, 64 * j:64 * j + 1]
                decay = jnp.exp(jnp.minimum(lr - lcol, 30.0))
                mixed.append((decay * sm).astype(BF16))
                a = dm[j * sh:(j + 1) * sh] * decay
                add = a if add is None else add + a
                w = a * sm
                col_e[2 * p + j, :, part] = jnp.sum(w, axis=0, keepdims=True)
                dr = dr + jnp.where(lane[:sh] == 2 * p + j, jnp.sum(w, axis=1, keepdims=True), 0.0)
            direct[part] = dr
            dst[k] += add
            gx = dot(jnp.concatenate(mixed, axis=0), gt)
            gxi[part, cols] = jnp.where(low, gx[:sh], gx[sh:])

    def two(ref, q):
        return jnp.concatenate([ref[2 * q], ref[2 * q + 1]], axis=1)

    kept = max(groups - 3, 0)
    halves = [slice(k * sh, (k + 1) * sh) for k in range(2)]

    def maps_before(q):
        for part, ref in zip(halves, (rf, smid)):
            gacc[1, part] += dot(gs[part, columns(q, 2)], two(ref, q), NT)

    def maps_after(q):
        for part, ref in zip(halves, (gmid, rb)):
            gacc[0, part] += dot(xs[part, columns(q, 2)], two(ref, q), NT)

    def values_before(q):
        cols = columns(q, 2)
        cs = [dot(c_all[part], two(ref, q)) for part, ref in zip(halves, (rf, smid))]
        gl[...] += dot_sel(gs[:, cols].astype(F32) * jnp.concatenate(cs, axis=0), sel[:, cols])

    def values_after(q):
        cols = columns(q, 2)
        bs = [dot(b_all[part], two(ref, q)) for part, ref in zip(halves, (gmid, rb))]
        br = e1_b[:, cols] * jnp.concatenate(bs, axis=0)
        gval[:, cols] = (gxi[:, cols] + br).astype(BF16)
        qd[...] += dot_sel(x[:, cols].astype(F32) * br, sel[:, cols])

    def through(q):
        cols = columns(q, 2)
        both = [
            jnp.sum(two(before, q).astype(F32) * two(after, q).astype(F32), axis=0, keepdims=True)
            for before, after in ((rf, gmid), (smid, rb))
        ]
        row = lax.broadcasted_iota(jnp.int32, (8, 2 * LANES), 0)
        both = ends_b[:, cols] * jnp.where(row == 0, both[0], both[1])
        tails[...] += sum(dot(part, sel[:, cols], NT) for part in split3(both))

    late_f = jnp.maximum(4 * z - 2, 0)
    late_b = jnp.maximum(6 * (zn - 1 - z) - 4, 0)

    first_base = jnp.maximum(pairs, jnp.where(early == 1, late_f, late_b) + 1 + groups)
    second_base = jnp.maximum(first_base + groups, jnp.where(early == 1, late_b, late_f) + 1 + groups)

    def base_of(edge, far_edge, first, late):
        return jnp.where(edge, 1, jnp.where(far_edge, late + 1, jnp.where(first, first_base, second_base)))

    base_f = base_of(z == 0, z == zn - 1, early == 1, late_f)
    base_b = base_of(z == zn - 1, z == 0, early == 0, late_b)
    at_end = (z == 0) | (z == zn - 1)
    send_at = jnp.where(at_end, jnp.maximum(2 * groups, pairs) + 1, first_base + groups)

    def step_of(i, edge, base):
        k = i - base
        return k, jnp.where(at_end, k // 2, k), (k >= 0) & (jnp.logical_not(at_end) | (k % 2 == 0))

    def send_maps(role):
        part = early if role == 0 else 1 - early
        for k, rows_of in enumerate(halves):
            px[hx, part, rows_of] = (gacc[part, rows_of] + dot(mixers[part, k], mates[part, rows_of])).astype(BF16)
        for k in range(1, hn):
            maps_copy(role, k).start()

    def along(i, src, to, k):
        there = lax.rem(z + k, zn)
        return pltpu.make_async_remote_copy(
            src, to.at[z], z_ss.at[i], z_rs.at[i, k - 1], device_id={"tm": there}, device_id_type=MESH
        )

    def all_sent(i, blocks):
        pltpu.make_async_remote_copy(
            blocks.at[pl.ds(0, zn - 1)], blocks.at[pl.ds(0, zn - 1)], z_ss.at[i], z_rs.at[i, 0],
            device_id={"tm": lax.rem(z + 1, zn)}, device_id_type=MESH,
        ).wait_send()

    def each_z(body):
        def turn(k, carry):
            body(k)
            return carry

        lax.fori_loop(1, zn, turn, 0)

    def both_heads(part):
        total = px[0, part].astype(F32)
        for k in range(1, hn):
            total = total + px[k, part].astype(F32)
        return total.astype(BF16)

    def product(ref, values):
        if part_rows % 16 == 0:
            return dot(ref[...].reshape(zn * part_rows, tokens), values).reshape(zn, part_rows, LANES)
        return jnp.stack([dot(ref[k], values) for k in range(zn)])

    def core_maps(role):
        return core_copy(2 if role == 0 else 6, psend.at[role], precv.at[role])

    def share_maps(role):
        for k in range(1, hn):
            maps_copy(role, k).wait()
        piece = both_heads(early if role == 0 else 1 - early)
        psend[role] = piece
        core_maps(role).start()
        plocal[role] = product(ut.at[bt, my_rows], piece)

    def z_copy_maps(role, k):
        part = early if role == 0 else 1 - early
        return along(2 if role == 0 else 4, zsend.at[part, lax.rem(z + k, zn)], zrecv.at[part], k)

    def spread_maps(role):
        part = early if role == 0 else 1 - early
        if role == 0:
            core_u.wait()
        core_maps(role).wait()
        zsend[part] = (plocal[role] + product(uto, precv[role])).astype(BF16)
        zrecv[part, z] = zsend[part, z]
        each_z(lambda k: z_copy_maps(role, k).start())

    def turn(i, carry):
        pf = i - late_f
        pb = i - late_b
        in_f, in_b = (pf >= 0) & (pf < pairs), (pb >= 0) & (pb < pairs)

        @pl.when(in_f & (z > 0))
        def _():
            with jax.named_scope("forward"):
                forward(pf, True)

        @pl.when(in_b & (z < zn - 1))
        def _():
            with jax.named_scope("backward"):
                backward(pb, True)

        @pl.when(i < pairs)
        def _():
            with jax.named_scope("local"):
                local_pair(i)

        kf, qf, on_f = step_of(i, z == 0, base_f)
        kb, qb, on_b = step_of(i, z == zn - 1, base_b)

        @pl.when(kf == 0)
        def _():
            maps_before(0)

        @pl.when(on_f & (qf == groups - 1))
        def _():
            maps_before(groups - 1)

        @pl.when(on_b & (qb == groups - 1))
        def _():
            maps_after(groups - 1)

        @pl.when(on_f & (qf > 0) & (qf < groups - 1))
        def _():
            with jax.named_scope("before"):
                maps_before(qf)
                values_before(qf - 1)

        @pl.when(kb == 0)
        def _():
            maps_after(0)

        @pl.when(on_b & (qb > 0) & (qb < groups - 1))
        def _():
            with jax.named_scope("after"):
                maps_after(qb)
                values_after(qb - 1)

        kt = i - jnp.maximum(late_f, late_b) - 2

        @pl.when((kt >= 0) & (kt < jnp.where(at_end, 2 * kept, pairs - 2)) & (kt % 2 == 0))
        def _():
            with jax.named_scope("through"):
                through(kt // 2)

        @pl.when(i == send_at)
        def _():
            with jax.named_scope("first map gradient"):
                send_maps(0)

        @pl.when(at_end & (i == send_at + 6))
        def _():
            with jax.named_scope("share first maps"):
                share_maps(0)

        @pl.when(at_end & (i == send_at + 8))
        def _():
            with jax.named_scope("spread first maps"):
                spread_maps(0)

        @pl.when(i == pairs)
        def _():
            with jax.named_scope("local sums"):
                for h in range(heads):
                    erows[h:h + 1, :] = col_e[h]
                net[...] = erows[...].T - direct[...]
                for k in range(2):
                    masked = jnp.where(causal, dst[k], 0.0)
                    mixers[0, k] = masked.astype(BF16)
                    mixers[1, k] = masked.T.astype(BF16)
                mates[0] = c_all
                mates[1] = b_all

        return carry

    lax.fori_loop(0, max(6 * (zn - 1) - 3, pairs, 10) + 2 * groups + 1, turn, 0)

    with jax.named_scope("last map gradient"):
        send_maps(1)

    @pl.when(jnp.logical_not(at_end))
    def _():
        with jax.named_scope("share first maps"):
            share_maps(0)

    with jax.named_scope("last values"):
        for q in range(max(groups - 2, 0), groups):
            values_before(q)
            values_after(q)
        @pl.when(at_end)
        def _():
            for q in range(kept, groups):
                through(q)

        @pl.when(jnp.logical_not(at_end))
        def _():
            through(groups - 1)

    with jax.named_scope("step gradients"):
        upper = ((ti <= si) & ((ti < sh) == (si < sh))).astype(F32).astype(BF16)
        carried = qd[...]
        weighted = direct[...] + carried
        g_log = net[...] + gl[...] - carried
        ends_sum = tails[...]
        tail = [
            jnp.sum(carried[k * sh:(k + 1) * sh], axis=0, keepdims=True) + ends_sum[k:k + 1] for k in range(2)
        ]
        back = dot_ones(upper, g_log) + jnp.where(first, tail[0], tail[1])
        gate, per_delta = gates[0], gates[1]
        g_pre = weighted * per_delta + rate * back * gate
        smsend[...] = jnp.zeros_like(smsend)
        smsend[0:1, :] = jnp.sum(g_pre, axis=0, keepdims=True)
        smsend[1:2, :] = jnp.sum(delta * back, axis=0, keepdims=True) * rate
    gpx[hx] = g_pre.T[:rpad, :].astype(BF16)
    for k in range(1, hn):
        steps_copy(k).start()
    with jax.named_scope("step weight product"):
        wsend[...] = dot(gpx[hx], uu).astype(BF16)

    core_w = core_copy(0, wsend, wrecv)
    core_s = core_copy(1, smsend, smrecv)
    core_f = core_copy(3, wfsend, wfrecv)
    core_w.start()
    core_s.start()

    def z_start_small(k):
        along(0, wzsend.at[lax.rem(z + k, zn) if units > 1 else 0], wzrecv, k).start()
        along(1, smzsend, smzrecv, k).start()

    def z_wait_small(k):
        along(0, wzsend.at[lax.rem(z + k, zn) if units > 1 else 0], wzrecv, k).wait_recv()
        along(1, smzsend, smzrecv, k).wait_recv()

    def z_start_sums(k):
        along(3, wgrecv.at[z], wgrecv, k).start()

    def z_wait_sums(k):
        along(3, wgrecv.at[z], wgrecv, k).wait_recv()

    @pl.when(jnp.logical_not(at_end))
    def _():
        with jax.named_scope("spread first maps"):
            spread_maps(0)

    with jax.named_scope("core w"):
        core_w.wait()
    core_s.wait()
    wsum[...] = wsend[...].astype(F32) + wrecv[...].astype(F32)
    mine = pl.ds(pl.multiple_of(bt * half, LANES), half)
    theirs = pl.ds(pl.multiple_of(lax.rem(bt + 1, bn) * half, LANES), half)
    for k in range(units):
        r, c = divmod(k, unit_cols)
        cols = pl.ds(pl.multiple_of(bt * half + c * unit, LANES), unit)
        wzsend[k] = wsum[r * unit_rows:(r + 1) * unit_rows, cols].astype(BF16)
    own_unit = z if units > 1 else 0
    wzrecv[z] = wzsend[own_unit]
    sz = smsend[...] + smrecv[...]
    smzsend[...] = sz
    smzrecv[z] = sz
    each_z(z_start_small)

    with jax.named_scope("share last maps"):
        share_maps(1)
    with jax.named_scope("spread last maps"):
        spread_maps(1)

    with jax.named_scope("small along z"):
        each_z(z_wait_small)
    total_w = wzrecv[0].astype(F32)
    total_s = smzrecv[0]
    for k in range(1, zn):
        total_w = total_w + wzrecv[k].astype(F32)
        total_s = total_s + smzrecv[k]
    wgrecv[own_unit] = total_w.astype(BF16)
    if units > 1:
        each_z(z_start_sums)
    gbias[...] = total_s[0:1, :heads]
    galog[...] = total_s[1:2, :heads]

    for k in range(1, hn):
        weights_copy(k).wait()
        steps_copy(k).wait()
    gp = jnp.concatenate([both_heads(0), both_heads(1)], axis=1)
    gpa = gpx[...].reshape(hn * rpad, tokens).astype(F32).T.astype(BF16)
    wa = wx[...].reshape(hn * rpad, width)
    with jax.named_scope("input gradient"):
        gin[...] = (dot(gp, wbc[...], NT) + dot(gpa, wa)).astype(BF16)

    with jax.named_scope("large along z"):
        for role in range(2):
            each_z(lambda k: z_copy_maps(role, k).wait_recv())
    total = [sum(zrecv[part, k].astype(F32) for k in range(zn)) for part in range(2)]
    if split:
        fsend[...] = jnp.concatenate(total, axis=1).astype(BF16)
        final = pltpu.make_async_remote_copy(
            fsend, frecv, c_ss.at[4], c_rs.at[4], device_id={"head": lax.rem(hx + 1, hn)}, device_id_type=MESH
        )
        final.start()

    with jax.named_scope("sums along z"):
        if units > 1:
            each_z(z_wait_sums)
    for k in range(units):
        r, c = divmod(k, unit_cols)
        wfsend[r * unit_rows:(r + 1) * unit_rows, c * unit:(c + 1) * unit] = wgrecv[k]
    core_f.start()
    gwdt[:, mine] = wfsend[...].astype(F32)[:heads, :]

    if split:
        gwbc[pl.ds(pl.multiple_of(hx * part_rows, 16), part_rows), :] = fsend[...].astype(F32)
        with jax.named_scope("last exchange"):
            final.wait()
        gwbc[pl.ds(pl.multiple_of((1 - hx) * part_rows, 16), part_rows), :] = frecv[...].astype(F32)
    else:
        gwbc[...] = jnp.concatenate(total, axis=1)
    with jax.named_scope("core f"):
        core_f.wait()
    gwdt[:, theirs] = wfrecv[...].astype(F32)[:heads, :]

    all_sent(0, wzrecv)
    all_sent(1, smzrecv)
    all_sent(2, zrecv.at[0])
    all_sent(4, zrecv.at[0])
    if units > 1:
        all_sent(3, wgrecv)

    @pl.when(z < zn - 1)
    def _():
        pltpu.make_async_remote_copy(
            sf, rf, f_ss, f_rs.at[0], device_id={"tm": lax.rem(z + 1, zn)}, device_id_type=MESH
        ).wait_send()

    @pl.when(z > 0)
    def _():
        pltpu.make_async_remote_copy(
            sb, rb, b_ss, b_rs.at[0], device_id={"tm": lax.rem(z + zn - 1, zn)}, device_id_type=MESH
        ).wait_send()


def on_device(sizes, u_input, head_values, grad_output, w_bc, w_dt, dt_bias, a_log):
    zn, hn, bn = sizes
    seqs, tokens, width = u_input.shape
    assert seqs == 1 and bn == 2
    heads = w_dt.shape[1]
    values = head_values.shape[2]
    both = w_bc.shape[1]
    pairs = heads // 2
    assert values == heads * 64 and both == 2 * LANES and heads % 4 == 0 and heads <= 32 and tokens == 2 * LANES
    block = width // (zn * bn)
    split = hn == 2 and block % 32 == 0
    share = hn if split else 1
    part_rows = block // share
    rpad = -(-heads // 16) * 16
    half = width // bn
    sh = tokens // 2
    unit_rows, unit = 16, half * rpad // (16 * zn)
    if (half * rpad) % (16 * zn) or unit == 0 or unit % LANES or half % unit:
        unit_rows, unit = rpad, half
    units = (rpad // unit_rows) * (half // unit)
    vm = pltpu.VMEM
    dma = pltpu.SemaphoreType.DMA
    scratch = [
        vm((tokens, width), BF16), vm((tokens, values), BF16), vm((tokens, values), BF16), vm((width, both), BF16),
        vm((heads, width), BF16), vm((1, heads), F32), vm((1, heads), F32),
        vm((LANES, width), BF16), vm((bn, share, zn, part_rows, tokens), BF16), vm((zn, part_rows, tokens), BF16), vm((8, LANES), F32), vm((tokens, both), BF16),
        vm((heads, 1, tokens), F32), vm((tokens, values), F32), vm((tokens, values), F32),
        vm((tokens, LANES), BF16), vm((tokens, LANES), BF16),
        vm((8, values), F32), vm((LANES, values), BF16), vm((tokens, values), BF16), vm((tokens, values), BF16),
        vm((2, pairs, LANES, LANES), F32), vm((2, pairs, LANES, LANES), F32), vm((tokens, values), F32),
        vm((2, sh, sh), F32), vm((2, sh, sh), F32), vm((heads, 1, tokens), F32), vm((LANES, tokens), F32),
        vm((tokens, LANES), F32), vm((tokens, LANES), F32), vm((tokens, LANES), F32), vm((tokens, LANES), F32),
        vm((2, tokens, LANES), F32), vm((8, LANES), F32),
        vm((2, tokens, LANES), F32), vm((2, 2, sh, sh), BF16), vm((2, tokens, LANES), BF16),
        vm((pairs, LANES, LANES), BF16), vm((pairs, LANES, LANES), BF16),
        vm((pairs, LANES, LANES), BF16), vm((pairs, LANES, LANES), BF16),
        vm((pairs, LANES, LANES), BF16), vm((pairs, LANES, LANES), BF16),
        vm((hn, rpad, width), BF16), vm((hn, 2, tokens, LANES), BF16), vm((hn, rpad, tokens), BF16),
        vm((2, tokens, LANES), BF16), vm((2, tokens, LANES), BF16), vm((2, zn, part_rows, LANES), F32),
        vm((2, zn, part_rows, LANES), BF16), vm((2, zn, part_rows, LANES), BF16),
        vm((part_rows, both), BF16), vm((part_rows, both), BF16),
        vm((rpad, width), BF16), vm((rpad, width), BF16), vm((rpad, width), F32),
        vm((units, unit_rows, unit), BF16), vm((zn, unit_rows, unit), BF16), vm((units, unit_rows, unit), BF16),
        vm((rpad, half), BF16), vm((rpad, half), BF16),
        vm((8, LANES), F32), vm((8, LANES), F32), vm((8, LANES), F32), vm((zn, 8, LANES), F32),
        dma, dma((pairs + 1,)), dma, dma((pairs + 1,)),
        dma((4, hn - 1)), dma((4, hn - 1)), dma((7,)), dma((7,)), dma((5,)), dma((5, zn - 1)),
    ]
    spec = pl.BlockSpec(memory_space=pltpu.VMEM)
    shapes = (
        ((tokens, width), BF16), ((tokens, values), BF16), ((block, both), F32),
        ((heads, width), F32), ((1, heads), F32), ((1, heads), F32),
    )
    kept = pl.pallas_call(
        functools.partial(kernel, zn, hn, bn, heads, split),
        out_shape=tuple(vm(*s) for s in shapes),
        in_specs=[pl.BlockSpec(memory_space=pl.ANY)] * 7,
        out_specs=[spec] * 6,
        scratch_shapes=scratch,
        compiler_params=pltpu.CompilerParams(
            collective_id=0, has_side_effects=True, vmem_limit_bytes=56 << 20
        ),
    )(
        u_input.reshape(tokens, width), head_values.reshape(tokens, values), grad_output.reshape(tokens, values),
        w_bc, w_dt.T, dt_bias.reshape(1, heads), a_log.reshape(1, heads),
    )
    gin, gval, gwbc, gwdt, gbias, galog = pl.pallas_call(
        write,
        out_shape=tuple(jax.ShapeDtypeStruct(*s) for s in shapes),
        in_specs=[spec] * 6,
        out_specs=[pl.BlockSpec(memory_space=pl.ANY)] * 6,
        scratch_shapes=[dma((6,))],
        compiler_params=pltpu.CompilerParams(vmem_limit_bytes=1 << 20),
    )(*kept)
    return (
        gin.reshape(1, tokens, width), gval.reshape(1, tokens, values), gwbc,
        gwdt.T, gbias.reshape(heads), galog.reshape(heads),
    )


def write(*refs):
    sems = refs[12]
    copies = [pltpu.make_async_copy(refs[i], refs[6 + i], sems.at[i]) for i in range(6)]
    for copy in copies:
        copy.start()
    for copy in copies:
        copy.wait()


def solution(mesh):
    sizes = (mesh.shape["tm"], mesh.shape["head"], mesh.shape["batch"])
    return jax.shard_map(
        functools.partial(on_device, sizes),
        mesh=mesh,
        in_specs=(
            P(("groups", "batch"), "tm", None),
            P(("groups", "batch"), "tm", "head"),
            P(("groups", "batch"), "tm", "head"),
            P(),
            P(None, "head"),
            P("head"),
            P("head"),
        ),
        out_specs=(
            P(("groups", "batch"), "tm", None),
            P(("groups", "batch"), "tm", "head"),
            P(("groups", "tm", "batch"), None),
            P("groups", "head"),
            P(("groups", "head")),
            P(("groups", "head")),
        ),
        check_vma=False,
    )
```
